32 devices in a mesh: replica: 8 (over z, y), shard: 4 (over x, core).
Axes of the slice: x: 2, y: 2, z: 4, core: 2. Of those that a mesh axis runs over, the one named last changes fastest.
Arguments:
- tokens: bfloat16 [16, 512, 768], P('replica', 'shard'), may hold values from -6 to 6
- cotangent: bfloat16 [16, 512, 768], P('replica', 'shard'), may hold values from -6 to 6
- clip_count: int32 [8], P('replica'), may hold values from 1 to 2, as said below
- ln1_gain: float32 [768], P('shard'), may hold values from 0.5 to 1.5
- ln1_bias: float32 [768], P('shard'), may hold values from -3 to 3
- qkv_weight: float32 [768, 2304], P('shard'), may hold values from -0.21875 to 0.21875
- q_bias: float32 [768], P('shard'), may hold values from -3 to 3
- v_bias: float32 [768], P('shard'), may hold values from -3 to 3
- out_weight: float32 [768, 768], P('shard'), may hold values from -0.875 to 0.875
- out_bias: float32 [768], P('shard'), may hold values from -3 to 3
- ln2_gain: float32 [768], P('shard'), may hold values from 0.5 to 1.5
- ln2_bias: float32 [768], P('shard'), may hold values from -3 to 3
- fc1_weight: float32 [768, 3072], P('shard'), may hold values from -0.21875 to 0.21875
- fc1_bias: float32 [3072], P('shard'), may hold values from -3 to 3
- fc2_weight: float32 [3072, 768], P('shard'), may hold values from -0.109375 to 0.109375
- fc2_bias: float32 [768], P('shard'), may hold values from -3 to 3
Outputs:
- outputs: bfloat16 [16, 512, 768], P('replica', 'shard')
- input_grad: float32 [16, 512, 768], P('replica', 'shard')
- ln1_gain_grad: float32 [768], P('shard')
- ln1_bias_grad: float32 [768], P('shard')
- qkv_weight_grad: float32 [768, 2304], P('shard')
- q_bias_grad: float32 [768], P('shard')
- v_bias_grad: float32 [768], P('shard')
- out_weight_grad: float32 [768, 768], P('shard')
- out_bias_grad: float32 [768], P('shard')
- ln2_gain_grad: float32 [768], P('shard')
- ln2_bias_grad: float32 [768], P('shard')
- fc1_weight_grad: float32 [768, 3072], P('shard')
- fc1_bias_grad: float32 [3072], P('shard')
- fc2_weight_grad: float32 [3072, 768], P('shard')
- fc2_bias_grad: float32 [768], P('shard')
The draws below stay inside these ranges and needn't reach their ends.
Inputs may be any that keep to these rules, and one draw needn't show every extreme that they name: Clip slots 0 to clip_count[r] - 1 of replica group r are live, the rest are padding; some group has 2 live slots and some group one.
All inputs are finite; a program needn't handle non-finite values.
Results may differ from the reference program's by a relative error of at most 0.015.
Values may be sent and summed in bfloat16 or wider, within the bound.
A program may use at most 192 MiB of HBM per device.

```python
import jax
import jax.numpy as jnp
from jax import lax

D = 768
HEADS = 12
HD = 64
FF = 3072
SLOTS = 2
SEQ = 512
CLIPS = 16
N_REPLICA = 8


def draw_clip_count(key, part):
    first_key, second_key = jax.random.split(jax.random.fold_in(key, 11))
    counts = jax.random.randint(first_key, (N_REPLICA,), 1, SLOTS + 1)
    order = jax.random.permutation(second_key, N_REPLICA)
    counts = counts.at[order[0]].set(SLOTS)
    counts = counts.at[order[1]].set(1)
    return counts.astype(jnp.int32)


def level_of(rng, extent, cuts, least, largest):
    def one(dim, blocks):
        steps = jax.random.uniform(jax.random.fold_in(jax.random.fold_in(rng, 6), dim), (blocks,), jnp.float32, least / len(cuts), largest / len(cuts))
        return jnp.repeat(jnp.exp(steps), extent[dim] // blocks).reshape((-1,) + (1,) * (len(extent) - dim - 1))

    level = one(*cuts[0])
    for cut in cuts[1:]:
        level = level * one(*cut)
    return level


def noise(key, shape, deviation, most, cuts=(), dtype=jnp.bfloat16):
    level = level_of(key, shape, cuts, -0.22, 0.18) if cuts else 1.0
    entries = jax.random.normal(key, shape, jnp.float32) * deviation * level
    return jnp.minimum(jnp.maximum(entries, -most), most).astype(dtype)


def setup_inputs(seed: int = 0) -> dict:
    seeds = jax.random.split(jax.random.key(seed), 17)
    return {
        "tokens": noise(seeds[0], (CLIPS, SEQ, D), 1.0, 6.0, ((0, 8), (1, 4))),
        "cotangent": noise(seeds[1], (CLIPS, SEQ, D), 1.0, 6.0, ((0, 8), (1, 4))),
        "clip_count": draw_clip_count(jax.random.fold_in(seeds[16], 71), 0),
        "ln1_gain": jnp.clip(1.0 + 0.1 * jax.random.normal(seeds[3], (D,), jnp.float32), 0.5, 1.5),
        "ln1_bias": noise(seeds[4], (D,), 0.5, 3.0, ((0, 4),), jnp.float32),
        "qkv_weight": noise(seeds[5], (D, 3 * D), D ** -0.5, 0.21875, ((0, 4),), jnp.float32),
        "q_bias": noise(seeds[6], (D,), 0.5, 3.0, ((0, 4),), jnp.float32),
        "v_bias": noise(seeds[7], (D,), 0.5, 3.0, ((0, 4),), jnp.float32),
        "out_weight": noise(seeds[8], (D, D), (D // 16) ** -0.5, 0.875, ((0, 4),), jnp.float32),
        "out_bias": noise(seeds[9], (D,), 0.5, 3.0, ((0, 4),), jnp.float32),
        "ln2_gain": jnp.clip(1.0 + 0.1 * jax.random.normal(seeds[10], (D,), jnp.float32), 0.5, 1.5),
        "ln2_bias": noise(seeds[11], (D,), 0.5, 3.0, ((0, 4),), jnp.float32),
        "fc1_weight": noise(seeds[12], (D, FF), D ** -0.5, 0.21875, ((0, 4),), jnp.float32),
        "fc1_bias": noise(seeds[13], (FF,), 0.5, 3.0, ((0, 4),), jnp.float32),
        "fc2_weight": noise(seeds[14], (FF, D), FF ** -0.5, 0.109375, ((0, 4),), jnp.float32),
        "fc2_bias": noise(seeds[15], (D,), 0.5, 3.0, ((0, 4),), jnp.float32),
    }


EPSILON = 1e-06
HIGHEST_PRECISION = lax.Precision.HIGHEST

@jax.custom_vjp
def low(v):
    return lax.optimization_barrier(v.astype(jnp.bfloat16)).astype(jnp.float32)

@jax.custom_vjp
def low_back(v):
    return v

def low_keep(v):
    return (low(v), None)

def low_pass(kept, grad):
    return (grad,)

def back_keep(v):
    return (v, None)

def back_low(kept, grad):
    return (low(grad),)
low.defvjp(low_keep, low_pass)
low_back.defvjp(back_keep, back_low)

def layer_norm(values, gain, shift):
    mean_value = lax.optimization_barrier(jnp.mean(values, axis=-1, keepdims=True))
    centred = values - mean_value
    spread = lax.optimization_barrier(jnp.mean(centred * centred, axis=-1, keepdims=True))
    return centred * lax.rsqrt(spread + EPSILON) * gain + shift

def clip_layer(params, clip_rows):
    gain_one, shift_one, weight_qkv, bias_query, bias_value, weight_out, bias_out, gain_two, shift_two, weight_up, bias_up, weight_down, bias_down = params
    length = clip_rows.shape[0]
    hidden_one = low(layer_norm(clip_rows, gain_one, shift_one))
    projected = jnp.dot(hidden_one, weight_qkv, precision=HIGHEST_PRECISION)
    queries = low(low_back(projected[:, :D] + bias_query))
    keyset = low(low_back(projected[:, D:2 * D]))
    valueset = low(low_back(projected[:, 2 * D:] + bias_value))
    scores = jnp.einsum('qhd,khd->hqk', queries.reshape(length, HEADS, HD), keyset.reshape(length, HEADS, HD), precision=HIGHEST_PRECISION)
    scores = low_back(scores * HD ** (-0.5))
    softened = jax.nn.softmax(scores, axis=-1)
    mixture = jnp.einsum('hqk,khd->qhd', low(softened), valueset.reshape(length, HEADS, HD), precision=HIGHEST_PRECISION).reshape(length, D)
    attended = low(low_back(mixture))
    middle = clip_rows + low_back(jnp.dot(attended, weight_out, precision=HIGHEST_PRECISION) + bias_out)
    hidden_two = low(layer_norm(middle, gain_two, shift_two))
    lifted = low_back(jnp.dot(hidden_two, weight_up, precision=HIGHEST_PRECISION) + bias_up)
    activated = low(jax.nn.gelu(lifted, approximate=False))
    return middle + low_back(jnp.dot(activated, weight_down, precision=HIGHEST_PRECISION) + bias_down)

def forward(params, tokens):
    rounded = tuple((low(weight) for weight in params))
    checked = jax.checkpoint(clip_layer)

    def advance(carried, clip_rows):
        return (carried, checked(rounded, clip_rows))
    unused, outputs = lax.scan(advance, jnp.zeros((), jnp.float32), tokens)
    return outputs

def reference(tokens, cotangent, clip_count, ln1_gain, ln1_bias, qkv_weight, q_bias, v_bias, out_weight, out_bias, ln2_gain, ln2_bias, fc1_weight, fc1_bias, fc2_weight, fc2_bias):
    params = (ln1_gain, ln1_bias, qkv_weight, q_bias, v_bias, out_weight, out_bias, ln2_gain, ln2_bias, fc1_weight, fc1_bias, fc2_weight, fc2_bias)
    inputs = tokens.astype(jnp.float32)
    outputs, pullback = jax.vjp(forward, params, inputs)
    live_slots = (jnp.arange(SLOTS)[None, :] < clip_count[:, None]).astype(jnp.float32).reshape(CLIPS)
    masked = cotangent.astype(jnp.float32) * live_slots[:, None, None]
    grads, input_grad = pullback(masked)
    result = (outputs * live_slots[:, None, None]).astype(jnp.bfloat16)
    return (result, input_grad, grads[0], grads[1], grads[2], grads[3], grads[4], grads[5], grads[6], grads[7], grads[8], grads[9], grads[10], grads[11], grads[12])
```

```python
import functools

import jax
import jax.numpy as jnp
from jax import lax
from jax.experimental import pallas as pl
from jax.experimental.pallas import tpu as pltpu
from jax.sharding import PartitionSpec as P

D = 768
HD = 64
EPSILON = 1e-06
GROUP = 4
SLICE = D // GROUP
LOCAL_HEADS = SLICE // HD
HALF = D // 2
MIDDLE = 4
PIECE = SLICE // MIDDLE
BRAIN = jnp.bfloat16
SINGLE = jnp.float32
MESH = pl.DeviceIdType.MESH

G1, B1, BO, G2, B2, C2, BQ, BV, C1 = range(9)
VECTOR_ROWS = 16


class Names:
    def __init__(self):
        self.total = 0

    def take(self, count):
        first = self.total
        self.total += count
        return first


ids = Names()
ID_TOKENS = ids.take(3)
ID_COTANGENT = ids.take(3)
ID_GRADIENT = ids.take(3)
ID_VECTORS = ids.take(3)
ID_QKV = ids.take(3)
ID_OUT = ids.take(3)
ID_UP = ids.take(3)
ID_MIX = ids.take(6)
ID_SUM_TWO = ids.take(3)
ID_SUM_RESULT = ids.take(3)
ID_SUM_ONE = ids.take(3)
ID_SMALL = ids.take(3)
ID_WEIGHTS = ids.take(4 * 16)
COPIES = ids.total
LOCALS = 16


def to_single(value):
    return value.astype(SINGLE)


def dot(left, right, left_dim, right_dim):
    return lax.dot_general(
        left, right, (((left_dim,), (right_dim,)), ((), ())), preferred_element_type=SINGLE
    )


def normalize(value):
    mean = jnp.sum(value, axis=-1, keepdims=True) * (1.0 / D)
    centred = value - mean
    spread = jnp.sum(centred * centred, axis=-1, keepdims=True) * (1.0 / D)
    scale = lax.rsqrt(spread + EPSILON)
    return centred * scale, scale


def norm_back(grad, normal, scale, gain):
    scaled = grad * gain
    first = jnp.sum(scaled, axis=-1, keepdims=True) * (1.0 / D)
    second = jnp.sum(scaled * normal, axis=-1, keepdims=True) * (1.0 / D)
    return scale * (scaled - first - normal * second)


def row_sum(value):
    return jnp.sum(value, axis=0, keepdims=True)


def kernel(
    replicas,
    tokens_in,
    cotangent_in,
    count_in,
    vectors_in,
    qkv_in,
    out_in,
    up_in,
    down_in,
    outputs_out,
    input_grad_out,
    vectors_out,
    qkv_out,
    out_out,
    up_out,
    down_out,
    qkv_wide,
    out_wide,
    up_wide,
    down_wide,
    qkv_cut,
    up_cut,
    qkv_own,
    up_own,
    out_all,
    down_own,
    vectors,
    tokens,
    cotangent,
    hidden_one,
    pairs,
    soft,
    mixed,
    middle_own,
    hidden_two,
    active,
    lifted_grad,
    gradient,
    middle_grad,
    mixed_grad,
    pairs_grad,
    sum_sent,
    sum_near,
    sum_far,
    sum_own,
    out_grad,
    qkv_grad,
    y_down,
    y_up,
    y_out,
    y_qkv,
    z_down,
    z_up,
    z_out,
    z_qkv,
    piece_down,
    piece_up,
    piece_out,
    piece_qkv,
    cross_up,
    cross_qkv,
    full_down,
    full_up,
    full_out,
    full_qkv,
    columns,
    small_sent,
    small_near,
    small_all,
    result_stage,
    *rest,
):
    outer = replicas // (2 * MIDDLE)
    if outer > 1:
        outer_down, outer_up, outer_out, outer_qkv, send, recv, send_all, recv_all, near = rest
    else:
        send, recv, send_all, recv_all, near = rest
    rows = tokens_in.shape[0]
    slot = rows // 2
    group_rows = rows * GROUP

    shard = lax.axis_index("shard")
    replica = lax.axis_index("replica")
    y = replica % 2
    z = (replica // 2) % MIDDLE
    far = replica // (2 * MIDDLE)
    y_peer = replica + 1 - 2 * y

    def mate(step):
        return 2 * ((shard // 2 + step // 2) % 2) + (shard + step) % 2

    def z_at(step):
        return (z + step) % MIDDLE

    def z_peer(step):
        return replica + 2 * (z_at(step) - z)

    finals = []

    def remote(source, target, index, **where):
        return pltpu.make_async_remote_copy(
            src_ref=source,
            dst_ref=target,
            send_sem=send.at[index],
            recv_sem=recv.at[index],
            device_id=where,
            device_id_type=MESH,
        )

    def push(make):
        make().start()
        finals.append(make)

    def local(source, target, index):
        return pltpu.make_async_copy(source, target, near.at[index])

    def block(index, size):
        return pl.ds(pl.multiple_of(index * size, size), size)

    loads = [
        local(tokens_in, tokens.at[block(shard, rows)], 0),
        local(vectors_in, vectors.at[shard], 1),
        local(qkv_in, qkv_wide, 2),
        local(cotangent_in, cotangent.at[block(shard, rows)], 3),
        local(up_in, up_wide, 4),
        local(out_in, out_wide, 5),
        local(down_in, down_wide, 6),
    ]
    for load in loads:
        load.start()
    barrier = pltpu.get_barrier_semaphore()
    for step in (1, 2, 3):
        pl.semaphore_signal(barrier, inc=1, device_id={"shard": mate(step)}, device_id_type=MESH)

    def greet(step, carry):
        peer = (replica + step) % replicas
        pl.semaphore_signal(barrier, inc=1, device_id={"replica": peer}, device_id_type=MESH)
        return carry

    lax.fori_loop(1, replicas, greet, 0)
    loads[0].wait()
    loads[1].wait()
    pl.semaphore_wait(barrier, replicas + 2)

    def gather_near(buffer, base):
        return remote(
            buffer.at[block(shard, rows)], buffer.at[block(shard, rows)], base, shard=mate(1)
        )

    def gather_across(buffer, base):
        return remote(
            buffer.at[block(shard, rows)], buffer.at[block(shard, rows)], base + 1, shard=mate(2)
        )

    def gather_on(buffer, base):
        there = block(mate(2), rows)
        return remote(buffer.at[there], buffer.at[there], base + 2, shard=mate(1))

    def gather_start(buffer, base):
        push(functools.partial(gather_across, buffer, base))
        push(functools.partial(gather_near, buffer, base))

    def gather_forward(buffer, base):
        gather_across(buffer, base).wait_recv()
        push(functools.partial(gather_on, buffer, base))

    def gather_wait(buffer, base, step):
        @pl.when(step == 1)
        def _():
            gather_near(buffer, base).wait_recv()

        @pl.when(step == 3)
        def _():
            gather_on(buffer, base).wait_recv()

    gather_start(tokens, ID_TOKENS)
    for step in (1, 2, 3):
        push(
            functools.partial(
                lambda step: remote(
                    vectors.at[shard],
                    vectors.at[shard],
                    ID_VECTORS + step - 1,
                    shard=mate(step),
                ),
                step,
            )
        )

    loads[2].wait()
    for member in range(GROUP):
        left = member * SLICE
        qkv_cut[member] = jnp.concatenate(
            [
                qkv_wide[:, part * D + left : part * D + left + SLICE].astype(BRAIN)
                for part in range(3)
            ],
            axis=1,
        )

    def send_qkv(step):
        return remote(
            qkv_cut.at[mate(step)],
            qkv_own.at[block(shard, SLICE)],
            ID_QKV + step - 1,
            shard=mate(step),
        )

    def send_up(step):
        return remote(
            up_cut.at[mate(step)],
            up_own.at[block(shard, SLICE)],
            ID_UP + step - 1,
            shard=mate(step),
        )

    def send_out(step):
        here = block(shard, SLICE)
        return remote(out_all.at[here], out_all.at[here], ID_OUT + step - 1, shard=mate(step))

    for step in (2, 3, 1):
        push(functools.partial(send_qkv, step))
    qkv_own[block(shard, SLICE), :] = qkv_cut[shard]
    loads[3].wait()
    loads[4].wait()
    loads[5].wait()
    loads[6].wait()
    second_live = to_single(jnp.minimum(count_in[0] - 1, 1))
    live_rows = jnp.where(
        lax.broadcasted_iota(jnp.int32, (rows, 1), 0) < slot, 1.0, second_live
    )
    own = block(shard, rows)
    cotangent[own, :] = (to_single(cotangent[own, :]) * live_rows).astype(BRAIN)
    out_all[block(shard, SLICE), :] = out_wide[...].astype(BRAIN)
    for member in range(GROUP):
        up_cut[member] = up_wide[:, member * D : (member + 1) * D].astype(BRAIN)
    up_own[block(shard, SLICE), :] = up_cut[shard]
    down_own[...] = down_wide[...].astype(BRAIN)
    columns[...] = jnp.zeros_like(columns)
    pairs_grad[...] = jnp.zeros_like(pairs_grad)

    gather_forward(tokens, ID_TOKENS)
    for step in (1, 2, 3):
        remote(
            vectors.at[shard], vectors.at[mate(step)], ID_VECTORS + step - 1, shard=mate(step)
        ).wait_recv()
    for step in (1, 2, 3):
        send_qkv(step).wait_recv()

    for step in (2, 3, 1):
        push(functools.partial(send_out, step))
    for step in (2, 3, 1):
        push(functools.partial(send_up, step))
    gather_start(cotangent, ID_COTANGENT)

    def whole(row):
        return jnp.concatenate([vectors[member, row : row + 1, :] for member in range(GROUP)], 1)

    def mine(row):
        return vectors[shard, row : row + 1, :]

    scale_row = jnp.where(
        lax.broadcasted_iota(jnp.int32, (1, 3 * SLICE), 1) < SLICE, HD**-0.5, 1.0
    )

    def project(step, carry):
        gather_wait(tokens, ID_TOKENS, step)
        here = block(mate(step), rows)
        normal, _ = normalize(to_single(tokens[here, :]))
        hidden = (normal * whole(G1) + whole(B1)).astype(BRAIN)
        hidden_one[here, :] = hidden
        bias = jnp.concatenate([mine(BQ), jnp.zeros((1, SLICE), SINGLE), mine(BV)], 1)
        product = (dot(hidden, qkv_own[...], 1, 0) + bias) * scale_row
        pairs[here, :] = product.astype(BRAIN)
        return carry

    lax.fori_loop(0, GROUP, project, 0)

    def clip_rows(ref, clip, left):
        return jnp.concatenate(
            [
                ref[pl.ds(pl.multiple_of(member * rows + clip * slot, slot), slot), left : left + HD]
                for member in range(GROUP)
            ],
            0,
        )

    def mixed_part(owner, clip):
        return mixed.at[owner, :, pl.ds(pl.multiple_of(clip * slot, slot), slot), :]

    def mix_near(clip):
        return remote(
            mixed_part(shard, clip), mixed_part(shard, clip), ID_MIX + clip, shard=mate(1)
        )

    def mix_across(clip):
        return remote(
            mixed_part(shard, clip), mixed_part(shard, clip), ID_MIX + 2 + clip, shard=mate(2)
        )

    def mix_on(clip):
        return remote(
            mixed_part(mate(2), clip), mixed_part(mate(2), clip), ID_MIX + 4 + clip, shard=mate(1)
        )

    def attend(clip, carry):
        for head in range(LOCAL_HEADS):
            query = clip_rows(pairs, clip, head * HD)
            key = clip_rows(pairs, clip, SLICE + head * HD)
            value = clip_rows(pairs, clip, 2 * SLICE + head * HD)
            scores = dot(key, query, 1, 1)
            highest = jnp.max(scores, axis=0, keepdims=True)
            expanded = jnp.exp(scores - highest)
            softened = expanded * (1.0 / row_sum(expanded))
            soft[clip * LOCAL_HEADS + head] = softened
            mixture = dot(value.T, softened.astype(BRAIN), 1, 0).T.astype(BRAIN)
            for member in range(GROUP):
                mixed[
                    shard,
                    member,
                    pl.ds(pl.multiple_of(clip * slot, slot), slot),
                    head * HD : (head + 1) * HD,
                ] = mixture[member * slot : (member + 1) * slot]
        mix_across(clip).start()
        mix_near(clip).start()
        return carry

    lax.fori_loop(0, 2, attend, 0)
    gather_forward(cotangent, ID_COTANGENT)
    for clip in (0, 1):
        finals.append(functools.partial(mix_near, clip))
        finals.append(functools.partial(mix_across, clip))
        mix_across(clip).wait_recv()
        push(functools.partial(mix_on, clip))
    for step in (1, 2, 3):
        send_out(step).wait_recv()
        send_up(step).wait_recv()
    gather_near(cotangent, ID_COTANGENT).wait_recv()
    gather_on(cotangent, ID_COTANGENT).wait_recv()
    for clip in (0, 1):
        mix_near(clip).wait_recv()
        mix_on(clip).wait_recv()

    def sum_near_copy(which, base, part):
        return remote(
            sum_sent.at[which, part], sum_near.at[which, part], base + part, shard=mate(1)
        )

    def sum_far_copy(which, base):
        return remote(sum_sent.at[which, 2], sum_far.at[which], base + 2, shard=mate(2))

    def sum_step(which, base, step, value):
        sum_own[which] = value

        @pl.when(step == 0)
        def _():
            sum_sent[which, 0] = sum_own[which].astype(BRAIN)
            sum_near_copy(which, base, 0).start()

        @pl.when(step == 1)
        def _():
            sum_near_copy(which, base, 0).wait_recv()
            sum_sent[which, 2] = (sum_own[which] + to_single(sum_near[which, 0])).astype(BRAIN)
            sum_far_copy(which, base).start()

        @pl.when(step == 2)
        def _():
            sum_sent[which, 1] = sum_own[which].astype(BRAIN)
            sum_near_copy(which, base, 1).start()

    def sum_end(which, base):
        sum_near_copy(which, base, 0).wait_send()
        sum_near_copy(which, base, 1).wait()
        sum_far_copy(which, base).wait()
        return sum_own[which] + to_single(sum_near[which, 1]) + to_single(sum_far[which])

    def feed(step, carry):
        chunk = mate(3 - step)
        here = block(chunk, rows)
        total = to_single(tokens[here, :]) + whole(BO)
        for member in range(GROUP):
            total += dot(
                mixed[member, chunk], out_all[member * SLICE : (member + 1) * SLICE, :], 1, 0
            )

        @pl.when(step == 3)
        def _():
            middle_own[...] = total

        normal, _ = normalize(total)
        hidden = (normal * whole(G2) + whole(B2)).astype(BRAIN)
        hidden_two[here, :] = hidden
        bias = jnp.concatenate(
            [vectors[shard, C1 + part : C1 + part + 1, :] for part in range(GROUP)], 1
        )
        lifted = dot(hidden, up_own[...], 1, 0) + bias
        share = 0.5 + 0.5 * lax.erf(lifted * (0.5**0.5))
        active[here, :] = (lifted * share).astype(BRAIN)
        slope = share + lifted * jnp.exp(lifted * lifted * -0.5) * 0.3989422804014327
        down = cotangent[here, :]
        columns[0:1, :] += row_sum(to_single(down))
        grad = (dot(down, down_own[...], 1, 1) * slope).astype(BRAIN)
        lifted_grad[here, :] = grad
        columns[1:2, :] += row_sum(to_single(grad))
        sum_step(0, ID_SUM_TWO, step, dot(grad, up_own[...], 1, 1))
        return carry

    lax.fori_loop(0, GROUP, feed, 0)

    stages = {}

    def weight(name, number, grad, halves, quarters, piece, crossed, full, outers):
        base = ID_WEIGHTS + 16 * number
        blocks = piece.shape[0]
        my_half = pl.ds(pl.multiple_of(y * HALF, HALF), HALF)
        their_half = pl.ds(pl.multiple_of((1 - y) * HALF, HALF), HALF)
        source = piece if crossed is None else crossed

        def piece_rows(step):
            return pl.ds(pl.multiple_of(z_at(step) * PIECE, PIECE), PIECE)

        def y_copy():
            return remote(grad.at[:, :, their_half], halves, base, replica=y_peer)

        def z_copy(step):
            return remote(
                halves.at[:, piece_rows(step), :],
                quarters.at[step - 1],
                base + step,
                replica=z_peer(step),
            )

        def cross_copy(step):
            return remote(
                piece.at[mate(step)], crossed.at[shard], base + 3 + step, shard=mate(step)
            )

        def z_back(step):
            return remote(
                source,
                full.at[y, :, piece_rows(0), :],
                base + 6 + step,
                replica=z_peer(step),
            )

        def y_back(step):
            part = full.at[y, :, piece_rows(-step + MIDDLE), :]
            return remote(part, part, base + 10 + step, replica=y_peer)

        def y_start():
            push(y_copy)

        def z_start():
            y_copy().wait_recv()
            for index in range(blocks):
                halves[index] = (
                    to_single(grad[index, :, my_half]) + to_single(halves[index])
                ).astype(BRAIN)
            for step in (2, 1, 3):
                push(functools.partial(z_copy, step))

        def outer_start():
            for step in (1, 2, 3):
                z_copy(step).wait_recv()
            for index in range(blocks):
                total = to_single(halves[index, piece_rows(0), :])
                for step in (1, 2, 3):
                    total += to_single(quarters[step - 1, index])
                piece[index] = total.astype(BRAIN)
            if outers is not None:
                outers[far] = piece[...]

                def outer_copy(step):
                    return pltpu.make_async_remote_copy(
                        src_ref=piece,
                        dst_ref=outers.at[far],
                        send_sem=send_all.at[number + 1, step],
                        recv_sem=recv_all.at[number + 1, step],
                        device_id={
                            "replica": replica
                            + 2 * MIDDLE * ((far + step) % outer - far)
                        },
                        device_id_type=MESH,
                    )

                for step in range(1, outer):
                    outer_copy(step).start()
                for step in range(1, outer):
                    outer_copy(step).wait()
                total = to_single(outers[0])
                for step in range(1, outer):
                    total += to_single(outers[step])
                piece[...] = total.astype(BRAIN)
            if crossed is not None:
                crossed[shard] = piece[shard]
                for step in (2, 3, 1):
                    push(functools.partial(cross_copy, step))

        def back_start():
            if crossed is not None:
                for step in (1, 2, 3):
                    cross_copy(step).wait_recv()
            for step in (2, 1, 3):
                push(functools.partial(z_back, step))
            for index in range(blocks):
                full[y, index, piece_rows(0), :] = source[index]
            push(functools.partial(y_back, 0))

        def back_on():
            for step in (1, 3, 2):
                z_back(step).wait_recv()
                push(functools.partial(y_back, step))

        def back_end():
            for step in range(MIDDLE):
                y_back(step).wait_recv()

        stages[name] = (y_start, z_start, outer_start, back_start, back_on, back_end)

    weight(
        "down", 0, up_cut, y_down, z_down, piece_down, None, full_down,
        outer_down if outer > 1 else None,
    )
    weight(
        "up", 1, qkv_grad.at[1], y_up, z_up, piece_up, cross_up, full_up,
        outer_up if outer > 1 else None,
    )
    weight(
        "out", 2, out_grad, y_out, z_out, piece_out, None, full_out,
        outer_out if outer > 1 else None,
    )
    weight(
        "qkv", 3, qkv_grad.at[0], y_qkv, z_qkv, piece_qkv, cross_qkv, full_qkv,
        outer_qkv if outer > 1 else None,
    )

    def run(name, stage):
        stages[name][stage]()

    for step in (1, 2, 3):
        send_up(step).wait_send()
    finals[:] = [item for item in finals if getattr(item, "func", None) is not send_up]

    def cut_product(target, left, right, width):
        for part in range(2):
            product = dot(left[:, part * HALF : (part + 1) * HALF], right[...], 0, 0)
            for half in range(2):
                target[2 * part + half, :, 0:width] = product[
                    half * SLICE : (half + 1) * SLICE
                ].astype(BRAIN)

    cut_product(up_cut, active, cotangent, D)
    run("down", 0)
    cut_product(qkv_grad.at[1], hidden_two, lifted_grad, D)
    run("up", 0)

    grad_two = sum_end(0, ID_SUM_TWO)
    normal, scale = normalize(middle_own[...])
    own_cotangent = to_single(cotangent[own, :])
    small_sent_rows = [row_sum(grad_two * normal), row_sum(grad_two)]
    total = own_cotangent + norm_back(grad_two, normal, scale, whole(G2))
    middle_grad[...] = total
    gradient[own, :] = total.astype(BRAIN)
    gather_start(gradient, ID_GRADIENT)
    columns[2:3, :] = small_sent_rows[0]
    columns[3:4, :] = small_sent_rows[1]

    def lower(step, carry):
        here = block(mate(3 - step), rows)
        sum_step(1, ID_SUM_RESULT, step, dot(active[here, :], down_own[...], 1, 0))
        return carry

    lax.fori_loop(0, GROUP, lower, 0)
    run("down", 1)
    gather_forward(gradient, ID_GRADIENT)
    run("up", 1)

    def back_out(step, carry):
        gather_wait(gradient, ID_GRADIENT, step)
        chunk = mate(step)
        grad = gradient[block(chunk, rows), :]
        columns[4:5, :] += row_sum(to_single(grad))
        mixed_grad[block(chunk, rows), :] = dot(
            grad, out_all[block(shard, SLICE), :], 1, 1
        ).astype(BRAIN)
        return carry

    lax.fori_loop(0, GROUP, back_out, 0)
    out_grad[0] = dot(mixed[shard].reshape(group_rows, SLICE), gradient[...], 0, 0).astype(BRAIN)
    run("out", 0)
    result = (
        middle_own[...] + sum_end(1, ID_SUM_RESULT) + whole(C2)
    ) * live_rows
    result_stage[...] = result.astype(BRAIN)
    result_copy = local(result_stage, outputs_out, 7)
    result_copy.start()

    def attend_back(clip, carry):
        for head in range(LOCAL_HEADS):
            query = clip_rows(pairs, clip, head * HD)
            key = clip_rows(pairs, clip, SLICE + head * HD)
            value = clip_rows(pairs, clip, 2 * SLICE + head * HD)
            grad = clip_rows(mixed_grad, clip, head * HD)
            softened = soft[clip * LOCAL_HEADS + head]
            grad_soft = dot(value, grad, 1, 1)
            inner = row_sum(grad_soft * softened)
            grad_scores = (softened * (grad_soft - inner)).astype(BRAIN)
            parts = (
                (dot(key.T, grad_scores, 1, 0).T * HD**-0.5).astype(BRAIN),
                dot(grad_scores, query, 1, 0).astype(BRAIN),
                dot(softened.astype(BRAIN), grad, 1, 0).astype(BRAIN),
            )
            for part, entry in enumerate(parts):
                left = part * SLICE + head * HD
                for member in range(GROUP):
                    pairs_grad[
                        pl.ds(pl.multiple_of(member * rows + clip * slot, slot), slot),
                        left : left + HD,
                    ] = entry[member * slot : (member + 1) * slot]
        return carry

    attend_back(0, 0)
    run("down", 2)
    run("up", 2)
    run("out", 1)
    attend_back(1, 0)
    run("down", 3)
    run("up", 3)

    cut_product(qkv_grad.at[0], hidden_one, pairs_grad, 3 * SLICE)
    qkv_grad[0, :, :, 3 * SLICE :] = jnp.zeros((GROUP, SLICE, SLICE), BRAIN)
    run("qkv", 0)

    def back_project(step, carry):
        here = block(mate(3 - step), rows)
        grad = pairs_grad[here, :]
        columns[5:6, 0 : 3 * SLICE] += row_sum(to_single(grad))
        sum_step(0, ID_SUM_ONE, step, dot(grad, qkv_own[...], 1, 1))
        return carry

    lax.fori_loop(0, GROUP, back_project, 0)
    run("out", 2)
    run("down", 4)
    run("up", 4)
    run("qkv", 1)
    run("out", 3)

    grad_one = sum_end(0, ID_SUM_ONE)
    normal, scale = normalize(to_single(tokens[own, :]))
    columns[6:7, :] = row_sum(grad_one * normal)
    columns[7:8, :] = row_sum(grad_one)
    middle_grad[...] += norm_back(grad_one, normal, scale, whole(G1))
    grad_copy = local(middle_grad, input_grad_out, 8)
    grad_copy.start()

    for member in range(GROUP):
        at = slice(member * SLICE, (member + 1) * SLICE)
        for place, row in enumerate((6, 7, 2, 3, 4, 0)):
            small_sent[member, place : place + 1, :] = columns[row : row + 1, at]

    def small_copy(step):
        return remote(
            small_sent.at[mate(step)], small_near.at[step - 1], ID_SMALL + step - 1, shard=mate(step)
        )

    for step in (1, 2, 3):
        push(functools.partial(small_copy, step))
    run("qkv", 2)
    run("out", 4)
    for step in (1, 2, 3):
        small_copy(step).wait_recv()
    summed = (
        small_sent[shard, 0:4, :] + small_near[0, 0:4, :] + small_near[1, 0:4, :] + small_near[2, 0:4, :]
    )
    small_all[replica, G1 : G1 + 2, :] = summed[0:2]
    small_all[replica, G2 : G2 + 2, :] = summed[2:4]
    small_all[replica, BO : BO + 1, :] = small_sent[shard, 4:5, :]
    small_all[replica, C2 : C2 + 1, :] = small_sent[shard, 5:6, :]
    small_all[replica, BQ : BQ + 1, :] = columns[5:6, 0:SLICE]
    small_all[replica, BV : BV + 1, :] = columns[5:6, 2 * SLICE : 3 * SLICE]
    for part in range(GROUP):
        small_all[replica, C1 + part : C1 + part + 1, :] = columns[
            1:2, part * SLICE : (part + 1) * SLICE
        ]
    small_all[replica, C1 + GROUP :, :] = jnp.zeros((VECTOR_ROWS - C1 - GROUP, SLICE), SINGLE)

    def spread_copy(step):
        return pltpu.make_async_remote_copy(
            src_ref=small_all.at[replica],
            dst_ref=small_all.at[replica],
            send_sem=send_all.at[0, step],
            recv_sem=recv_all.at[0, step],
            device_id={"replica": (replica + step) % replicas},
            device_id_type=MESH,
        )

    def spread_start(step, carry):
        spread_copy(step).start()
        return carry

    lax.fori_loop(1, replicas, spread_start, 0)

    run("down", 5)
    for index in range(GROUP):
        for half in range(2):
            down_wide[
                index * SLICE : (index + 1) * SLICE, half * HALF : (half + 1) * HALF
            ] = to_single(full_down[half, index])
    down_copy = local(down_wide, down_out, 9)
    down_copy.start()
    run("up", 5)
    for index in range(GROUP):
        for half in range(2):
            left = index * D + half * HALF
            up_wide[:, left : left + HALF] = to_single(full_up[half, index])
    up_copy = local(up_wide, up_out, 10)
    up_copy.start()
    run("qkv", 3)
    run("out", 5)
    for half in range(2):
        out_wide[:, half * HALF : (half + 1) * HALF] = to_single(full_out[half, 0])
    out_copy = local(out_wide, out_out, 11)
    out_copy.start()
    run("qkv", 4)

    def spread_wait(step, carry):
        spread_copy(step).wait()
        return carry

    lax.fori_loop(1, replicas, spread_wait, 0)
    small_sum = small_all[0]
    for step in range(1, replicas):
        small_sum += small_all[step]
    small_all[0] = small_sum
    vectors_copy = local(small_all.at[0], vectors_out, 12)
    vectors_copy.start()
    run("qkv", 5)
    for part in range(3):
        half, left = ((0, 0), (0, SLICE), (1, 0))[part]
        qkv_wide[:, part * D : (part + 1) * D] = to_single(
            jnp.concatenate(
                [full_qkv[half, index, :, left : left + SLICE] for index in range(GROUP)], 1
            )
        )
    qkv_copy = local(qkv_wide, qkv_out, 13)
    qkv_copy.start()
    for item in finals:
        item().wait_send()
    for item in (result_copy, grad_copy, down_copy, up_copy, out_copy, vectors_copy, qkv_copy):
        item.wait()


def local(replicas, *arguments):
    (
        tokens, cotangent, clip_count, ln1_gain, ln1_bias, qkv_weight, q_bias, v_bias,
        out_weight, out_bias, ln2_gain, ln2_bias, fc1_weight, fc1_bias, fc2_weight, fc2_bias,
    ) = arguments
    slots, local_tokens, _ = tokens.shape
    rows = slots * local_tokens
    group_rows = rows * GROUP
    outer = replicas // (2 * MIDDLE)
    table = jnp.stack(
        [ln1_gain, ln1_bias, out_bias, ln2_gain, ln2_bias, fc2_bias, q_bias, v_bias]
        + [fc1_bias[part * SLICE : (part + 1) * SLICE] for part in range(GROUP)]
        + [jnp.zeros_like(ln1_gain)] * (VECTOR_ROWS - C1 - GROUP)
    )
    table = table.astype(BRAIN).astype(SINGLE)
    counts = (GROUP, GROUP, 1, GROUP)
    scratch = [
        pltpu.VMEM((SLICE, 3 * D), SINGLE),
        pltpu.VMEM((SLICE, D), SINGLE),
        pltpu.VMEM((SLICE, 4 * D), SINGLE),
        pltpu.VMEM((D, D), SINGLE),
        pltpu.VMEM((GROUP, SLICE, 3 * SLICE), BRAIN),
        pltpu.VMEM((GROUP, SLICE, D), BRAIN),
        pltpu.VMEM((D, 3 * SLICE), BRAIN),
        pltpu.VMEM((D, D), BRAIN),
        pltpu.VMEM((D, D), BRAIN),
        pltpu.VMEM((D, D), BRAIN),
        pltpu.VMEM((GROUP, VECTOR_ROWS, SLICE), SINGLE),
        pltpu.VMEM((group_rows, D), BRAIN),
        pltpu.VMEM((group_rows, D), BRAIN),
        pltpu.VMEM((group_rows, D), BRAIN),
        pltpu.VMEM((group_rows, 3 * SLICE), BRAIN),
        pltpu.VMEM((2 * LOCAL_HEADS, group_rows // 2, group_rows // 2), SINGLE),
        pltpu.VMEM((GROUP, GROUP, rows, SLICE), BRAIN),
        pltpu.VMEM((rows, D), SINGLE),
        pltpu.VMEM((group_rows, D), BRAIN),
        pltpu.VMEM((group_rows, D), BRAIN),
        pltpu.VMEM((group_rows, D), BRAIN),
        pltpu.VMEM((group_rows, D), BRAIN),
        pltpu.VMEM((rows, D), SINGLE),
        pltpu.VMEM((group_rows, SLICE), BRAIN),
        pltpu.VMEM((group_rows, 3 * SLICE), BRAIN),
        pltpu.VMEM((2, 3, rows, D), BRAIN),
        pltpu.VMEM((2, 2, rows, D), BRAIN),
        pltpu.VMEM((2, rows, D), BRAIN),
        pltpu.VMEM((2, rows, D), SINGLE),
        pltpu.VMEM((1, SLICE, D), BRAIN),
        pltpu.VMEM((2, GROUP, SLICE, D), BRAIN),
    ]
    scratch += [pltpu.VMEM((count, SLICE, HALF), BRAIN) for count in counts]
    scratch += [pltpu.VMEM((MIDDLE - 1, count, PIECE, HALF), BRAIN) for count in counts]
    scratch += [pltpu.VMEM((count, PIECE, HALF), BRAIN) for count in counts]
    scratch += [pltpu.VMEM((GROUP, PIECE, HALF), BRAIN) for _ in range(2)]
    scratch += [pltpu.VMEM((2, count, SLICE, HALF), BRAIN) for count in counts]
    scratch += [
        pltpu.VMEM((8, D), SINGLE),
        pltpu.VMEM((GROUP, 8, SLICE), SINGLE),
        pltpu.VMEM((GROUP - 1, 8, SLICE), SINGLE),
        pltpu.VMEM((replicas, VECTOR_ROWS, SLICE), SINGLE),
        pltpu.VMEM((rows, D), BRAIN),
    ]
    if outer > 1:
        scratch += [pltpu.VMEM((outer, count, PIECE, HALF), BRAIN) for count in counts]
    scratch += [
        pltpu.SemaphoreType.DMA((COPIES,)),
        pltpu.SemaphoreType.DMA((COPIES,)),
        pltpu.SemaphoreType.DMA((5, replicas)),
        pltpu.SemaphoreType.DMA((5, replicas)),
        pltpu.SemaphoreType.DMA((LOCALS,)),
    ]
    anywhere = pl.BlockSpec(memory_space=pl.ANY)
    outputs, input_grad, small, qkv_grad, out_grad, up_grad, down_grad = pl.pallas_call(
        functools.partial(kernel, replicas),
        out_shape=(
            jax.ShapeDtypeStruct((rows, D), BRAIN),
            jax.ShapeDtypeStruct((rows, D), SINGLE),
            jax.ShapeDtypeStruct((VECTOR_ROWS, SLICE), SINGLE),
            jax.ShapeDtypeStruct(qkv_weight.shape, SINGLE),
            jax.ShapeDtypeStruct(out_weight.shape, SINGLE),
            jax.ShapeDtypeStruct(fc1_weight.shape, SINGLE),
            jax.ShapeDtypeStruct(fc2_weight.shape, SINGLE),
        ),
        in_specs=[
            anywhere,
            anywhere,
            pl.BlockSpec(memory_space=pltpu.SMEM),
            anywhere,
            anywhere,
            anywhere,
            anywhere,
            anywhere,
        ],
        out_specs=(anywhere,) * 7,
        scratch_shapes=scratch,
        compiler_params=pltpu.CompilerParams(
            collective_id=0, has_side_effects=True, vmem_limit_bytes=65000 * 1024
        ),
        name="layer",
    )(
        tokens.reshape(rows, D),
        cotangent.reshape(rows, D),
        clip_count,
        table,
        qkv_weight,
        out_weight,
        fc1_weight,
        fc2_weight,
    )
    return (
        outputs.reshape(tokens.shape),
        input_grad.reshape(tokens.shape),
        small[G1],
        small[B1],
        qkv_grad,
        small[BQ],
        small[BV],
        out_grad,
        small[BO],
        small[G2],
        small[B2],
        up_grad,
        small[C1 : C1 + GROUP].reshape(-1),
        down_grad,
        small[C2],
    )


def solution(mesh):
    token, vector, matrix = P("replica", "shard", None), P("shard"), P("shard", None)
    return jax.shard_map(
        functools.partial(local, mesh.shape["replica"]),
        mesh=mesh,
        in_specs=(
            token, token, P("replica"), vector, vector, matrix, vector, vector,
            matrix, vector, vector, vector, matrix, vector, matrix, vector,
        ),
        out_specs=(
            token, token, vector, vector, matrix, vector, vector, matrix,
            vector, vector, vector, matrix, vector, matrix, vector,
        ),
        check_vma=False,
    )
```

```python
import functools
import types

import jax
import jax.numpy as jnp
from jax import lax
from jax.experimental import pallas as pl
from jax.experimental.pallas import tpu as pltpu
from jax.sharding import PartitionSpec as P

D = 768
HD = 64
EPSILON = 1e-06
GROUP = 4
SLICE = D // GROUP
LOCAL_HEADS = SLICE // HD
HALF = D // 2
TILE = 128
PAIR = SLICE // 2
PIECE = SLICE // 4
QKV = 3 * SLICE
BRAIN = jnp.bfloat16
SINGLE = jnp.float32
MESH = pl.DeviceIdType.MESH

G1, B1, BO, G2, B2, C2, BQ, BV, C1 = range(9)
VECTOR_ROWS = 16

WEIGHTS = (
    (GROUP, D, False, ((0, 128, True), (128, 128, True), (256, 128, True), (384, 128, True), (512, 256, False))),
    (GROUP, D, True, ((0, 128, True), (128, 128, True), (256, 128, True), (384, 128, True), (512, 256, False))),
    (1, D, False, ((0, 768, False),)),
    (GROUP, 640, True, ((0, 128, True), (128, 128, True), (256, 128, True), (384, 128, True), (512, 128, True))),
)
DOWN, UP, OUT, QKVS = range(4)
ITEMS = sum(len(parts) for _, _, _, parts in WEIGHTS)

MIXES = (((0, 0), (0, 1)), ((0, 2), (1, 2)), ((1, 0), (1, 1)))


PLAN = (
    (),
    (),
    (1, 41, 11, 21),
    (),
    (91, 31),
    (2, 51),
    (12, 61),
    (),
    (22, 3, 4),
    (32, 13, 14),
    (),
    (52, 23, 24, 71),
    (81, 33, 62),
    (42, 72, 53),
    (5, 34, 82),
    (),
    (15, 92, 63),
    (25,),
    (),
    (73, 35, 43, 44, 111, 83, 101),
    (),
    (74, 121, 84, 131, 93, 141, 75, 64, 54, 112, 151, 85, 122, 45, 65, 113, 132, 102),
    (55, 123, 142, 114, 133, 152),
    (124, 94, 115, 134, 125, 143, 103, 104, 153, 144, 135, 154, 95, 145, 105, 155),
)


class Names:
    def __init__(self):
        self.total = 0

    def take(self, count):
        first = self.total
        self.total += count
        return first


ids = Names()
ID_TOKENS = ids.take(6)
ID_COTANGENT = ids.take(6)
ID_GRADIENT = ids.take(6)
ID_VECTORS = ids.take(3)
ID_QKV = ids.take(9)
ID_OUT = ids.take(9)
ID_UP = ids.take(9)
ID_MIX = ids.take(9)
ID_SUM_TWO = ids.take(6)
ID_SUM_RESULT = ids.take(6)
ID_SUM_ONE = ids.take(6)
ID_SMALL = ids.take(3)
ID_WEIGHTS = ids.take(9 * ITEMS)
COPIES = ids.total
LOCALS = 32


def to_single(value):
    return value.astype(SINGLE)


def rounded(value):
    return value.astype(BRAIN).astype(SINGLE)


def dot(left, right, left_dim, right_dim):
    return lax.dot_general(
        left, right, (((left_dim,), (right_dim,)), ((), ())), preferred_element_type=SINGLE
    )


def normalize(value):
    mean = jnp.sum(value, axis=-1, keepdims=True) * (1.0 / D)
    centred = value - mean
    spread = jnp.sum(centred * centred, axis=-1, keepdims=True) * (1.0 / D)
    scale = lax.rsqrt(spread + EPSILON)
    return centred * scale, scale


def norm_back(grad, normal, scale, gain):
    scaled = grad * gain
    first = jnp.sum(scaled, axis=-1, keepdims=True) * (1.0 / D)
    second = jnp.sum(scaled * normal, axis=-1, keepdims=True) * (1.0 / D)
    return scale * (scaled - first - normal * second)


def row_sum(value):
    return jnp.sum(value, axis=0, keepdims=True)


def gathered(fields, refs):
    result, refs = {}, list(refs)
    for name, count in fields:
        result[name] = [refs.pop(0) for _ in range(count)] if count > 1 else refs.pop(0)
    return types.SimpleNamespace(**result)


def counted(fields):
    return [(name, len(entry) if isinstance(entry, list) else 1) for name, entry in fields.items()]


def flat(fields):
    result = []
    for entry in fields.values():
        result += entry if isinstance(entry, list) else [entry]
    return result


def kernel(replicas, fields, *refs):
    r = gathered(fields, refs)
    levels = (replicas // 8).bit_length() - 1
    slot = r.tokens_in.shape[1]
    pair = 2 * slot
    length = GROUP * slot

    shard = lax.axis_index("shard")
    replica = lax.axis_index("replica")
    chip = shard // 2
    core = shard % 2
    y = replica % 2
    z_low = (replica // 2) % 2
    z_high = (replica // 4) % 2
    inner = (z_low + z_high) % 2 == 1
    edge = (z_low + z_high) % 2 == 0
    block_of_eight = replica // 8
    y_peer = replica + 1 - 2 * y
    z_pair = replica + 2 * (1 - 2 * z_low)

    def mate(step):
        return 2 * ((chip + step // 2) % 2) + (shard + step) % 2

    finals, conditional = [], []

    def remote(source, target, index, **where):
        return pltpu.make_async_remote_copy(
            src_ref=source,
            dst_ref=target,
            send_sem=r.send.at[index],
            recv_sem=r.recv.at[index],
            device_id=where,
            device_id_type=MESH,
        )

    def push(make, *arguments):
        make(*arguments).start()
        finals.append(functools.partial(make, *arguments))

    def push_if(condition, make, *arguments):
        @pl.when(condition)
        def _():
            make(*arguments).start()

        conditional.append((condition, functools.partial(make, *arguments)))

    def local(source, target, index):
        return pltpu.make_async_copy(source, target, r.near.at[index])

    def at(index, size, offset=0):
        return pl.ds(pl.multiple_of(index * size + offset, size), size)

    def here(ref, clip):
        return ref.at[clip, at(shard, slot), :]

    qkv_load = local(r.qkv_in, r.qkv_wide, 0)
    token_loads = [local(r.tokens_in.at[clip], here(r.tokens, clip), 1 + clip) for clip in (0, 1)]
    vector_loads = [
        local(r.vectors_in[row], r.vectors_raw[row], 3 + row)
        for row in range(9)
    ]
    cotangent_loads = [
        local(r.cotangent_in.at[clip], here(r.cotangent, clip), 12 + clip) for clip in (0, 1)
    ]
    wide_loads = [
        local(r.up_in, r.up_wide, 14),
        local(r.out_in, r.out_wide, 15),
        local(r.down_in, r.down_wide, 16),
    ]
    for load in [qkv_load] + token_loads + vector_loads + cotangent_loads + wide_loads:
        load.start()
    barrier = pltpu.get_barrier_semaphore()
    for step in (1, 2, 3):
        pl.semaphore_signal(barrier, inc=1, device_id={"shard": mate(step)}, device_id_type=MESH)

    def greet(step, carry):
        peer = (replica + step) % replicas
        pl.semaphore_signal(barrier, inc=1, device_id={"replica": peer}, device_id_type=MESH)
        return carry

    lax.fori_loop(1, replicas, greet, 0)
    qkv_load.wait()
    for member in range(GROUP):
        left = member * SLICE
        r.qkv_cut[member] = jnp.concatenate(
            [
                r.qkv_wide[:, part * D + left : part * D + left + SLICE].astype(BRAIN)
                for part in range(3)
            ],
            axis=1,
        )
    for load in token_loads + vector_loads:
        load.wait()
    pl.semaphore_wait(barrier, replicas + 2)

    def gather_part(buffer, clip, member):
        return buffer.at[clip, at(member, slot), :]

    def gather_near(buffer, base, clip):
        part = gather_part(buffer, clip, shard)
        return remote(part, part, base + 3 * clip, shard=mate(1))

    def gather_across(buffer, base, clip):
        part = gather_part(buffer, clip, shard)
        return remote(part, part, base + 3 * clip + 1, shard=mate(2))

    def gather_on(buffer, base, clip):
        part = gather_part(buffer, clip, mate(2))
        return remote(part, part, base + 3 * clip + 2, shard=mate(1))

    def gather_start(buffer, base, clip):
        push(gather_across, buffer, base, clip)
        push(gather_near, buffer, base, clip)

    def gather_forward(buffer, base, clip):
        gather_across(buffer, base, clip).wait_recv()
        push(gather_on, buffer, base, clip)

    def quarter(member, y_side, z_side):
        return at((member * 2 + y_side) * 2 + z_side, PIECE)

    def share_across(cut, buffer, base, step):
        source = buffer.at[quarter(shard, y, z_low), :]
        if cut is not None:
            source = cut.at[mate(step), at(2 * y + z_low, PIECE), :]
        return remote(
            source, buffer.at[quarter(shard, y, z_low), :], base + step - 2, shard=mate(step)
        )

    def share_z(buffer, base, step):
        part = buffer.at[quarter(mate(step), y, z_low), :]
        return remote(part, part, base + step, replica=z_pair)

    def share_y(buffer, base, step, second):
        side = 1 - z_low if second else z_low
        part = buffer.at[quarter(mate(step), y, side), :]
        return remote(part, part, base + 2 * second + 2 + step, replica=y_peer)

    def share_near(cut, buffer, base):
        target = buffer.at[at(shard, SLICE), :]
        source = target if cut is None else cut.at[mate(1)]
        return remote(source, target, base + 8, shard=mate(1))

    def share_start(cut, buffer, base, steps):
        for step in steps:
            push(share_across, cut, buffer, base, step)
        push(share_near, cut, buffer, base)

    def share_on(cut, buffer, base, steps):
        for step in steps:
            share_across(cut, buffer, base, step).wait_recv()
            push(share_z, buffer, base, step)
            push(share_y, buffer, base, step, 0)

    def share_last(buffer, base, steps):
        for step in steps:
            share_z(buffer, base, step).wait_recv()
            push(share_y, buffer, base, step, 1)

    def share_wait(cut, buffer, base, steps):
        for step in steps:
            share_y(buffer, base, step, 0).wait_recv()
            share_y(buffer, base, step, 1).wait_recv()
        share_near(cut, buffer, base).wait_recv()

    BOTH, ONE = (2, 3), (2,)

    share_start(r.qkv_cut, r.qkv_own, ID_QKV, BOTH)
    gather_start(r.tokens, ID_TOKENS, 0)
    for row in range(8):
        r.vectors[shard, row : row + 1, :] = rounded(
            r.vectors_raw[row][...].reshape(1, SLICE)
        )
    long_row = rounded(r.vectors_raw[8][...].reshape(1, D))
    for part in range(GROUP):
        r.vectors[shard, C1 + part : C1 + part + 1, :] = long_row[
            :, part * SLICE : (part + 1) * SLICE
        ]
    r.vectors[shard, C1 + GROUP :, :] = jnp.zeros((VECTOR_ROWS - C1 - GROUP, SLICE), SINGLE)

    def send_vectors(step):
        return remote(
            r.vectors.at[shard], r.vectors.at[shard], ID_VECTORS + step - 1, shard=mate(step)
        )

    for step in (1, 2, 3):
        push(send_vectors, step)
    for load in wide_loads:
        load.wait()
    for member in range(GROUP):
        r.up_cut[member] = r.up_wide[:, member * D : (member + 1) * D].astype(BRAIN)
    r.out_all[at(shard, SLICE), :] = r.out_wide[...].astype(BRAIN)
    share_start(None, r.out_all, ID_OUT, ONE)
    share_start(r.up_cut, r.up_own, ID_UP, BOTH)
    gather_start(r.tokens, ID_TOKENS, 1)

    r.qkv_own[at(shard, SLICE), :] = r.qkv_cut[shard]
    share_on(r.qkv_cut, r.qkv_own, ID_QKV, BOTH)
    for load in cotangent_loads:
        load.wait()
    second_live = to_single(jnp.minimum(r.count_in[0] - 1, 1))
    own = at(shard, slot)
    r.cotangent[1, own, :] = (to_single(r.cotangent[1, own, :]) * second_live).astype(BRAIN)
    r.up_own[at(shard, SLICE), :] = r.up_cut[shard]
    r.down_own[...] = r.down_wide[...].astype(BRAIN)
    r.columns[...] = jnp.zeros_like(r.columns)
    share_last(r.qkv_own, ID_QKV, BOTH)
    gather_forward(r.tokens, ID_TOKENS, 0)

    def whole(row):
        return jnp.concatenate([r.vectors[member, row : row + 1, :] for member in range(GROUP)], 1)

    def mine(row):
        return r.vectors[shard, row : row + 1, :]

    for step in (1, 2, 3):
        send_vectors(step).wait_recv()
    share_wait(r.qkv_cut, r.qkv_own, ID_QKV, BOTH)
    scale_row = jnp.where(lax.broadcasted_iota(jnp.int32, (1, QKV), 1) < SLICE, HD**-0.5, 1.0)
    qkv_bias = jnp.concatenate([mine(BQ), jnp.zeros((1, SLICE), SINGLE), mine(BV)], 1)

    def project(clip, side):
        rows = at((chip + side) % 2, pair)
        normal, _ = normalize(to_single(r.tokens[clip, rows, :]))
        hidden = (normal * whole(G1) + whole(B1)).astype(BRAIN)
        r.hidden_one[clip, rows, :] = hidden
        product = (dot(hidden, r.qkv_own[...], 1, 0) + qkv_bias) * scale_row
        r.pairs[clip, rows, :] = product.astype(BRAIN)

    def mix_near(part):
        ref = r.mixed.at[shard, part]
        return remote(ref, ref, ID_MIX + 3 * part, shard=mate(1))

    def mix_across(part):
        ref = r.mixed.at[shard, part]
        return remote(ref, ref, ID_MIX + 3 * part + 1, shard=mate(2))

    def mix_on(part):
        ref = r.mixed.at[mate(2), part]
        return remote(ref, ref, ID_MIX + 3 * part + 2, shard=mate(1))

    def mix_forward(part):
        mix_across(part).wait_recv()
        push(mix_on, part)

    def head_of(ref, clip, left):
        return ref[clip, :, left : left + HD]

    def attend(part, place):
        clip, head = MIXES[part][place]
        query = head_of(r.pairs, clip, head * HD)
        key = head_of(r.pairs, clip, SLICE + head * HD)
        value = head_of(r.pairs, clip, 2 * SLICE + head * HD)
        scores = dot(key, query, 1, 1)
        highest = jnp.max(scores, axis=0, keepdims=True)
        expanded = jnp.exp(scores - highest)
        softened = expanded * (1.0 / row_sum(expanded))
        r.soft[clip * LOCAL_HEADS + head] = softened
        mixture = dot(value.T, softened.astype(BRAIN), 1, 0).T.astype(BRAIN)
        r.mixed[shard, part, :, place * HD : (place + 1) * HD] = mixture

    def mix_start(part):
        push(mix_across, part)
        push(mix_near, part)

    gather_near(r.tokens, ID_TOKENS, 0).wait_recv()
    project(0, 0)
    gather_on(r.tokens, ID_TOKENS, 0).wait_recv()
    project(0, 1)
    attend(0, 0)
    share_on(None, r.out_all, ID_OUT, ONE)
    share_on(r.up_cut, r.up_own, ID_UP, BOTH)
    attend(0, 1)
    mix_start(0)
    attend(1, 0)
    gather_near(r.tokens, ID_TOKENS, 1).wait_recv()
    project(1, 0)
    gather_forward(r.tokens, ID_TOKENS, 1)
    gather_on(r.tokens, ID_TOKENS, 1).wait_recv()
    project(1, 1)
    attend(1, 1)
    mix_start(1)
    gather_start(r.cotangent, ID_COTANGENT, 0)
    share_last(r.out_all, ID_OUT, ONE)
    share_last(r.up_own, ID_UP, BOTH)
    mix_forward(0)
    attend(2, 0)
    attend(2, 1)
    mix_start(2)
    gather_start(r.cotangent, ID_COTANGENT, 1)

    def out_on():
        part = r.out_all.at[at(mate(2), SLICE), :]
        return remote(part, part, ID_OUT + 1, shard=mate(1))

    share_wait(None, r.out_all, ID_OUT, ONE)
    push(out_on)
    mix_forward(1)
    out_on().wait_recv()
    for part in (0, 1):
        mix_near(part).wait_recv()
        mix_on(part).wait_recv()
    share_wait(r.up_cut, r.up_own, ID_UP, BOTH)

    def sum_near(which, base, clip, kind):
        return remote(
            r.sum_sent.at[which, clip, kind],
            r.sum_near.at[which, clip, kind],
            base + 3 * clip + kind,
            shard=mate(1),
        )

    def sum_far(which, base, clip):
        return remote(
            r.sum_sent.at[which, clip, 2],
            r.sum_far.at[which, clip],
            base + 3 * clip + 2,
            shard=mate(2),
        )

    def sum_kept(which, clip, kind):
        if which == 0:
            return r.sum_own.at[clip, kind]
        return r.up_wide.at[0:slot, at(2 * clip + kind, D)]

    def sum_step(which, base, clip, kind, value):
        r.stage[...] = value
        r.sum_sent[which, clip, kind] = r.stage[at(1 - core, slot), :].astype(BRAIN)
        sum_kept(which, clip, kind)[...] = r.stage[at(core, slot), :]
        remote(
            r.sum_sent.at[which, clip, kind],
            r.sum_near.at[which, clip, kind],
            base + 3 * clip + kind,
            shard=mate(1),
        ).start()

    def sum_on(which, base, clip):
        sum_near(which, base, clip, 0).wait_recv()
        r.sum_sent[which, clip, 2] = (
            sum_kept(which, clip, 0)[...] + to_single(r.sum_near[which, clip, 0])
        ).astype(BRAIN)
        sum_far(which, base, clip).start()

    def sum_end(which, base, clip):
        sum_near(which, base, clip, 0).wait_send()
        sum_near(which, base, clip, 1).wait()
        sum_far(which, base, clip).wait()
        return (
            sum_kept(which, clip, 1)[...]
            + to_single(r.sum_near[which, clip, 1])
            + to_single(r.sum_far[which, clip])
        )

    def rows_of(kind):
        return at((chip + 1 + kind) % 2, pair)

    long_bias = jnp.concatenate(
        [r.vectors[shard, C1 + part : C1 + part + 1, :] for part in range(GROUP)], 1
    )

    def pass_on(across, on):
        across.wait_recv()
        on.start()

    def feed(clip, kind, carry):
        rows = rows_of(kind)
        if clip == 0:

            @pl.when(kind == 1)
            def _():
                pass_on(
                    gather_across(r.cotangent, ID_COTANGENT, 0),
                    gather_on(r.cotangent, ID_COTANGENT, 0),
                )

        total = to_single(r.tokens[clip, rows, :]) + whole(BO)
        for member in range(GROUP):
            heads = jnp.concatenate(
                [
                    r.mixed[member, 2 * clip, rows, :],
                    r.mixed[member, 1, rows, clip * HD : (clip + 1) * HD],
                ],
                1,
            )
            total += dot(heads, r.out_all[member * SLICE : (member + 1) * SLICE, :], 1, 0)

        @pl.when(kind == 1)
        def _():
            r.stage[...] = total
            r.middle_own[clip] = r.stage[at(core, slot), :]

        normal, _ = normalize(total)
        hidden = (normal * whole(G2) + whole(B2)).astype(BRAIN)
        r.hidden_two[clip, rows, :] = hidden
        lifted = dot(hidden, r.up_own[...], 1, 0) + long_bias
        share = 0.5 + 0.5 * lax.erf(lifted * (0.5**0.5))
        r.active[clip, rows, :] = (lifted * share).astype(BRAIN)
        r.down_wide[at(kind, pair), :] = share + lifted * jnp.exp(lifted * lifted * -0.5) * 0.3989422804014327
        return carry

    def feed_back(clip, kind, carry):
        rows = rows_of(kind)
        if clip == 0:

            @pl.when(kind == 1)
            def _():
                pass_on(mix_across(2), mix_on(2))

        down = r.cotangent[clip, rows, :]
        r.columns[0:1, :] += row_sum(to_single(down))
        grad = (dot(down, r.down_own[...], 1, 1) * r.down_wide[at(kind, pair), :]).astype(BRAIN)
        r.lifted_grad[clip, rows, :] = grad
        r.columns[1:2, :] += row_sum(to_single(grad))
        sum_step(0, ID_SUM_TWO, clip, kind, dot(grad, r.up_own[...], 1, 1))
        return carry

    def both(step, clip):
        lax.fori_loop(0, 2, functools.partial(step, clip), 0)

    both(feed, 0)
    finals.append(functools.partial(gather_on, r.cotangent, ID_COTANGENT, 0))
    gather_near(r.cotangent, ID_COTANGENT, 0).wait_recv()
    gather_on(r.cotangent, ID_COTANGENT, 0).wait_recv()
    both(feed_back, 0)
    finals.append(functools.partial(mix_on, 2))
    mix_near(2).wait_recv()
    mix_on(2).wait_recv()
    sum_on(0, ID_SUM_TWO, 0)
    both(feed, 1)
    gather_forward(r.cotangent, ID_COTANGENT, 1)
    gather_near(r.cotangent, ID_COTANGENT, 1).wait_recv()
    gather_on(r.cotangent, ID_COTANGENT, 1).wait_recv()
    stages = []

    def weight(index, number, crosses, columns, y_first, grad):
        base = ID_WEIGHTS + 9 * number
        halves, line, middle, full = (
            refs[index] for refs in (r.halves, r.lines, r.middles, r.fulls)
        )
        crossed = r.crossed[index // 2] if crosses else None
        blocks = grad.shape[0]
        cols = slice(columns[0], columns[0] + columns[1])
        size = PAIR if y_first else PIECE
        first, first_peer, second, second_peer = (
            (y, y_peer, z_low, z_pair) if y_first else (z_low, z_pair, y, y_peer)
        )
        source = (crossed if crosses else line).at[:, 0:size, cols]
        held = slice(0, PAIR) if y_first else at(second, PIECE)

        def final_rows(side):
            return at(first, PAIR) if y_first else at(2 * first + side, PIECE)

        def first_copy():
            return remote(
                grad.at[:, at(1 - first, PAIR), cols],
                halves.at[:, :, cols],
                base,
                replica=first_peer,
            )

        def second_copy():
            given = slice(0, PAIR) if y_first else at(1 - second, PIECE)
            return remote(
                halves.at[:, given, cols],
                line.at[:, 0:size, cols],
                base + 1,
                replica=second_peer,
            )

        def far_copy():
            apart = 2 if y_first else 4
            return remote(
                halves.at[:, held, cols],
                middle.at[:, 0:size, cols],
                base + 2,
                replica=replica + apart * (1 - 2 * z_high),
            )

        def farther_copy(level):
            apart = 8 * 2**level * (1 - 2 * ((block_of_eight // 2**level) % 2))
            return pltpu.make_async_remote_copy(
                src_ref=line.at[:, 0:size, cols],
                dst_ref=r.extras[index].at[level, :, 0:size, cols],
                send_sem=r.send_all.at[number + 1, level],
                recv_sem=r.recv_all.at[number + 1, level],
                device_id={"replica": replica + apart},
                device_id_type=MESH,
            )

        def cross_copy(step):
            return remote(
                line.at[mate(step), 0:size, cols],
                crossed.at[shard, 0:size, cols],
                base + 2 + step,
                shard=mate(step),
            )

        def second_back():
            return remote(
                source, full.at[:, final_rows(second), cols], base + 6, replica=second_peer
            )

        def first_back(late):
            if not late:
                return remote(
                    source, full.at[:, final_rows(second), cols], base + 7, replica=first_peer
                )
            ref = full.at[:, final_rows(1 - second), cols]
            return remote(ref, ref, base + 8 - y_first, replica=first_peer)

        def start():
            push(first_copy)

        def second_start():
            first_copy().wait_recv()
            for block in range(blocks):
                halves[block, :, cols] = (
                    to_single(grad[block, at(first, PAIR), cols])
                    + to_single(halves[block, :, cols])
                ).astype(BRAIN)
            if y_first:
                push_if(edge, second_copy)
            else:
                push(second_copy)

        def far_start():
            second_copy().wait_recv()
            for block in range(blocks):
                halves[block, held, cols] = (
                    to_single(halves[block, held, cols]) + to_single(line[block, 0:size, cols])
                ).astype(BRAIN)
            far_copy().start()

        def cross_start():
            far_copy().wait()
            for block in range(blocks):
                line[block, 0:size, cols] = (
                    to_single(halves[block, held, cols]) + to_single(middle[block, 0:size, cols])
                ).astype(BRAIN)
            for level in range(levels):
                farther_copy(level).start()
                farther_copy(level).wait()
                line[:, 0:size, cols] = (
                    to_single(line[:, 0:size, cols])
                    + to_single(r.extras[index][level, :, 0:size, cols])
                ).astype(BRAIN)
            if crosses:
                crossed[shard, 0:size, cols] = line[shard, 0:size, cols]
                for step in (2, 3, 1):
                    cross_copy(step).start()

        def back_start():
            if crosses:
                for step in (1, 2, 3):
                    cross_copy(step).wait()
            second_back().start()
            first_back(False).start()
            for block in range(blocks):
                full[block, final_rows(second), cols] = source[block]
            conditional.append((inner if y_first else None, second_back))
            conditional.append(
                (inner if y_first else None, functools.partial(first_back, False))
            )

        def back_on():
            second_back().wait_recv()
            push(first_back, True)

        def back_end():
            if not y_first:
                first_back(False).wait_recv()
            first_back(True).wait_recv()

        def only(condition, step):
            def run_if():
                pl.when(condition)(step)

            return run_if if y_first else step

        def edge_on():
            @pl.when(edge)
            def _():
                second_back().wait_recv()

            push_if(edge, first_back, True)

        stages.append(
            (
                start,
                second_start,
                only(inner, far_start),
                only(inner, cross_start),
                only(inner, back_start),
                edge_on if y_first else back_on,
                back_end,
            )
        )

    grads = (r.up_cut, r.up_grad, r.out_grad, r.qkv_grad)
    for index, (_, _, crosses, parts) in enumerate(WEIGHTS):
        for start_column, width, y_first in parts:
            weight(index, len(stages), crosses, (start_column, width), y_first, grads[index])

    def run(*codes):
        for code in codes:
            stages[code // 10][code % 10]()

    rest = []
    for item in finals:
        if item.func in (share_across, share_near) and item.args[0] is r.up_cut:
            item().wait_send()
        else:
            rest.append(item)
    finals[:] = rest

    def cut_product(target, left, right, width):
        for part in range(2):
            product = dot(
                left[:, :, part * HALF : (part + 1) * HALF].reshape(2 * length, HALF),
                right[...].reshape(2 * length, width),
                0,
                0,
            )
            for half in range(2):
                target[2 * part + half, :, 0:width] = product[
                    half * SLICE : (half + 1) * SLICE
                ].astype(BRAIN)

    steps = iter(PLAN)

    def plan():
        run(*next(steps))

    cut_product(r.up_cut, r.active, r.cotangent, D)
    run(40, 0, 10, 20, 30)
    plan()
    both(feed_back, 1)
    sum_on(0, ID_SUM_TWO, 1)
    cut_product(r.up_grad, r.hidden_two, r.lifted_grad, D)
    run(90, 50, 60, 70, 80)
    plan()

    for clip in (0, 1):
        grad_two = sum_end(0, ID_SUM_TWO, clip)
        normal, scale = normalize(r.middle_own[clip])
        r.columns[2:3, :] += row_sum(grad_two * normal)
        r.columns[3:4, :] += row_sum(grad_two)
        total = to_single(r.cotangent[clip, own, :]) + norm_back(
            grad_two, normal, scale, whole(G2)
        )
        r.down_wide[4 * slot + clip * slot : 5 * slot + clip * slot, :] = total
        r.gradient[clip, own, :] = total.astype(BRAIN)
        gather_start(r.gradient, ID_GRADIENT, clip)
        plan()

    def lower(clip, kind, carry):
        value = dot(r.active[clip, rows_of(kind), :], r.down_own[...], 1, 0)
        sum_step(1, ID_SUM_RESULT, clip, kind, value)
        return carry

    for clip in (0, 1):
        both(lower, clip)
        plan()

    def back_out(clip):
        gather_near(r.gradient, ID_GRADIENT, clip).wait_recv()
        gather_on(r.gradient, ID_GRADIENT, clip).wait_recv()
        grad = r.gradient[clip]
        r.columns[4:5, :] += row_sum(to_single(grad))
        r.mixed_grad[clip] = dot(grad, r.out_all[at(shard, SLICE), :], 1, 1).astype(BRAIN)

    def attend_back(clip, head):
        query = head_of(r.pairs, clip, head * HD)
        key = head_of(r.pairs, clip, SLICE + head * HD)
        value = head_of(r.pairs, clip, 2 * SLICE + head * HD)
        grad = head_of(r.mixed_grad, clip, head * HD)
        softened = r.soft[clip * LOCAL_HEADS + head]
        grad_soft = dot(value, grad, 1, 1)
        inner = row_sum(grad_soft * softened)
        grad_scores = (softened * (grad_soft - inner)).astype(BRAIN)
        entries = (
            (dot(key.T, grad_scores, 1, 0).T * HD**-0.5).astype(BRAIN),
            dot(grad_scores, query, 1, 0).astype(BRAIN),
            dot(softened.astype(BRAIN), grad, 1, 0).astype(BRAIN),
        )
        for part, entry in enumerate(entries):
            left = part * SLICE + head * HD
            r.pairs_grad[clip, :, left : left + HD] = entry

    for clip in (0, 1):
        gather_forward(r.gradient, ID_GRADIENT, clip)
        plan()
        back_out(clip)
        plan()
        if clip == 1:
            for other in (0, 1):
                sum_on(1, ID_SUM_RESULT, other)
        for head in range(LOCAL_HEADS):
            attend_back(clip, head)
            plan()
    product = None
    for clip in (0, 1):
        heads = jnp.concatenate(
            [r.mixed[shard, 2 * clip], r.mixed[shard, 1, :, clip * HD : (clip + 1) * HD]], 1
        )
        term = dot(heads, r.gradient[clip], 0, 0)
        product = term if product is None else product + term
    r.out_grad[0] = product.astype(BRAIN)
    run(100)
    plan()
    cut_product(r.qkv_grad, r.hidden_one, r.pairs_grad, QKV)
    r.qkv_grad[:, :, QKV:] = jnp.zeros((GROUP, SLICE, HD), BRAIN)
    run(110, 120, 130, 140, 150)
    plan()

    def back_project(clip, kind, carry):
        grad = r.pairs_grad[clip, rows_of(kind), :]
        r.columns[5:6, 0:QKV] += row_sum(to_single(grad))
        sum_step(0, ID_SUM_ONE, clip, kind, dot(grad, r.qkv_own[...], 1, 1))
        return carry

    for clip in (0, 1):
        both(back_project, clip)
        plan()
    for clip in (0, 1):
        sum_on(0, ID_SUM_ONE, clip)
    plan()
    for clip in (0, 1):
        live = 1.0 if clip == 0 else second_live
        result = r.middle_own[clip] + sum_end(1, ID_SUM_RESULT, clip) + whole(C2)
        r.hidden_one[clip, 0:slot, :] = (result * live).astype(BRAIN)
    result_copy = local(r.hidden_one.at[:, 0:slot, :], r.result_out, 17)
    result_copy.start()
    plan()
    for clip in (0, 1):
        grad_one = sum_end(0, ID_SUM_ONE, clip)
        normal, scale = normalize(to_single(r.tokens[clip, own, :]))
        r.columns[6:7, :] += row_sum(grad_one * normal)
        r.columns[7:8, :] += row_sum(grad_one)
        r.down_wide[4 * slot + clip * slot : 5 * slot + clip * slot, :] += norm_back(grad_one, normal, scale, whole(G1))
    grad_copies = [
        local(
            r.down_wide.at[4 * slot + clip * slot : 5 * slot + clip * slot],
            r.input_grad_out.at[clip],
            18 + 6 * clip,
        )
        for clip in (0, 1)
    ]
    for item in grad_copies:
        item.start()

    for member in range(GROUP):
        cols = slice(member * SLICE, (member + 1) * SLICE)
        for place, row in enumerate((6, 7, 2, 3, 4, 0)):
            r.small_sent[member, place : place + 1, :] = r.columns[row : row + 1, cols]

    def small_copy(step):
        return remote(
            r.small_sent.at[mate(step)],
            r.small_near.at[step - 1],
            ID_SMALL + step - 1,
            shard=mate(step),
        )

    for step in (1, 2, 3):
        push(small_copy, step)
    plan()
    for step in (1, 2, 3):
        small_copy(step).wait_recv()
    summed = r.small_sent[shard, 0:4, :]
    for step in (1, 2, 3):
        summed += r.small_near[step - 1, 0:4, :]
    r.small_all[replica, G1 : G1 + 2, :] = summed[0:2]
    r.small_all[replica, G2 : G2 + 2, :] = summed[2:4]
    r.small_all[replica, BO : BO + 1, :] = r.small_sent[shard, 4:5, :]
    r.small_all[replica, C2 : C2 + 1, :] = r.small_sent[shard, 5:6, :]
    r.small_all[replica, BQ : BQ + 1, :] = r.columns[5:6, 0:SLICE]
    r.small_all[replica, BV : BV + 1, :] = r.columns[5:6, 2 * SLICE : QKV]
    for part in range(GROUP):
        r.small_all[replica, C1 + part : C1 + part + 1, :] = r.columns[
            1:2, part * SLICE : (part + 1) * SLICE
        ]
    r.small_all[replica, C1 + GROUP :, :] = jnp.zeros((VECTOR_ROWS - C1 - GROUP, SLICE), SINGLE)

    def spread_copy(step):
        return pltpu.make_async_remote_copy(
            src_ref=r.small_all.at[replica],
            dst_ref=r.small_all.at[replica],
            send_sem=r.send_all.at[0, step],
            recv_sem=r.recv_all.at[0, step],
            device_id={"replica": (replica + step) % replicas},
            device_id_type=MESH,
        )

    def spread_start(step, carry):
        spread_copy(step).start()
        return carry

    lax.fori_loop(1, replicas, spread_start, 0)
    plan()

    def spread_wait(step, carry):
        spread_copy(step).wait()
        return carry

    lax.fori_loop(1, replicas, spread_wait, 0)
    small_sum = r.small_all[0]
    for step in range(1, replicas):
        small_sum += r.small_all[step]
    r.small_all[0] = small_sum
    copies = grad_copies + [result_copy, local(r.small_all.at[0], r.small_out, 19)]
    copies[-1].start()
    run(106)
    copies.append(local(r.fulls[OUT], r.sums_out[OUT], 20))
    copies[-1].start()
    run(6, 16, 26, 36, 46)
    copies.append(local(r.fulls[DOWN], r.sums_out[DOWN], 21))
    copies[-1].start()
    run(116, 126, 136, 146, 156)
    copies.append(local(r.fulls[QKVS], r.sums_out[QKVS], 22))
    copies[-1].start()
    run(56, 66, 76, 86, 96)
    copies.append(local(r.fulls[UP], r.sums_out[UP], 23))
    copies[-1].start()
    for item in finals:
        item().wait_send()
    for condition, item in conditional:
        if condition is None:
            item().wait_send()
        else:

            @pl.when(condition)
            def _():
                item().wait_send()

    for item in copies:
        item.wait()


def finish(fields, *refs):
    r = gathered(fields, refs)
    units = []

    def unit(source, held, wide, target, widen):
        index = len(units)
        units.append(
            (
                pltpu.make_async_copy(source, held, r.near.at[index]),
                pltpu.make_async_copy(wide, target, r.near.at[index]),
                widen,
            )
        )

    def keep():
        pass

    def down(index):
        rows = slice(index * SLICE, (index + 1) * SLICE)

        def widen():
            r.wide[DOWN][rows, :] = to_single(r.narrow[DOWN][index])

        unit(
            r.sums_in[DOWN].at[index],
            r.narrow[DOWN].at[index],
            r.wide[DOWN].at[rows],
            r.results[DOWN].at[rows],
            widen,
        )

    def up(index):
        cols = slice(index * D, (index + 1) * D)

        def widen():
            r.wide[UP][:, cols] = to_single(r.narrow[UP][index])

        unit(
            r.sums_in[UP].at[index],
            r.narrow[UP].at[index],
            r.wide[UP].at[:, cols],
            r.results[UP].at[:, cols],
            widen,
        )

    def qkv(index):
        rows = slice(index * PIECE, (index + 1) * PIECE)

        def widen():
            for part in range(3):
                cols = slice(part * SLICE, (part + 1) * SLICE)
                r.wide[QKVS][rows, part * D : (part + 1) * D] = to_single(
                    jnp.concatenate(
                        [r.narrow[QKVS][member, rows, cols] for member in range(GROUP)], 1
                    )
                )

        unit(
            r.sums_in[QKVS].at[:, rows],
            r.narrow[QKVS].at[:, rows],
            r.wide[QKVS].at[rows],
            r.results[QKVS].at[rows],
            widen,
        )

    def out():
        def widen():
            r.wide[OUT][...] = to_single(r.narrow[OUT][0])

        unit(r.sums_in[OUT], r.narrow[OUT], r.wide[OUT], r.results[OUT], widen)

    unit(r.input_grad_in, r.input_grad_held, r.input_grad_held, r.input_grad, keep)
    unit(r.result_in, r.result_held, r.result_held, r.result, keep)
    for index in range(GROUP):
        down(index)
        up(index)
    out()
    for index in range(GROUP):
        qkv(index)
    for load, _, _ in units:
        load.start()
    for row in range(8):
        r.vectors[row][...] = r.small_in[row : row + 1, :].reshape(SLICE)
    r.vectors[8][...] = jnp.concatenate(
        [r.small_in[C1 + part : C1 + part + 1, :] for part in range(GROUP)], 1
    ).reshape(D)
    for load, store, widen in units:
        load.wait()
        widen()
        store.start()
    for _, store, _ in units:
        store.wait()


def layer(replicas, *arguments):
    (
        tokens, cotangent, clip_count, ln1_gain, ln1_bias, qkv_weight, q_bias, v_bias,
        out_weight, out_bias, ln2_gain, ln2_bias, fc1_weight, fc1_bias, fc2_weight, fc2_bias,
    ) = arguments
    slots, slot, _ = tokens.shape
    length = slot * GROUP
    levels = (replicas // 8).bit_length() - 1
    vectors = (
        ln1_gain, ln1_bias, out_bias, ln2_gain, ln2_bias, fc2_bias, q_bias, v_bias, fc1_bias,
    )
    anywhere = pl.BlockSpec(memory_space=pl.ANY)
    in_memory = pl.BlockSpec(memory_space=pltpu.VMEM)
    in_hbm = pl.BlockSpec(memory_space=pltpu.HBM)
    shape = jax.ShapeDtypeStruct

    inputs = dict(
        tokens_in=anywhere,
        cotangent_in=anywhere,
        count_in=pl.BlockSpec(memory_space=pltpu.SMEM),
        vectors_in=[anywhere] * 9,
        qkv_in=anywhere,
        out_in=anywhere,
        up_in=anywhere,
        down_in=anywhere,
    )
    outputs = dict(
        result_out=shape(tokens.shape, BRAIN),
        input_grad_out=shape(tokens.shape, SINGLE),
        small_out=shape((VECTOR_ROWS, SLICE), SINGLE),
        sums_out=[shape((blocks, SLICE, columns), BRAIN) for blocks, columns, _, _ in WEIGHTS],
    )
    scratch = dict(
        qkv_wide=pltpu.VMEM(qkv_weight.shape, SINGLE),
        out_wide=pltpu.VMEM(out_weight.shape, SINGLE),
        up_wide=pltpu.VMEM(fc1_weight.shape, SINGLE),
        down_wide=pltpu.VMEM(fc2_weight.shape, SINGLE),
        qkv_cut=pltpu.VMEM((GROUP, SLICE, QKV), BRAIN),
        up_cut=pltpu.VMEM((GROUP, SLICE, D), BRAIN),
        qkv_own=pltpu.VMEM((D, QKV), BRAIN),
        up_own=pltpu.VMEM((D, D), BRAIN),
        out_all=pltpu.VMEM((D, D), BRAIN),
        down_own=pltpu.VMEM((D, D), BRAIN),
        vectors=pltpu.VMEM((GROUP, VECTOR_ROWS, SLICE), SINGLE),
        vectors_raw=[pltpu.VMEM(vector.shape, SINGLE) for vector in vectors],
        tokens=pltpu.VMEM((2, length, D), BRAIN),
        cotangent=pltpu.VMEM((2, length, D), BRAIN),
        hidden_one=pltpu.VMEM((2, length, D), BRAIN),
        pairs=pltpu.VMEM((2, length, QKV), BRAIN),
        soft=pltpu.VMEM((2 * LOCAL_HEADS, length, length), SINGLE),
        mixed=pltpu.VMEM((GROUP, 3, length, TILE), BRAIN),
        middle_own=pltpu.VMEM((2, slot, D), SINGLE),
        hidden_two=pltpu.VMEM((2, length, D), BRAIN),
        active=pltpu.VMEM((2, length, D), BRAIN),
        lifted_grad=pltpu.VMEM((2, length, D), BRAIN),
        gradient=pltpu.VMEM((2, length, D), BRAIN),
        mixed_grad=pltpu.VMEM((2, length, SLICE), BRAIN),
        pairs_grad=pltpu.VMEM((2, length, QKV), BRAIN),
        stage=pltpu.VMEM((2 * slot, D), SINGLE),
        sum_sent=pltpu.VMEM((2, 2, 3, slot, D), BRAIN),
        sum_near=pltpu.VMEM((2, 2, 2, slot, D), BRAIN),
        sum_far=pltpu.VMEM((2, 2, slot, D), BRAIN),
        sum_own=pltpu.VMEM((2, 2, slot, D), SINGLE),
        up_grad=pltpu.VMEM((GROUP, SLICE, D), BRAIN),
        out_grad=pltpu.VMEM((1, SLICE, D), BRAIN),
        qkv_grad=pltpu.VMEM((GROUP, SLICE, QKV + HD), BRAIN),
        columns=pltpu.VMEM((8, D), SINGLE),
        small_sent=pltpu.VMEM((GROUP, 8, SLICE), SINGLE),
        small_near=pltpu.VMEM((GROUP - 1, 8, SLICE), SINGLE),
        small_all=pltpu.VMEM((replicas, VECTOR_ROWS, SLICE), SINGLE),
        halves=[pltpu.VMEM((w[0], PAIR, w[1]), BRAIN) for w in WEIGHTS],
        lines=[pltpu.VMEM((w[0], PAIR, w[1]), BRAIN) for w in WEIGHTS],
        middles=[pltpu.VMEM((w[0], PAIR, w[1]), BRAIN) for w in WEIGHTS],
        fulls=[pltpu.VMEM((w[0], SLICE, w[1]), BRAIN) for w in WEIGHTS],
        crossed=[pltpu.VMEM((GROUP, PAIR, w[1]), BRAIN) for w in WEIGHTS if w[2]],
        extras=[
            pltpu.VMEM((levels, w[0], PAIR, w[1]) if levels else (1, 1, 16, TILE), BRAIN)
            for w in WEIGHTS
        ],
        send=pltpu.SemaphoreType.DMA((COPIES,)),
        recv=pltpu.SemaphoreType.DMA((COPIES,)),
        send_all=pltpu.SemaphoreType.DMA((1 + ITEMS, replicas)),
        recv_all=pltpu.SemaphoreType.DMA((1 + ITEMS, replicas)),
        near=pltpu.SemaphoreType.DMA((LOCALS,)),
    )
    sums = pl.pallas_call(
        functools.partial(kernel, replicas, counted(inputs) + counted(outputs) + counted(scratch)),
        out_shape=tuple(flat(outputs)),
        in_specs=flat(inputs),
        out_specs=(anywhere,) * len(flat(outputs)),
        scratch_shapes=flat(scratch),
        compiler_params=pltpu.CompilerParams(
            collective_id=0, has_side_effects=True, vmem_limit_bytes=65000 * 1024
        ),
        name="layer",
    )(
        tokens, cotangent, clip_count, *vectors, qkv_weight, out_weight, fc1_weight, fc2_weight
    )

    matrices = [fc2_weight, fc1_weight, out_weight, qkv_weight]
    last_inputs = dict(
        result_in=in_hbm, input_grad_in=in_hbm, small_in=in_memory, sums_in=[in_hbm] * 4
    )
    last_outputs = dict(
        result=shape(tokens.shape, BRAIN),
        input_grad=shape(tokens.shape, SINGLE),
        results=[shape(array.shape, SINGLE) for array in matrices],
        vectors=[shape(vector.shape, SINGLE) for vector in vectors],
    )
    last_scratch = dict(
        narrow=[pltpu.VMEM((blocks, SLICE, columns), BRAIN) for blocks, columns, _, _ in WEIGHTS],
        wide=[pltpu.VMEM(array.shape, SINGLE) for array in matrices],
        input_grad_held=pltpu.VMEM(tokens.shape, SINGLE),
        result_held=pltpu.VMEM(tokens.shape, BRAIN),
        near=pltpu.SemaphoreType.DMA((16,)),
    )
    values = pl.pallas_call(
        functools.partial(
            finish, counted(last_inputs) + counted(last_outputs) + counted(last_scratch)
        ),
        out_shape=tuple(flat(last_outputs)),
        in_specs=flat(last_inputs),
        out_specs=(anywhere,) * 6 + (in_memory,) * 9,
        scratch_shapes=flat(last_scratch),
        compiler_params=pltpu.CompilerParams(vmem_limit_bytes=60 << 20),
        name="finish",
    )(*sums)
    o = gathered(counted(last_outputs), values)
    return (
        o.result,
        o.input_grad,
        o.vectors[G1],
        o.vectors[B1],
        o.results[QKVS],
        o.vectors[BQ],
        o.vectors[BV],
        o.results[OUT],
        o.vectors[BO],
        o.vectors[G2],
        o.vectors[B2],
        o.results[UP],
        o.vectors[C1],
        o.results[DOWN],
        o.vectors[C2],
    )


def solution(mesh):
    token, vector, matrix = P("replica", "shard", None), P("shard"), P("shard", None)
    return jax.shard_map(
        functools.partial(layer, mesh.shape["replica"]),
        mesh=mesh,
        in_specs=(
            token, token, P("replica"), vector, vector, matrix, vector, vector,
            matrix, vector, vector, vector, matrix, vector, matrix, vector,
        ),
        out_specs=(
            token, token, vector, vector, matrix, vector, vector, matrix,
            vector, vector, vector, matrix, vector, matrix, vector,
        ),
        check_vma=False,
    )
```

```python
import functools
import types

import jax
import jax.numpy as jnp
from jax import lax
from jax.experimental import pallas as pl
from jax.experimental.pallas import tpu as pltpu
from jax.sharding import PartitionSpec as P

D = 768
HD = 64
EPSILON = 1e-06
GROUP = 4
SLICE = D // GROUP
LOCAL_HEADS = SLICE // HD
HALF = D // 2
TILE = 128
PAIR = SLICE // 2
PIECE = SLICE // 4
QKV = 3 * SLICE
BRAIN = jnp.bfloat16
SINGLE = jnp.float32
MESH = pl.DeviceIdType.MESH

G1, B1, BO, G2, B2, C2, BQ, BV, C1 = range(9)
VECTOR_ROWS = 16

WEIGHTS = (
    (GROUP, D, False, ((0, 128, True), (128, 128, True), (256, 128, True), (384, 128, True), (512, 256, False))),
    (GROUP, D, True, ((0, 128, True), (128, 128, True), (256, 128, True), (384, 128, True), (512, 256, False))),
    (1, D, False, ((0, 768, False),)),
    (GROUP, 640, True, ((0, 128, True), (128, 128, True), (256, 128, True), (384, 128, True), (512, 128, True))),
)
DOWN, UP, OUT, QKVS = range(4)
ITEMS = sum(len(parts) for _, _, _, parts in WEIGHTS)

MIXES = (((0, 0), (0, 1)), ((0, 2), (1, 2)), ((1, 0), (1, 1)))


PLAN = (
    (),
    (),
    (1, 41, 11, 21),
    (),
    (91, 31),
    (2, 51),
    (12, 61),
    (),
    (22, 3, 4),
    (32, 13, 14),
    (),
    (52, 23, 24, 71),
    (81, 33, 62),
    (42, 72, 53),
    (5, 34, 82),
    (),
    (15, 92, 63),
    (25,),
    (),
    (73, 35, 43, 44, 111, 83, 101),
    (),
    (74, 121, 84, 131, 93, 141, 75, 64, 54, 112, 151, 85, 122, 45, 65, 113, 132, 102),
    (55, 123, 142, 114, 133, 152),
    (124, 94, 115, 134, 125, 143, 103, 104, 153, 144, 135, 154, 95, 145, 105, 155),
)


class Names:
    def __init__(self):
        self.total = 0

    def take(self, count):
        first = self.total
        self.total += count
        return first


ids = Names()
ID_TOKENS = ids.take(6)
ID_COTANGENT = ids.take(12)
ID_GRADIENT = ids.take(6)
ID_VECTORS = ids.take(3)
ID_QKV = ids.take(9)
ID_OUT = ids.take(9)
ID_UP = ids.take(9)
ID_MIX = ids.take(9)
ID_SUM_TWO = ids.take(6)
ID_SUM_RESULT = ids.take(6)
ID_SUM_ONE = ids.take(6)
ID_SMALL = ids.take(3)
ID_WEIGHTS = ids.take(9 * ITEMS)
COPIES = ids.total
LOCALS = 32


def to_single(value):
    return value.astype(SINGLE)


def rounded(value):
    return value.astype(BRAIN).astype(SINGLE)


def dot(left, right, left_dim, right_dim):
    return lax.dot_general(
        left, right, (((left_dim,), (right_dim,)), ((), ())), preferred_element_type=SINGLE
    )


def normalize(value):
    mean = jnp.sum(value, axis=-1, keepdims=True) * (1.0 / D)
    centred = value - mean
    spread = jnp.sum(centred * centred, axis=-1, keepdims=True) * (1.0 / D)
    scale = lax.rsqrt(spread + EPSILON)
    return centred * scale, scale


def norm_back(grad, normal, scale, gain):
    scaled = grad * gain
    first = jnp.sum(scaled, axis=-1, keepdims=True) * (1.0 / D)
    second = jnp.sum(scaled * normal, axis=-1, keepdims=True) * (1.0 / D)
    return scale * (scaled - first - normal * second)


def row_sum(value):
    return jnp.sum(value, axis=0, keepdims=True)


def gathered(fields, refs):
    result, refs = {}, list(refs)
    for name, count in fields:
        result[name] = [refs.pop(0) for _ in range(count)] if count > 1 else refs.pop(0)
    return types.SimpleNamespace(**result)


def counted(fields):
    return [(name, len(entry) if isinstance(entry, list) else 1) for name, entry in fields.items()]


def flat(fields):
    result = []
    for entry in fields.values():
        result += entry if isinstance(entry, list) else [entry]
    return result


def kernel(replicas, fields, *refs):
    r = gathered(fields, refs)
    levels = (replicas // 8).bit_length() - 1
    slot = r.tokens_in.shape[1]
    pair = 2 * slot
    length = GROUP * slot

    shard = lax.axis_index("shard")
    replica = lax.axis_index("replica")
    chip = shard // 2
    core = shard % 2
    y = replica % 2
    z_low = (replica // 2) % 2
    z_high = (replica // 4) % 2
    inner = (z_low + z_high) % 2 == 1
    edge = (z_low + z_high) % 2 == 0
    block_of_eight = replica // 8
    y_peer = replica + 1 - 2 * y
    z_pair = replica + 2 * (1 - 2 * z_low)

    def mate(step):
        return 2 * ((chip + step // 2) % 2) + (shard + step) % 2

    finals, conditional = [], []

    def remote(source, target, index, **where):
        return pltpu.make_async_remote_copy(
            src_ref=source,
            dst_ref=target,
            send_sem=r.send.at[index],
            recv_sem=r.recv.at[index],
            device_id=where,
            device_id_type=MESH,
        )

    def push(make, *arguments):
        make(*arguments).start()
        finals.append(functools.partial(make, *arguments))

    def push_if(condition, make, *arguments):
        @pl.when(condition)
        def _():
            make(*arguments).start()

        conditional.append((condition, functools.partial(make, *arguments)))

    def local(source, target, index):
        return pltpu.make_async_copy(source, target, r.near.at[index])

    def at(index, size, offset=0):
        return pl.ds(pl.multiple_of(index * size + offset, size), size)

    def here(ref, clip):
        return ref.at[clip, at(shard, slot), :]

    def quarter_rows(step):
        return at((2 * y + z_low + step) % 4, PIECE)

    qkv_loads = [
        local(r.qkv_in.at[quarter_rows(step)], r.qkv_wide.at[quarter_rows(step)], 25 + step)
        for step in range(4)
    ]
    token_loads = [local(r.tokens_in.at[clip], here(r.tokens, clip), 1 + clip) for clip in (0, 1)]
    vector_loads = [
        local(r.vectors_in[row], r.vectors_raw[row], 3 + row)
        for row in range(9)
    ]
    cotangent_loads = [
        local(r.cotangent_in.at[clip], here(r.cotangent, clip), 12 + clip) for clip in (0, 1)
    ]
    wide_loads = [
        local(r.up_in, r.up_wide, 14),
        local(r.out_in, r.out_wide, 15),
        local(r.down_in, r.down_wide, 16),
    ]
    for load in qkv_loads + token_loads + vector_loads + cotangent_loads + wide_loads:
        load.start()
    barrier = pltpu.get_barrier_semaphore()
    for step in (1, 2, 3):
        pl.semaphore_signal(barrier, inc=1, device_id={"shard": mate(step)}, device_id_type=MESH)

    def greet(step, carry):
        peer = (replica + step) % replicas
        pl.semaphore_signal(barrier, inc=1, device_id={"replica": peer}, device_id_type=MESH)
        return carry

    lax.fori_loop(1, replicas, greet, 0)

    def cut_rows(step):
        qkv_loads[step].wait()
        rows = quarter_rows(step)
        for member in range(GROUP):
            left = member * SLICE
            r.qkv_cut[member, rows, :] = jnp.concatenate(
                [
                    r.qkv_wide[rows, part * D + left : part * D + left + SLICE].astype(BRAIN)
                    for part in range(3)
                ],
                axis=1,
            )

    cut_rows(0)
    for load in token_loads + vector_loads:
        load.wait()
    pl.semaphore_wait(barrier, replicas + 2)

    def gather_part(buffer, clip, member):
        if clip >= 2:
            return buffer.at[0, at(2 * member + clip - 2, slot // 2), :]
        return buffer.at[clip, at(member, slot), :]

    def gather_near(buffer, base, clip):
        part = gather_part(buffer, clip, shard)
        return remote(part, part, base + 3 * clip, shard=mate(1))

    def gather_across(buffer, base, clip):
        part = gather_part(buffer, clip, shard)
        return remote(part, part, base + 3 * clip + 1, shard=mate(2))

    def gather_on(buffer, base, clip):
        part = gather_part(buffer, clip, mate(2))
        return remote(part, part, base + 3 * clip + 2, shard=mate(1))

    def gather_start(buffer, base, clip):
        push(gather_across, buffer, base, clip)
        push(gather_near, buffer, base, clip)

    def gather_forward(buffer, base, clip):
        gather_across(buffer, base, clip).wait_recv()
        push(gather_on, buffer, base, clip)

    def quarter(member, y_side, z_side):
        return at((member * 2 + y_side) * 2 + z_side, PIECE)

    def share_across(cut, buffer, base, step):
        source = buffer.at[quarter(shard, y, z_low), :]
        if cut is not None:
            source = cut.at[mate(step), at(2 * y + z_low, PIECE), :]
        return remote(
            source, buffer.at[quarter(shard, y, z_low), :], base + step - 2, shard=mate(step)
        )

    def share_z(buffer, base, step):
        part = buffer.at[quarter(mate(step), y, z_low), :]
        return remote(part, part, base + step, replica=z_pair)

    def share_y(buffer, base, step, second):
        side = 1 - z_low if second else z_low
        part = buffer.at[quarter(mate(step), y, side), :]
        return remote(part, part, base + 2 * second + 2 + step, replica=y_peer)

    def share_near(cut, buffer, base):
        target = buffer.at[at(shard, SLICE), :]
        source = target if cut is None else cut.at[mate(1)]
        return remote(source, target, base + 8, shard=mate(1))

    def share_first(cut, buffer, base, steps):
        for step in steps:
            push(share_across, cut, buffer, base, step)

    def share_start(cut, buffer, base, steps):
        share_first(cut, buffer, base, steps)
        push(share_near, cut, buffer, base)

    def share_on(cut, buffer, base, steps):
        for step in steps:
            share_across(cut, buffer, base, step).wait_recv()
            push(share_z, buffer, base, step)
            push(share_y, buffer, base, step, 0)

    def share_last(buffer, base, steps):
        for step in steps:
            share_z(buffer, base, step).wait_recv()
            push(share_y, buffer, base, step, 1)

    def share_wait(cut, buffer, base, steps):
        for step in steps:
            share_y(buffer, base, step, 0).wait_recv()
            share_y(buffer, base, step, 1).wait_recv()
        share_near(cut, buffer, base).wait_recv()

    BOTH, ONE = (2, 3), (2,)
    FIRST, SECOND = 2, 3

    share_first(r.qkv_cut, r.qkv_own, ID_QKV, BOTH)
    gather_start(r.tokens, ID_TOKENS, 0)
    for row in range(8):
        r.vectors[shard, row : row + 1, :] = rounded(
            r.vectors_raw[row][...].reshape(1, SLICE)
        )
    long_row = rounded(r.vectors_raw[8][...].reshape(1, D))
    for part in range(GROUP):
        r.vectors[shard, C1 + part : C1 + part + 1, :] = long_row[
            :, part * SLICE : (part + 1) * SLICE
        ]
    r.vectors[shard, C1 + GROUP :, :] = jnp.zeros((VECTOR_ROWS - C1 - GROUP, SLICE), SINGLE)

    def send_vectors(step):
        return remote(
            r.vectors.at[shard], r.vectors.at[shard], ID_VECTORS + step - 1, shard=mate(step)
        )

    for step in (1, 2, 3):
        push(send_vectors, step)
    for load in wide_loads:
        load.wait()
    for member in range(GROUP):
        r.up_cut[member] = r.up_wide[:, member * D : (member + 1) * D].astype(BRAIN)
    r.out_all[at(shard, SLICE), :] = r.out_wide[...].astype(BRAIN)
    share_start(None, r.out_all, ID_OUT, ONE)
    share_start(r.up_cut, r.up_own, ID_UP, BOTH)
    gather_start(r.tokens, ID_TOKENS, 1)

    for step in (1, 2, 3):
        cut_rows(step)
    push(share_near, r.qkv_cut, r.qkv_own, ID_QKV)
    r.qkv_own[at(shard, SLICE), :] = r.qkv_cut[shard]
    share_on(r.qkv_cut, r.qkv_own, ID_QKV, BOTH)
    for load in cotangent_loads:
        load.wait()
    second_live = to_single(jnp.minimum(r.count_in[0] - 1, 1))
    own = at(shard, slot)
    r.cotangent[1, own, :] = (to_single(r.cotangent[1, own, :]) * second_live).astype(BRAIN)
    r.up_own[at(shard, SLICE), :] = r.up_cut[shard]
    r.down_own[...] = r.down_wide[...].astype(BRAIN)
    r.columns[...] = jnp.zeros_like(r.columns)
    share_last(r.qkv_own, ID_QKV, BOTH)
    gather_forward(r.tokens, ID_TOKENS, 0)

    def whole(row):
        return jnp.concatenate([r.vectors[member, row : row + 1, :] for member in range(GROUP)], 1)

    def mine(row):
        return r.vectors[shard, row : row + 1, :]

    for step in (1, 2, 3):
        send_vectors(step).wait_recv()
    share_wait(r.qkv_cut, r.qkv_own, ID_QKV, BOTH)
    scale_row = jnp.where(lax.broadcasted_iota(jnp.int32, (1, QKV), 1) < SLICE, HD**-0.5, 1.0)
    qkv_bias = jnp.concatenate([mine(BQ), jnp.zeros((1, SLICE), SINGLE), mine(BV)], 1)

    def project(clip, side):
        rows = at((chip + side) % 2, pair)
        normal, _ = normalize(to_single(r.tokens[clip, rows, :]))
        hidden = (normal * whole(G1) + whole(B1)).astype(BRAIN)
        r.hidden_one[clip, rows, :] = hidden
        product = (dot(hidden, r.qkv_own[...], 1, 0) + qkv_bias) * scale_row
        r.pairs[clip, rows, :] = product.astype(BRAIN)

    def mix_near(part):
        ref = r.mixed.at[shard, part]
        return remote(ref, ref, ID_MIX + 3 * part, shard=mate(1))

    def mix_across(part):
        ref = r.mixed.at[shard, part]
        return remote(ref, ref, ID_MIX + 3 * part + 1, shard=mate(2))

    def mix_on(part):
        ref = r.mixed.at[mate(2), part]
        return remote(ref, ref, ID_MIX + 3 * part + 2, shard=mate(1))

    def mix_forward(part):
        mix_across(part).wait_recv()
        push(mix_on, part)

    def head_of(ref, clip, left):
        return ref[clip, :, left : left + HD]

    def attend(part, place):
        clip, head = MIXES[part][place]
        query = head_of(r.pairs, clip, head * HD)
        key = head_of(r.pairs, clip, SLICE + head * HD)
        value = head_of(r.pairs, clip, 2 * SLICE + head * HD)
        scores = dot(key, query, 1, 1)
        highest = jnp.max(scores, axis=0, keepdims=True)
        expanded = jnp.exp(scores - highest)
        softened = expanded * (1.0 / row_sum(expanded))
        r.soft[clip * LOCAL_HEADS + head] = softened
        mixture = dot(value.T, softened.astype(BRAIN), 1, 0).T.astype(BRAIN)
        r.mixed[shard, part, :, place * HD : (place + 1) * HD] = mixture

    def mix_start(part):
        push(mix_across, part)
        push(mix_near, part)

    gather_near(r.tokens, ID_TOKENS, 0).wait_recv()
    project(0, 0)
    gather_on(r.tokens, ID_TOKENS, 0).wait_recv()
    project(0, 1)
    attend(0, 0)
    share_on(None, r.out_all, ID_OUT, ONE)
    share_on(r.up_cut, r.up_own, ID_UP, BOTH)
    attend(0, 1)
    mix_start(0)
    gather_start(r.cotangent, ID_COTANGENT, FIRST)
    attend(1, 0)
    gather_near(r.tokens, ID_TOKENS, 1).wait_recv()
    project(1, 0)
    gather_forward(r.tokens, ID_TOKENS, 1)
    gather_on(r.tokens, ID_TOKENS, 1).wait_recv()
    project(1, 1)
    attend(1, 1)
    mix_start(1)
    gather_start(r.cotangent, ID_COTANGENT, SECOND)
    share_last(r.out_all, ID_OUT, ONE)
    share_last(r.up_own, ID_UP, BOTH)
    mix_forward(0)
    attend(2, 0)
    attend(2, 1)
    mix_start(2)
    gather_start(r.cotangent, ID_COTANGENT, 1)

    def out_on():
        part = r.out_all.at[at(mate(2), SLICE), :]
        return remote(part, part, ID_OUT + 1, shard=mate(1))

    share_wait(None, r.out_all, ID_OUT, ONE)
    push(out_on)
    mix_forward(1)
    out_on().wait_recv()
    for part in (0, 1):
        mix_near(part).wait_recv()
        mix_on(part).wait_recv()
    share_wait(r.up_cut, r.up_own, ID_UP, BOTH)

    def sum_near(which, base, clip, kind):
        return remote(
            r.sum_sent.at[which, clip, kind],
            r.sum_near.at[which, clip, kind],
            base + 3 * clip + kind,
            shard=mate(1),
        )

    def sum_far(which, base, clip):
        return remote(
            r.sum_sent.at[which, clip, 2],
            r.sum_far.at[which, clip],
            base + 3 * clip + 2,
            shard=mate(2),
        )

    def sum_kept(which, clip, kind):
        if which == 0:
            return r.sum_own.at[clip, kind]
        return r.up_wide.at[0:slot, at(2 * clip + kind, D)]

    def sum_step(which, base, clip, kind, value):
        r.stage[...] = value
        r.sum_sent[which, clip, kind] = r.stage[at(1 - core, slot), :].astype(BRAIN)
        sum_kept(which, clip, kind)[...] = r.stage[at(core, slot), :]
        remote(
            r.sum_sent.at[which, clip, kind],
            r.sum_near.at[which, clip, kind],
            base + 3 * clip + kind,
            shard=mate(1),
        ).start()

    def sum_on(which, base, clip):
        sum_near(which, base, clip, 0).wait_recv()
        r.sum_sent[which, clip, 2] = (
            sum_kept(which, clip, 0)[...] + to_single(r.sum_near[which, clip, 0])
        ).astype(BRAIN)
        sum_far(which, base, clip).start()

    def sum_end(which, base, clip):
        sum_near(which, base, clip, 0).wait_send()
        sum_near(which, base, clip, 1).wait()
        sum_far(which, base, clip).wait()
        return (
            sum_kept(which, clip, 1)[...]
            + to_single(r.sum_near[which, clip, 1])
            + to_single(r.sum_far[which, clip])
        )

    def rows_of(kind):
        return at((chip + 1 + kind) % 2, pair)

    long_bias = jnp.concatenate(
        [r.vectors[shard, C1 + part : C1 + part + 1, :] for part in range(GROUP)], 1
    )

    def pass_on(across, on):
        across.wait_recv()
        on.start()

    def feed(clip, kind, carry):
        rows = rows_of(kind)

        @pl.when(kind == 1)
        def _():
            for part in ((FIRST, SECOND), (1,))[clip]:
                pass_on(
                    gather_across(r.cotangent, ID_COTANGENT, part),
                    gather_on(r.cotangent, ID_COTANGENT, part),
                )

        total = to_single(r.tokens[clip, rows, :]) + whole(BO)
        for member in range(GROUP):
            heads = jnp.concatenate(
                [
                    r.mixed[member, 2 * clip, rows, :],
                    r.mixed[member, 1, rows, clip * HD : (clip + 1) * HD],
                ],
                1,
            )
            total += dot(heads, r.out_all[member * SLICE : (member + 1) * SLICE, :], 1, 0)

        @pl.when(kind == 1)
        def _():
            r.stage[...] = total
            r.middle_own[clip] = r.stage[at(core, slot), :]

        normal, _ = normalize(total)
        hidden = (normal * whole(G2) + whole(B2)).astype(BRAIN)
        r.hidden_two[clip, rows, :] = hidden
        lifted = dot(hidden, r.up_own[...], 1, 0) + long_bias
        share = 0.5 + 0.5 * lax.erf(lifted * (0.5**0.5))
        r.active[clip, rows, :] = (lifted * share).astype(BRAIN)
        r.down_wide[at(kind, pair), :] = share + lifted * jnp.exp(lifted * lifted * -0.5) * 0.3989422804014327
        return carry

    def feed_back(clip, kind, carry):
        rows = rows_of(kind)
        if clip == 0:

            @pl.when(kind == 1)
            def _():
                pass_on(mix_across(2), mix_on(2))

        down = r.cotangent[clip, rows, :]
        r.columns[0:1, :] += row_sum(to_single(down))
        grad = (dot(down, r.down_own[...], 1, 1) * r.down_wide[at(kind, pair), :]).astype(BRAIN)
        r.lifted_grad[clip, rows, :] = grad
        r.columns[1:2, :] += row_sum(to_single(grad))
        sum_step(0, ID_SUM_TWO, clip, kind, dot(grad, r.up_own[...], 1, 1))
        return carry

    def both(step, clip):
        lax.fori_loop(0, 2, functools.partial(step, clip), 0)

    both(feed, 0)
    for half in (FIRST, SECOND):
        finals.append(functools.partial(gather_on, r.cotangent, ID_COTANGENT, half))
        gather_near(r.cotangent, ID_COTANGENT, half).wait_recv()
        gather_on(r.cotangent, ID_COTANGENT, half).wait_recv()
    both(feed_back, 0)
    finals.append(functools.partial(mix_on, 2))
    mix_near(2).wait_recv()
    mix_on(2).wait_recv()
    sum_on(0, ID_SUM_TWO, 0)
    both(feed, 1)
    finals.append(functools.partial(gather_on, r.cotangent, ID_COTANGENT, 1))
    gather_near(r.cotangent, ID_COTANGENT, 1).wait_recv()
    gather_on(r.cotangent, ID_COTANGENT, 1).wait_recv()
    stages = []

    def weight(index, number, crosses, columns, y_first, grad):
        base = ID_WEIGHTS + 9 * number
        halves, line, middle, full = (
            refs[index] for refs in (r.halves, r.lines, r.middles, r.fulls)
        )
        crossed = r.crossed[index // 2] if crosses else None
        blocks = grad.shape[0]
        cols = slice(columns[0], columns[0] + columns[1])
        size = PAIR if y_first else PIECE
        first, first_peer, second, second_peer = (
            (y, y_peer, z_low, z_pair) if y_first else (z_low, z_pair, y, y_peer)
        )
        source = (crossed if crosses else line).at[:, 0:size, cols]
        held = slice(0, PAIR) if y_first else at(second, PIECE)

        def final_rows(side):
            return at(first, PAIR) if y_first else at(2 * first + side, PIECE)

        def first_copy():
            return remote(
                grad.at[:, at(1 - first, PAIR), cols],
                halves.at[:, :, cols],
                base,
                replica=first_peer,
            )

        def second_copy():
            given = slice(0, PAIR) if y_first else at(1 - second, PIECE)
            return remote(
                halves.at[:, given, cols],
                line.at[:, 0:size, cols],
                base + 1,
                replica=second_peer,
            )

        def far_copy():
            apart = 2 if y_first else 4
            return remote(
                halves.at[:, held, cols],
                middle.at[:, 0:size, cols],
                base + 2,
                replica=replica + apart * (1 - 2 * z_high),
            )

        def farther_copy(level):
            apart = 8 * 2**level * (1 - 2 * ((block_of_eight // 2**level) % 2))
            return pltpu.make_async_remote_copy(
                src_ref=line.at[:, 0:size, cols],
                dst_ref=r.extras[index].at[level, :, 0:size, cols],
                send_sem=r.send_all.at[number + 1, level],
                recv_sem=r.recv_all.at[number + 1, level],
                device_id={"replica": replica + apart},
                device_id_type=MESH,
            )

        def cross_copy(step):
            return remote(
                line.at[mate(step), 0:size, cols],
                crossed.at[shard, 0:size, cols],
                base + 2 + step,
                shard=mate(step),
            )

        def second_back():
            return remote(
                source, full.at[:, final_rows(second), cols], base + 6, replica=second_peer
            )

        def first_back(late):
            if not late:
                return remote(
                    source, full.at[:, final_rows(second), cols], base + 7, replica=first_peer
                )
            ref = full.at[:, final_rows(1 - second), cols]
            return remote(ref, ref, base + 8 - y_first, replica=first_peer)

        def start():
            push(first_copy)

        def second_start():
            first_copy().wait_recv()
            for block in range(blocks):
                halves[block, :, cols] = (
                    to_single(grad[block, at(first, PAIR), cols])
                    + to_single(halves[block, :, cols])
                ).astype(BRAIN)
            if y_first:
                push_if(edge, second_copy)
            else:
                push(second_copy)

        def far_start():
            second_copy().wait_recv()
            for block in range(blocks):
                halves[block, held, cols] = (
                    to_single(halves[block, held, cols]) + to_single(line[block, 0:size, cols])
                ).astype(BRAIN)
            far_copy().start()

        def cross_start():
            far_copy().wait()
            for block in range(blocks):
                line[block, 0:size, cols] = (
                    to_single(halves[block, held, cols]) + to_single(middle[block, 0:size, cols])
                ).astype(BRAIN)
            for level in range(levels):
                farther_copy(level).start()
                farther_copy(level).wait()
                line[:, 0:size, cols] = (
                    to_single(line[:, 0:size, cols])
                    + to_single(r.extras[index][level, :, 0:size, cols])
                ).astype(BRAIN)
            if crosses:
                crossed[shard, 0:size, cols] = line[shard, 0:size, cols]
                for step in (2, 3, 1):
                    cross_copy(step).start()

        def back_start():
            if crosses:
                for step in (1, 2, 3):
                    cross_copy(step).wait()
            second_back().start()
            first_back(False).start()
            for block in range(blocks):
                full[block, final_rows(second), cols] = source[block]
            conditional.append((inner if y_first else None, second_back))
            conditional.append(
                (inner if y_first else None, functools.partial(first_back, False))
            )

        def back_on():
            second_back().wait_recv()
            push(first_back, True)

        def back_end():
            if not y_first:
                first_back(False).wait_recv()
            first_back(True).wait_recv()

        def only(condition, step):
            def run_if():
                pl.when(condition)(step)

            return run_if if y_first else step

        def edge_on():
            @pl.when(edge)
            def _():
                second_back().wait_recv()

            push_if(edge, first_back, True)

        stages.append(
            (
                start,
                second_start,
                only(inner, far_start),
                only(inner, cross_start),
                only(inner, back_start),
                edge_on if y_first else back_on,
                back_end,
            )
        )

    grads = (r.up_cut, r.up_grad, r.out_grad, r.qkv_grad)
    for index, (_, _, crosses, parts) in enumerate(WEIGHTS):
        for start_column, width, y_first in parts:
            weight(index, len(stages), crosses, (start_column, width), y_first, grads[index])

    def run(*codes):
        for code in codes:
            stages[code // 10][code % 10]()

    rest = []
    for item in finals:
        if item.func in (share_across, share_near) and item.args[0] is r.up_cut:
            item().wait_send()
        else:
            rest.append(item)
    finals[:] = rest

    def cut_product(target, left, right, width):
        for part in range(2):
            product = dot(
                left[:, :, part * HALF : (part + 1) * HALF].reshape(2 * length, HALF),
                right[...].reshape(2 * length, width),
                0,
                0,
            )
            for half in range(2):
                target[2 * part + half, :, 0:width] = product[
                    half * SLICE : (half + 1) * SLICE
                ].astype(BRAIN)

    steps = iter(PLAN)

    def plan():
        run(*next(steps))

    cut_product(r.up_cut, r.active, r.cotangent, D)
    run(40, 0, 10, 20, 30)
    plan()
    both(feed_back, 1)
    sum_on(0, ID_SUM_TWO, 1)
    cut_product(r.up_grad, r.hidden_two, r.lifted_grad, D)
    run(90, 50, 60, 70, 80)
    plan()

    for clip in (0, 1):
        grad_two = sum_end(0, ID_SUM_TWO, clip)
        normal, scale = normalize(r.middle_own[clip])
        r.columns[2:3, :] += row_sum(grad_two * normal)
        r.columns[3:4, :] += row_sum(grad_two)
        total = to_single(r.cotangent[clip, own, :]) + norm_back(
            grad_two, normal, scale, whole(G2)
        )
        r.down_wide[4 * slot + clip * slot : 5 * slot + clip * slot, :] = total
        r.gradient[clip, own, :] = total.astype(BRAIN)
        gather_start(r.gradient, ID_GRADIENT, clip)
        plan()

    def lower(clip, kind, carry):
        value = dot(r.active[clip, rows_of(kind), :], r.down_own[...], 1, 0)
        sum_step(1, ID_SUM_RESULT, clip, kind, value)
        return carry

    for clip in (0, 1):
        both(lower, clip)
        plan()

    def back_out(clip):
        gather_near(r.gradient, ID_GRADIENT, clip).wait_recv()
        gather_on(r.gradient, ID_GRADIENT, clip).wait_recv()
        grad = r.gradient[clip]
        r.columns[4:5, :] += row_sum(to_single(grad))
        r.mixed_grad[clip] = dot(grad, r.out_all[at(shard, SLICE), :], 1, 1).astype(BRAIN)

    def attend_back(clip, head):
        query = head_of(r.pairs, clip, head * HD)
        key = head_of(r.pairs, clip, SLICE + head * HD)
        value = head_of(r.pairs, clip, 2 * SLICE + head * HD)
        grad = head_of(r.mixed_grad, clip, head * HD)
        softened = r.soft[clip * LOCAL_HEADS + head]
        grad_soft = dot(value, grad, 1, 1)
        inner = row_sum(grad_soft * softened)
        grad_scores = (softened * (grad_soft - inner)).astype(BRAIN)
        entries = (
            (dot(key.T, grad_scores, 1, 0).T * HD**-0.5).astype(BRAIN),
            dot(grad_scores, query, 1, 0).astype(BRAIN),
            dot(softened.astype(BRAIN), grad, 1, 0).astype(BRAIN),
        )
        for part, entry in enumerate(entries):
            left = part * SLICE + head * HD
            r.pairs_grad[clip, :, left : left + HD] = entry

    for clip in (0, 1):
        gather_forward(r.gradient, ID_GRADIENT, clip)
        plan()
        back_out(clip)
        plan()
        if clip == 1:
            for other in (0, 1):
                sum_on(1, ID_SUM_RESULT, other)
        for head in range(LOCAL_HEADS):
            attend_back(clip, head)
            plan()
    product = None
    for clip in (0, 1):
        heads = jnp.concatenate(
            [r.mixed[shard, 2 * clip], r.mixed[shard, 1, :, clip * HD : (clip + 1) * HD]], 1
        )
        term = dot(heads, r.gradient[clip], 0, 0)
        product = term if product is None else product + term
    r.out_grad[0] = product.astype(BRAIN)
    run(100)
    plan()
    cut_product(r.qkv_grad, r.hidden_one, r.pairs_grad, QKV)
    r.qkv_grad[:, :, QKV:] = jnp.zeros((GROUP, SLICE, HD), BRAIN)
    run(110, 120, 130, 140, 150)
    plan()

    def back_project(clip, kind, carry):
        grad = r.pairs_grad[clip, rows_of(kind), :]
        r.columns[5:6, 0:QKV] += row_sum(to_single(grad))
        sum_step(0, ID_SUM_ONE, clip, kind, dot(grad, r.qkv_own[...], 1, 1))
        return carry

    for clip in (0, 1):
        both(back_project, clip)
        plan()
    for clip in (0, 1):
        sum_on(0, ID_SUM_ONE, clip)
    plan()
    for clip in (0, 1):
        live = 1.0 if clip == 0 else second_live
        result = r.middle_own[clip] + sum_end(1, ID_SUM_RESULT, clip) + whole(C2)
        r.hidden_one[clip, 0:slot, :] = (result * live).astype(BRAIN)
    result_copy = local(r.hidden_one.at[:, 0:slot, :], r.result_out, 17)
    result_copy.start()
    plan()
    for clip in (0, 1):
        grad_one = sum_end(0, ID_SUM_ONE, clip)
        normal, scale = normalize(to_single(r.tokens[clip, own, :]))
        r.columns[6:7, :] += row_sum(grad_one * normal)
        r.columns[7:8, :] += row_sum(grad_one)
        r.down_wide[4 * slot + clip * slot : 5 * slot + clip * slot, :] += norm_back(grad_one, normal, scale, whole(G1))
    grad_copies = [
        local(
            r.down_wide.at[4 * slot + clip * slot : 5 * slot + clip * slot],
            r.input_grad_out.at[clip],
            18 + 6 * clip,
        )
        for clip in (0, 1)
    ]
    for item in grad_copies:
        item.start()

    for member in range(GROUP):
        cols = slice(member * SLICE, (member + 1) * SLICE)
        for place, row in enumerate((6, 7, 2, 3, 4, 0)):
            r.small_sent[member, place : place + 1, :] = r.columns[row : row + 1, cols]

    def small_copy(step):
        return remote(
            r.small_sent.at[mate(step)],
            r.small_near.at[step - 1],
            ID_SMALL + step - 1,
            shard=mate(step),
        )

    for step in (1, 2, 3):
        push(small_copy, step)
    plan()
    for step in (1, 2, 3):
        small_copy(step).wait_recv()
    summed = r.small_sent[shard, 0:4, :]
    for step in (1, 2, 3):
        summed += r.small_near[step - 1, 0:4, :]
    r.small_all[replica, G1 : G1 + 2, :] = summed[0:2]
    r.small_all[replica, G2 : G2 + 2, :] = summed[2:4]
    r.small_all[replica, BO : BO + 1, :] = r.small_sent[shard, 4:5, :]
    r.small_all[replica, C2 : C2 + 1, :] = r.small_sent[shard, 5:6, :]
    r.small_all[replica, BQ : BQ + 1, :] = r.columns[5:6, 0:SLICE]
    r.small_all[replica, BV : BV + 1, :] = r.columns[5:6, 2 * SLICE : QKV]
    for part in range(GROUP):
        r.small_all[replica, C1 + part : C1 + part + 1, :] = r.columns[
            1:2, part * SLICE : (part + 1) * SLICE
        ]
    r.small_all[replica, C1 + GROUP :, :] = jnp.zeros((VECTOR_ROWS - C1 - GROUP, SLICE), SINGLE)

    def spread_copy(step):
        return pltpu.make_async_remote_copy(
            src_ref=r.small_all.at[replica],
            dst_ref=r.small_all.at[replica],
            send_sem=r.send_all.at[0, step],
            recv_sem=r.recv_all.at[0, step],
            device_id={"replica": (replica + step) % replicas},
            device_id_type=MESH,
        )

    def spread_start(step, carry):
        spread_copy(step).start()
        return carry

    lax.fori_loop(1, replicas, spread_start, 0)
    plan()

    def spread_wait(step, carry):
        spread_copy(step).wait()
        return carry

    lax.fori_loop(1, replicas, spread_wait, 0)
    small_sum = r.small_all[0]
    for step in range(1, replicas):
        small_sum += r.small_all[step]
    r.small_all[0] = small_sum
    copies = grad_copies + [result_copy, local(r.small_all.at[0], r.small_out, 19)]
    copies[-1].start()
    for item in finals:
        item().wait_send()
    for condition, item in conditional:
        if condition is None:
            item().wait_send()
        else:

            @pl.when(condition)
            def _():
                item().wait_send()

    run(106)
    copies.append(local(r.fulls[OUT], r.sums_out[OUT], 20))
    copies[-1].start()
    run(6, 16, 26, 36, 46)
    copies.append(local(r.fulls[DOWN], r.sums_out[DOWN], 21))
    copies[-1].start()
    run(116, 126, 136, 146, 156)
    copies.append(local(r.fulls[QKVS], r.sums_out[QKVS], 22))
    copies[-1].start()
    run(56, 66, 76, 86, 96)
    copies.append(local(r.fulls[UP], r.sums_out[UP], 23))
    copies[-1].start()
    for item in copies:
        item.wait()


def finish(fields, *refs):
    r = gathered(fields, refs)
    units = []

    def unit(source, held, wide, target, widen):
        index = len(units)
        units.append(
            (
                pltpu.make_async_copy(source, held, r.near.at[index]),
                pltpu.make_async_copy(wide, target, r.near.at[index]),
                widen,
            )
        )

    def keep():
        pass

    def down(index):
        rows = slice(index * SLICE, (index + 1) * SLICE)

        def widen():
            r.wide[DOWN][rows, :] = to_single(r.narrow[DOWN][index])

        unit(
            r.sums_in[DOWN].at[index],
            r.narrow[DOWN].at[index],
            r.wide[DOWN].at[rows],
            r.results[DOWN].at[rows],
            widen,
        )

    def up(index):
        cols = slice(index * D, (index + 1) * D)

        def widen():
            r.wide[UP][:, cols] = to_single(r.narrow[UP][index])

        unit(
            r.sums_in[UP].at[index],
            r.narrow[UP].at[index],
            r.wide[UP].at[:, cols],
            r.results[UP].at[:, cols],
            widen,
        )

    def qkv(index):
        rows = slice(index * PIECE, (index + 1) * PIECE)

        def widen():
            for part in range(3):
                cols = slice(part * SLICE, (part + 1) * SLICE)
                r.wide[QKVS][rows, part * D : (part + 1) * D] = to_single(
                    jnp.concatenate(
                        [r.narrow[QKVS][member, rows, cols] for member in range(GROUP)], 1
                    )
                )

        unit(
            r.sums_in[QKVS].at[:, rows],
            r.narrow[QKVS].at[:, rows],
            r.wide[QKVS].at[rows],
            r.results[QKVS].at[rows],
            widen,
        )

    def out():
        def widen():
            r.wide[OUT][...] = to_single(r.narrow[OUT][0])

        unit(r.sums_in[OUT], r.narrow[OUT], r.wide[OUT], r.results[OUT], widen)

    unit(r.input_grad_in, r.input_grad_held, r.input_grad_held, r.input_grad, keep)
    unit(r.result_in, r.result_held, r.result_held, r.result, keep)
    for index in range(GROUP):
        down(index)
        up(index)
    out()
    for index in range(GROUP):
        qkv(index)
    for load, _, _ in units:
        load.start()
    for row in range(8):
        r.vectors[row][...] = r.small_in[row : row + 1, :].reshape(SLICE)
    r.vectors[8][...] = jnp.concatenate(
        [r.small_in[C1 + part : C1 + part + 1, :] for part in range(GROUP)], 1
    ).reshape(D)
    for load, store, widen in units:
        load.wait()
        widen()
        store.start()
    for _, store, _ in units:
        store.wait()


def layer(replicas, *arguments):
    (
        tokens, cotangent, clip_count, ln1_gain, ln1_bias, qkv_weight, q_bias, v_bias,
        out_weight, out_bias, ln2_gain, ln2_bias, fc1_weight, fc1_bias, fc2_weight, fc2_bias,
    ) = arguments
    slots, slot, _ = tokens.shape
    length = slot * GROUP
    levels = (replicas // 8).bit_length() - 1
    vectors = (
        ln1_gain, ln1_bias, out_bias, ln2_gain, ln2_bias, fc2_bias, q_bias, v_bias, fc1_bias,
    )
    anywhere = pl.BlockSpec(memory_space=pl.ANY)
    in_memory = pl.BlockSpec(memory_space=pltpu.VMEM)
    in_hbm = pl.BlockSpec(memory_space=pltpu.HBM)
    shape = jax.ShapeDtypeStruct

    inputs = dict(
        tokens_in=anywhere,
        cotangent_in=anywhere,
        count_in=pl.BlockSpec(memory_space=pltpu.SMEM),
        vectors_in=[anywhere] * 9,
        qkv_in=anywhere,
        out_in=anywhere,
        up_in=anywhere,
        down_in=anywhere,
    )
    outputs = dict(
        result_out=shape(tokens.shape, BRAIN),
        input_grad_out=shape(tokens.shape, SINGLE),
        small_out=shape((VECTOR_ROWS, SLICE), SINGLE),
        sums_out=[shape((blocks, SLICE, columns), BRAIN) for blocks, columns, _, _ in WEIGHTS],
    )
    scratch = dict(
        qkv_wide=pltpu.VMEM(qkv_weight.shape, SINGLE),
        out_wide=pltpu.VMEM(out_weight.shape, SINGLE),
        up_wide=pltpu.VMEM(fc1_weight.shape, SINGLE),
        down_wide=pltpu.VMEM(fc2_weight.shape, SINGLE),
        qkv_cut=pltpu.VMEM((GROUP, SLICE, QKV), BRAIN),
        up_cut=pltpu.VMEM((GROUP, SLICE, D), BRAIN),
        qkv_own=pltpu.VMEM((D, QKV), BRAIN),
        up_own=pltpu.VMEM((D, D), BRAIN),
        out_all=pltpu.VMEM((D, D), BRAIN),
        down_own=pltpu.VMEM((D, D), BRAIN),
        vectors=pltpu.VMEM((GROUP, VECTOR_ROWS, SLICE), SINGLE),
        vectors_raw=[pltpu.VMEM(vector.shape, SINGLE) for vector in vectors],
        tokens=pltpu.VMEM((2, length, D), BRAIN),
        cotangent=pltpu.VMEM((2, length, D), BRAIN),
        hidden_one=pltpu.VMEM((2, length, D), BRAIN),
        pairs=pltpu.VMEM((2, length, QKV), BRAIN),
        soft=pltpu.VMEM((2 * LOCAL_HEADS, length, length), SINGLE),
        mixed=pltpu.VMEM((GROUP, 3, length, TILE), BRAIN),
        middle_own=pltpu.VMEM((2, slot, D), SINGLE),
        hidden_two=pltpu.VMEM((2, length, D), BRAIN),
        active=pltpu.VMEM((2, length, D), BRAIN),
        lifted_grad=pltpu.VMEM((2, length, D), BRAIN),
        gradient=pltpu.VMEM((2, length, D), BRAIN),
        mixed_grad=pltpu.VMEM((2, length, SLICE), BRAIN),
        pairs_grad=pltpu.VMEM((2, length, QKV), BRAIN),
        stage=pltpu.VMEM((2 * slot, D), SINGLE),
        sum_sent=pltpu.VMEM((2, 2, 3, slot, D), BRAIN),
        sum_near=pltpu.VMEM((2, 2, 2, slot, D), BRAIN),
        sum_far=pltpu.VMEM((2, 2, slot, D), BRAIN),
        sum_own=pltpu.VMEM((2, 2, slot, D), SINGLE),
        up_grad=pltpu.VMEM((GROUP, SLICE, D), BRAIN),
        out_grad=pltpu.VMEM((1, SLICE, D), BRAIN),
        qkv_grad=pltpu.VMEM((GROUP, SLICE, QKV + HD), BRAIN),
        columns=pltpu.VMEM((8, D), SINGLE),
        small_sent=pltpu.VMEM((GROUP, 8, SLICE), SINGLE),
        small_near=pltpu.VMEM((GROUP - 1, 8, SLICE), SINGLE),
        small_all=pltpu.VMEM((replicas, VECTOR_ROWS, SLICE), SINGLE),
        halves=[pltpu.VMEM((w[0], PAIR, w[1]), BRAIN) for w in WEIGHTS],
        lines=[pltpu.VMEM((w[0], PAIR, w[1]), BRAIN) for w in WEIGHTS],
        middles=[pltpu.VMEM((w[0], PAIR, w[1]), BRAIN) for w in WEIGHTS],
        fulls=[pltpu.VMEM((w[0], SLICE, w[1]), BRAIN) for w in WEIGHTS],
        crossed=[pltpu.VMEM((GROUP, PAIR, w[1]), BRAIN) for w in WEIGHTS if w[2]],
        extras=[
            pltpu.VMEM((levels, w[0], PAIR, w[1]) if levels else (1, 1, 16, TILE), BRAIN)
            for w in WEIGHTS
        ],
        send=pltpu.SemaphoreType.DMA((COPIES,)),
        recv=pltpu.SemaphoreType.DMA((COPIES,)),
        send_all=pltpu.SemaphoreType.DMA((1 + ITEMS, replicas)),
        recv_all=pltpu.SemaphoreType.DMA((1 + ITEMS, replicas)),
        near=pltpu.SemaphoreType.DMA((LOCALS,)),
    )
    sums = pl.pallas_call(
        functools.partial(kernel, replicas, counted(inputs) + counted(outputs) + counted(scratch)),
        out_shape=tuple(flat(outputs)),
        in_specs=flat(inputs),
        out_specs=(anywhere,) * len(flat(outputs)),
        scratch_shapes=flat(scratch),
        compiler_params=pltpu.CompilerParams(
            collective_id=0, has_side_effects=True, vmem_limit_bytes=65000 * 1024
        ),
        name="layer",
    )(
        tokens, cotangent, clip_count, *vectors, qkv_weight, out_weight, fc1_weight, fc2_weight
    )

    matrices = [fc2_weight, fc1_weight, out_weight, qkv_weight]
    last_inputs = dict(
        result_in=in_hbm, input_grad_in=in_hbm, small_in=in_memory, sums_in=[in_hbm] * 4
    )
    last_outputs = dict(
        result=shape(tokens.shape, BRAIN),
        input_grad=shape(tokens.shape, SINGLE),
        results=[shape(array.shape, SINGLE) for array in matrices],
        vectors=[shape(vector.shape, SINGLE) for vector in vectors],
    )
    last_scratch = dict(
        narrow=[pltpu.VMEM((blocks, SLICE, columns), BRAIN) for blocks, columns, _, _ in WEIGHTS],
        wide=[pltpu.VMEM(array.shape, SINGLE) for array in matrices],
        input_grad_held=pltpu.VMEM(tokens.shape, SINGLE),
        result_held=pltpu.VMEM(tokens.shape, BRAIN),
        near=pltpu.SemaphoreType.DMA((16,)),
    )
    values = pl.pallas_call(
        functools.partial(
            finish, counted(last_inputs) + counted(last_outputs) + counted(last_scratch)
        ),
        out_shape=tuple(flat(last_outputs)),
        in_specs=flat(last_inputs),
        out_specs=(anywhere,) * 6 + (in_memory,) * 9,
        scratch_shapes=flat(last_scratch),
        compiler_params=pltpu.CompilerParams(vmem_limit_bytes=60 << 20),
        name="finish",
    )(*sums)
    o = gathered(counted(last_outputs), values)
    return (
        o.result,
        o.input_grad,
        o.vectors[G1],
        o.vectors[B1],
        o.results[QKVS],
        o.vectors[BQ],
        o.vectors[BV],
        o.results[OUT],
        o.vectors[BO],
        o.vectors[G2],
        o.vectors[B2],
        o.results[UP],
        o.vectors[C1],
        o.results[DOWN],
        o.vectors[C2],
    )


def solution(mesh):
    token, vector, matrix = P("replica", "shard", None), P("shard"), P("shard", None)
    return jax.shard_map(
        functools.partial(layer, mesh.shape["replica"]),
        mesh=mesh,
        in_specs=(
            token, token, P("replica"), vector, vector, matrix, vector, vector,
            matrix, vector, vector, vector, matrix, vector, matrix, vector,
        ),
        out_specs=(
            token, token, vector, vector, matrix, vector, vector, matrix,
            vector, vector, vector, matrix, vector, matrix, vector,
        ),
        check_vma=False,
    )
```

```python
import functools
import types

import jax
import jax.numpy as jnp
from jax import lax
from jax.experimental import pallas as pl
from jax.experimental.pallas import tpu as pltpu
from jax.sharding import PartitionSpec as P

D = 768
HD = 64
EPSILON = 1e-06
GROUP = 4
SLICE = D // GROUP
LOCAL_HEADS = SLICE // HD
HALF = D // 2
TILE = 128
PAIR = SLICE // 2
PIECE = SLICE // 4
QKV = 3 * SLICE
BRAIN = jnp.bfloat16
SINGLE = jnp.float32
MESH = pl.DeviceIdType.MESH

G1, B1, BO, G2, B2, C2, BQ, BV, C1 = range(9)
VECTOR_ROWS = 16

WEIGHTS = (
    (GROUP, D, False, ((0, 128, True), (128, 128, True), (256, 128, True), (384, 128, True), (512, 256, False))),
    (GROUP, D, True, ((0, 128, True), (128, 128, True), (256, 128, True), (384, 128, True), (512, 256, False))),
    (1, D, False, ((0, 768, False),)),
    (GROUP, 640, True, ((0, 128, True), (128, 128, True), (256, 128, True), (384, 128, True), (512, 128, True))),
)
DOWN, UP, OUT, QKVS = range(4)
ITEMS = sum(len(parts) for _, _, _, parts in WEIGHTS)

MIXES = (((0, 0), (0, 1)), ((0, 2), (1, 2)), ((1, 0), (1, 1)))


PLAN = (
    (),
    (),
    (1, 41, 11, 21),
    (),
    (91, 31),
    (2, 51),
    (12, 61),
    (),
    (22, 3, 4),
    (32, 13, 14),
    (),
    (52, 23, 24, 71),
    (81, 33, 62),
    (42, 72, 53),
    (5, 34, 82),
    (),
    (15, 92, 63),
    (25,),
    (),
    (73, 35, 43, 44, 111, 83, 101),
    (),
    (74, 121, 84, 131, 93, 141, 75, 64, 54, 112, 151, 85, 122, 45, 65, 113, 132, 102),
    (55, 123, 142, 114, 133, 152),
    (124, 94, 115, 134, 125, 143, 103, 104, 153, 144, 135, 154, 95, 145, 105, 155),
)


class Names:
    def __init__(self):
        self.total = 0

    def take(self, count):
        first = self.total
        self.total += count
        return first


ids = Names()
ID_TOKENS = ids.take(6)
ID_COTANGENT = ids.take(12)
ID_GRADIENT = ids.take(6)
ID_VECTORS = ids.take(3)
ID_QKV = ids.take(9)
ID_OUT = ids.take(9)
ID_UP = ids.take(9)
ID_MIX = ids.take(9)
ID_SUM_TWO = ids.take(6)
ID_SUM_RESULT = ids.take(6)
ID_SUM_ONE = ids.take(6)
ID_SMALL = ids.take(3)
ID_WEIGHTS = ids.take(9 * ITEMS)
COPIES = ids.total
LOCALS = 32


def to_single(value):
    return value.astype(SINGLE)


def rounded(value):
    return value.astype(BRAIN).astype(SINGLE)


def dot(left, right, left_dim, right_dim):
    return lax.dot_general(
        left, right, (((left_dim,), (right_dim,)), ((), ())), preferred_element_type=SINGLE
    )


def normalize(value):
    mean = jnp.sum(value, axis=-1, keepdims=True) * (1.0 / D)
    centred = value - mean
    spread = jnp.sum(centred * centred, axis=-1, keepdims=True) * (1.0 / D)
    scale = lax.rsqrt(spread + EPSILON)
    return centred * scale, scale


def norm_back(grad, normal, scale, gain):
    scaled = grad * gain
    first = jnp.sum(scaled, axis=-1, keepdims=True) * (1.0 / D)
    second = jnp.sum(scaled * normal, axis=-1, keepdims=True) * (1.0 / D)
    return scale * (scaled - first - normal * second)


def row_sum(value):
    return jnp.sum(value, axis=0, keepdims=True)


def gathered(fields, refs):
    result, refs = {}, list(refs)
    for name, count in fields:
        result[name] = [refs.pop(0) for _ in range(count)] if count > 1 else refs.pop(0)
    return types.SimpleNamespace(**result)


def counted(fields):
    return [(name, len(entry) if isinstance(entry, list) else 1) for name, entry in fields.items()]


def flat(fields):
    result = []
    for entry in fields.values():
        result += entry if isinstance(entry, list) else [entry]
    return result


def kernel(replicas, fields, *refs):
    r = gathered(fields, refs)
    levels = (replicas // 8).bit_length() - 1
    slot = r.tokens_in.shape[1]
    pair = 2 * slot
    length = GROUP * slot

    shard = lax.axis_index("shard")
    replica = lax.axis_index("replica")
    chip = shard // 2
    core = shard % 2
    y = replica % 2
    z_low = (replica // 2) % 2
    z_high = (replica // 4) % 2
    inner = (z_low + z_high) % 2 == 1
    edge = (z_low + z_high) % 2 == 0
    block_of_eight = replica // 8
    y_peer = replica + 1 - 2 * y
    z_pair = replica + 2 * (1 - 2 * z_low)

    def mate(step):
        return 2 * ((chip + step // 2) % 2) + (shard + step) % 2

    finals, conditional = [], []

    def remote(source, target, index, **where):
        return pltpu.make_async_remote_copy(
            src_ref=source,
            dst_ref=target,
            send_sem=r.send.at[index],
            recv_sem=r.recv.at[index],
            device_id=where,
            device_id_type=MESH,
        )

    def push(make, *arguments):
        make(*arguments).start()
        finals.append(functools.partial(make, *arguments))

    def push_if(condition, make, *arguments):
        @pl.when(condition)
        def _():
            make(*arguments).start()

        conditional.append((condition, functools.partial(make, *arguments)))

    def local(source, target, index):
        return pltpu.make_async_copy(source, target, r.near.at[index])

    def at(index, size, offset=0):
        return pl.ds(pl.multiple_of(index * size + offset, size), size)

    def here(ref, clip):
        return ref.at[clip, at(shard, slot), :]

    def quarter_rows(step):
        return at((2 * y + z_low + step) % 4, PIECE)

    qkv_loads = [
        local(r.qkv_in.at[quarter_rows(step)], r.qkv_wide.at[quarter_rows(step)], 25 + step)
        for step in range(4)
    ]
    token_loads = [local(r.tokens_in.at[clip], here(r.tokens, clip), 1 + clip) for clip in (0, 1)]
    vector_loads = [
        local(r.vectors_in[row], r.vectors_raw[row], 3 + row)
        for row in range(9)
    ]
    cotangent_loads = [
        local(r.cotangent_in.at[clip], here(r.cotangent, clip), 12 + clip) for clip in (0, 1)
    ]
    wide_loads = [
        local(r.up_in, r.up_wide, 14),
        local(r.out_in, r.out_wide, 15),
        local(r.down_in, r.down_wide, 16),
    ]
    for load in qkv_loads + token_loads + vector_loads + cotangent_loads + wide_loads:
        load.start()
    barrier = pltpu.get_barrier_semaphore()
    for step in (1, 2, 3):
        pl.semaphore_signal(barrier, inc=1, device_id={"shard": mate(step)}, device_id_type=MESH)

    def greet(step, carry):
        peer = (replica + step) % replicas
        pl.semaphore_signal(barrier, inc=1, device_id={"replica": peer}, device_id_type=MESH)
        return carry

    lax.fori_loop(1, replicas, greet, 0)

    def cut_rows(step):
        qkv_loads[step].wait()
        rows = quarter_rows(step)
        for member in range(GROUP):
            left = member * SLICE
            r.qkv_cut[member, rows, :] = jnp.concatenate(
                [
                    r.qkv_wide[rows, part * D + left : part * D + left + SLICE].astype(BRAIN)
                    for part in range(3)
                ],
                axis=1,
            )

    cut_rows(0)
    for load in token_loads + vector_loads:
        load.wait()
    pl.semaphore_wait(barrier, replicas + 2)

    def gather_part(buffer, clip, member):
        if clip >= 2:
            return buffer.at[0, at(2 * member + clip - 2, slot // 2), :]
        return buffer.at[clip, at(member, slot), :]

    def gather_near(buffer, base, clip):
        part = gather_part(buffer, clip, shard)
        return remote(part, part, base + 3 * clip, shard=mate(1))

    def gather_across(buffer, base, clip):
        part = gather_part(buffer, clip, shard)
        return remote(part, part, base + 3 * clip + 1, shard=mate(2))

    def gather_on(buffer, base, clip):
        part = gather_part(buffer, clip, mate(2))
        return remote(part, part, base + 3 * clip + 2, shard=mate(1))

    def gather_start(buffer, base, clip):
        push(gather_across, buffer, base, clip)
        push(gather_near, buffer, base, clip)

    def gather_forward(buffer, base, clip):
        gather_across(buffer, base, clip).wait_recv()
        push(gather_on, buffer, base, clip)

    def quarter(member, y_side, z_side):
        return at((member * 2 + y_side) * 2 + z_side, PIECE)

    def share_across(cut, buffer, base, step):
        source = buffer.at[quarter(shard, y, z_low), :]
        if cut is not None:
            source = cut.at[mate(step), at(2 * y + z_low, PIECE), :]
        return remote(
            source, buffer.at[quarter(shard, y, z_low), :], base + step - 2, shard=mate(step)
        )

    def share_z(buffer, base, step):
        part = buffer.at[quarter(mate(step), y, z_low), :]
        return remote(part, part, base + step, replica=z_pair)

    def share_y(buffer, base, step, second):
        side = 1 - z_low if second else z_low
        part = buffer.at[quarter(mate(step), y, side), :]
        return remote(part, part, base + 2 * second + 2 + step, replica=y_peer)

    def share_near(cut, buffer, base):
        target = buffer.at[at(shard, SLICE), :]
        source = target if cut is None else cut.at[mate(1)]
        return remote(source, target, base + 8, shard=mate(1))

    def share_first(cut, buffer, base, steps):
        for step in steps:
            push(share_across, cut, buffer, base, step)

    def share_start(cut, buffer, base, steps):
        share_first(cut, buffer, base, steps)
        push(share_near, cut, buffer, base)

    def share_on(cut, buffer, base, steps):
        for step in steps:
            share_across(cut, buffer, base, step).wait_recv()
            push(share_z, buffer, base, step)
            push(share_y, buffer, base, step, 0)

    def share_last(buffer, base, steps):
        for step in steps:
            share_z(buffer, base, step).wait_recv()
            push(share_y, buffer, base, step, 1)

    def share_wait(cut, buffer, base, steps):
        for step in steps:
            share_y(buffer, base, step, 0).wait_recv()
            share_y(buffer, base, step, 1).wait_recv()
        share_near(cut, buffer, base).wait_recv()

    BOTH, ONE = (2, 3), (2,)
    FIRST, SECOND = 2, 3

    share_first(r.qkv_cut, r.qkv_own, ID_QKV, BOTH)
    gather_start(r.tokens, ID_TOKENS, 0)
    for row in range(8):
        r.vectors[shard, row : row + 1, :] = rounded(
            r.vectors_raw[row][...].reshape(1, SLICE)
        )
    long_row = rounded(r.vectors_raw[8][...].reshape(1, D))
    for part in range(GROUP):
        r.vectors[shard, C1 + part : C1 + part + 1, :] = long_row[
            :, part * SLICE : (part + 1) * SLICE
        ]
    r.vectors[shard, C1 + GROUP :, :] = jnp.zeros((VECTOR_ROWS - C1 - GROUP, SLICE), SINGLE)

    def send_vectors(step):
        return remote(
            r.vectors.at[shard], r.vectors.at[shard], ID_VECTORS + step - 1, shard=mate(step)
        )

    for step in (1, 2, 3):
        push(send_vectors, step)
    for load in wide_loads:
        load.wait()
    for member in range(GROUP):
        r.up_cut[member] = r.up_wide[:, member * D : (member + 1) * D].astype(BRAIN)
    r.out_all[at(shard, SLICE), :] = r.out_wide[...].astype(BRAIN)
    share_start(None, r.out_all, ID_OUT, ONE)
    share_start(r.up_cut, r.up_own, ID_UP, BOTH)
    gather_start(r.tokens, ID_TOKENS, 1)

    for step in (1, 2, 3):
        cut_rows(step)
    push(share_near, r.qkv_cut, r.qkv_own, ID_QKV)
    r.qkv_own[at(shard, SLICE), :] = r.qkv_cut[shard]
    share_on(r.qkv_cut, r.qkv_own, ID_QKV, BOTH)
    for load in cotangent_loads:
        load.wait()
    second_live = to_single(jnp.minimum(r.count_in[0] - 1, 1))
    own = at(shard, slot)
    r.cotangent[1, own, :] = (to_single(r.cotangent[1, own, :]) * second_live).astype(BRAIN)
    r.up_own[at(shard, SLICE), :] = r.up_cut[shard]
    r.down_own[...] = r.down_wide[...].astype(BRAIN)
    r.columns[...] = jnp.zeros_like(r.columns)
    share_last(r.qkv_own, ID_QKV, BOTH)
    gather_forward(r.tokens, ID_TOKENS, 0)

    def whole(row):
        return jnp.concatenate([r.vectors[member, row : row + 1, :] for member in range(GROUP)], 1)

    def mine(row):
        return r.vectors[shard, row : row + 1, :]

    for step in (1, 2, 3):
        send_vectors(step).wait_recv()
    share_wait(r.qkv_cut, r.qkv_own, ID_QKV, BOTH)
    scale_row = jnp.where(lax.broadcasted_iota(jnp.int32, (1, QKV), 1) < SLICE, HD**-0.5, 1.0)
    qkv_bias = jnp.concatenate([mine(BQ), jnp.zeros((1, SLICE), SINGLE), mine(BV)], 1)

    def project(clip, side):
        rows = at((chip + side) % 2, pair)
        normal, _ = normalize(to_single(r.tokens[clip, rows, :]))
        hidden = (normal * whole(G1) + whole(B1)).astype(BRAIN)
        r.hidden_one[clip, rows, :] = hidden
        product = (dot(hidden, r.qkv_own[...], 1, 0) + qkv_bias) * scale_row
        r.pairs[clip, rows, :] = product.astype(BRAIN)

    def mix_near(part):
        ref = r.mixed.at[shard, part]
        return remote(ref, ref, ID_MIX + 3 * part, shard=mate(1))

    def mix_across(part):
        ref = r.mixed.at[shard, part]
        return remote(ref, ref, ID_MIX + 3 * part + 1, shard=mate(2))

    def mix_on(part):
        ref = r.mixed.at[mate(2), part]
        return remote(ref, ref, ID_MIX + 3 * part + 2, shard=mate(1))

    def mix_forward(part):
        mix_across(part).wait_recv()
        push(mix_on, part)

    def head_of(ref, clip, left):
        return ref[clip, :, left : left + HD]

    def attend(part, place):
        clip, head = MIXES[part][place]
        query = head_of(r.pairs, clip, head * HD)
        key = head_of(r.pairs, clip, SLICE + head * HD)
        value = head_of(r.pairs, clip, 2 * SLICE + head * HD)
        scores = dot(key, query, 1, 1)
        highest = jnp.max(scores, axis=0, keepdims=True)
        expanded = jnp.exp(scores - highest)
        softened = expanded * (1.0 / row_sum(expanded))
        r.soft[clip * LOCAL_HEADS + head] = softened
        mixture = dot(value.T, softened.astype(BRAIN), 1, 0).T.astype(BRAIN)
        r.mixed[shard, part, :, place * HD : (place + 1) * HD] = mixture

    def mix_start(part):
        push(mix_across, part)
        push(mix_near, part)

    gather_near(r.tokens, ID_TOKENS, 0).wait_recv()
    project(0, 0)
    gather_on(r.tokens, ID_TOKENS, 0).wait_recv()
    project(0, 1)
    attend(0, 0)
    share_on(None, r.out_all, ID_OUT, ONE)
    share_on(r.up_cut, r.up_own, ID_UP, BOTH)
    attend(0, 1)
    mix_start(0)
    gather_start(r.cotangent, ID_COTANGENT, FIRST)
    attend(1, 0)
    gather_near(r.tokens, ID_TOKENS, 1).wait_recv()
    project(1, 0)
    gather_forward(r.tokens, ID_TOKENS, 1)
    gather_on(r.tokens, ID_TOKENS, 1).wait_recv()
    project(1, 1)
    attend(1, 1)
    mix_start(1)
    gather_start(r.cotangent, ID_COTANGENT, SECOND)
    share_last(r.out_all, ID_OUT, ONE)
    share_last(r.up_own, ID_UP, BOTH)
    mix_forward(0)
    attend(2, 0)
    attend(2, 1)
    mix_start(2)
    gather_start(r.cotangent, ID_COTANGENT, 1)

    def out_on():
        part = r.out_all.at[at(mate(2), SLICE), :]
        return remote(part, part, ID_OUT + 1, shard=mate(1))

    share_wait(None, r.out_all, ID_OUT, ONE)
    push(out_on)
    mix_forward(1)
    out_on().wait_recv()
    for part in (0, 1):
        mix_near(part).wait_recv()
        mix_on(part).wait_recv()
    share_wait(r.up_cut, r.up_own, ID_UP, BOTH)

    def sum_near(which, base, clip, kind):
        return remote(
            r.sum_sent.at[which, clip, kind],
            r.sum_near.at[which, clip, kind],
            base + 3 * clip + kind,
            shard=mate(1),
        )

    def sum_far(which, base, clip):
        return remote(
            r.sum_sent.at[which, clip, 2],
            r.sum_far.at[which, clip],
            base + 3 * clip + 2,
            shard=mate(2),
        )

    def sum_kept(which, clip, kind):
        if which == 0:
            return r.sum_own.at[clip, kind]
        return r.up_wide.at[0:slot, at(2 * clip + kind, D)]

    def sum_step(which, base, clip, kind, value):
        r.stage[...] = value
        r.sum_sent[which, clip, kind] = r.stage[at(1 - core, slot), :].astype(BRAIN)
        sum_kept(which, clip, kind)[...] = r.stage[at(core, slot), :]
        remote(
            r.sum_sent.at[which, clip, kind],
            r.sum_near.at[which, clip, kind],
            base + 3 * clip + kind,
            shard=mate(1),
        ).start()

    def sum_on(which, base, clip):
        sum_near(which, base, clip, 0).wait_recv()
        r.sum_sent[which, clip, 2] = (
            sum_kept(which, clip, 0)[...] + to_single(r.sum_near[which, clip, 0])
        ).astype(BRAIN)
        sum_far(which, base, clip).start()

    def sum_end(which, base, clip):
        sum_near(which, base, clip, 0).wait_send()
        sum_near(which, base, clip, 1).wait()
        sum_far(which, base, clip).wait()
        return (
            sum_kept(which, clip, 1)[...]
            + to_single(r.sum_near[which, clip, 1])
            + to_single(r.sum_far[which, clip])
        )

    def rows_of(kind):
        return at((chip + 1 + kind) % 2, pair)

    long_bias = jnp.concatenate(
        [r.vectors[shard, C1 + part : C1 + part + 1, :] for part in range(GROUP)], 1
    )

    def pass_on(across, on):
        across.wait_recv()
        on.start()

    def feed(clip, kind, carry):
        rows = rows_of(kind)

        @pl.when(kind == 1)
        def _():
            for part in ((FIRST, SECOND), (1,))[clip]:
                pass_on(
                    gather_across(r.cotangent, ID_COTANGENT, part),
                    gather_on(r.cotangent, ID_COTANGENT, part),
                )

        total = to_single(r.tokens[clip, rows, :]) + whole(BO)
        for member in range(GROUP):
            heads = jnp.concatenate(
                [
                    r.mixed[member, 2 * clip, rows, :],
                    r.mixed[member, 1, rows, clip * HD : (clip + 1) * HD],
                ],
                1,
            )
            total += dot(heads, r.out_all[member * SLICE : (member + 1) * SLICE, :], 1, 0)

        @pl.when(kind == 1)
        def _():
            r.stage[...] = total
            r.middle_own[clip] = r.stage[at(core, slot), :]

        normal, _ = normalize(total)
        hidden = (normal * whole(G2) + whole(B2)).astype(BRAIN)
        r.hidden_two[clip, rows, :] = hidden
        lifted = dot(hidden, r.up_own[...], 1, 0) + long_bias
        share = 0.5 + 0.5 * lax.erf(lifted * (0.5**0.5))
        r.active[clip, rows, :] = (lifted * share).astype(BRAIN)
        r.down_wide[at(kind, pair), :] = share + lifted * jnp.exp(lifted * lifted * -0.5) * 0.3989422804014327
        return carry

    def feed_back(clip, kind, carry):
        rows = rows_of(kind)
        if clip == 0:

            @pl.when(kind == 1)
            def _():
                pass_on(mix_across(2), mix_on(2))

        down = r.cotangent[clip, rows, :]
        r.columns[0:1, :] += row_sum(to_single(down))
        grad = (dot(down, r.down_own[...], 1, 1) * r.down_wide[at(kind, pair), :]).astype(BRAIN)
        r.lifted_grad[clip, rows, :] = grad
        r.columns[1:2, :] += row_sum(to_single(grad))
        sum_step(0, ID_SUM_TWO, clip, kind, dot(grad, r.up_own[...], 1, 1))
        return carry

    def both(step, clip):
        lax.fori_loop(0, 2, functools.partial(step, clip), 0)

    both(feed, 0)
    for half in (FIRST, SECOND):
        finals.append(functools.partial(gather_on, r.cotangent, ID_COTANGENT, half))
        gather_near(r.cotangent, ID_COTANGENT, half).wait_recv()
        gather_on(r.cotangent, ID_COTANGENT, half).wait_recv()
    both(feed_back, 0)
    finals.append(functools.partial(mix_on, 2))
    mix_near(2).wait_recv()
    mix_on(2).wait_recv()
    sum_on(0, ID_SUM_TWO, 0)
    both(feed, 1)
    finals.append(functools.partial(gather_on, r.cotangent, ID_COTANGENT, 1))
    gather_near(r.cotangent, ID_COTANGENT, 1).wait_recv()
    gather_on(r.cotangent, ID_COTANGENT, 1).wait_recv()
    stages = []

    def weight(index, number, crosses, columns, y_first, grad):
        base = ID_WEIGHTS + 9 * number
        halves, line, middle, full = (
            refs[index] for refs in (r.halves, r.lines, r.middles, r.fulls)
        )
        crossed = r.crossed[index // 2] if crosses else None
        blocks = grad.shape[0]
        cols = slice(columns[0], columns[0] + columns[1])
        size = PAIR if y_first else PIECE
        first, first_peer, second, second_peer = (
            (y, y_peer, z_low, z_pair) if y_first else (z_low, z_pair, y, y_peer)
        )
        source = (crossed if crosses else line).at[:, 0:size, cols]
        held = slice(0, PAIR) if y_first else at(second, PIECE)

        def final_rows(side):
            return at(first, PAIR) if y_first else at(2 * first + side, PIECE)

        def first_copy():
            return remote(
                grad.at[:, at(1 - first, PAIR), cols],
                halves.at[:, :, cols],
                base,
                replica=first_peer,
            )

        def second_copy():
            given = slice(0, PAIR) if y_first else at(1 - second, PIECE)
            return remote(
                halves.at[:, given, cols],
                line.at[:, 0:size, cols],
                base + 1,
                replica=second_peer,
            )

        def far_copy():
            apart = 2 if y_first else 4
            return remote(
                halves.at[:, held, cols],
                middle.at[:, 0:size, cols],
                base + 2,
                replica=replica + apart * (1 - 2 * z_high),
            )

        def farther_copy(level):
            apart = 8 * 2**level * (1 - 2 * ((block_of_eight // 2**level) % 2))
            return pltpu.make_async_remote_copy(
                src_ref=line.at[:, 0:size, cols],
                dst_ref=r.extras[index].at[level, :, 0:size, cols],
                send_sem=r.send_all.at[number + 1, level],
                recv_sem=r.recv_all.at[number + 1, level],
                device_id={"replica": replica + apart},
                device_id_type=MESH,
            )

        def cross_copy(step):
            return remote(
                line.at[mate(step), 0:size, cols],
                crossed.at[shard, 0:size, cols],
                base + 2 + step,
                shard=mate(step),
            )

        def second_back():
            return remote(
                source, full.at[:, final_rows(second), cols], base + 6, replica=second_peer
            )

        def first_back(late):
            if not late:
                return remote(
                    source, full.at[:, final_rows(second), cols], base + 7, replica=first_peer
                )
            ref = full.at[:, final_rows(1 - second), cols]
            return remote(ref, ref, base + 8 - y_first, replica=first_peer)

        def start():
            push(first_copy)

        def second_start():
            first_copy().wait_recv()
            for block in range(blocks):
                halves[block, :, cols] = (
                    to_single(grad[block, at(first, PAIR), cols])
                    + to_single(halves[block, :, cols])
                ).astype(BRAIN)
            if y_first:
                push_if(edge, second_copy)
            else:
                push(second_copy)

        def far_start():
            second_copy().wait_recv()
            for block in range(blocks):
                halves[block, held, cols] = (
                    to_single(halves[block, held, cols]) + to_single(line[block, 0:size, cols])
                ).astype(BRAIN)
            far_copy().start()

        def cross_start():
            far_copy().wait()
            for block in range(blocks):
                line[block, 0:size, cols] = (
                    to_single(halves[block, held, cols]) + to_single(middle[block, 0:size, cols])
                ).astype(BRAIN)
            for level in range(levels):
                farther_copy(level).start()
                farther_copy(level).wait()
                line[:, 0:size, cols] = (
                    to_single(line[:, 0:size, cols])
                    + to_single(r.extras[index][level, :, 0:size, cols])
                ).astype(BRAIN)
            if crosses:
                crossed[shard, 0:size, cols] = line[shard, 0:size, cols]
                for step in (2, 3, 1):
                    cross_copy(step).start()

        def back_start():
            if crosses:
                for step in (1, 2, 3):
                    cross_copy(step).wait()
            second_back().start()
            first_back(False).start()
            for block in range(blocks):
                full[block, final_rows(second), cols] = source[block]
            conditional.append((inner if y_first else None, second_back))
            conditional.append(
                (inner if y_first else None, functools.partial(first_back, False))
            )

        def back_on():
            second_back().wait_recv()
            push(first_back, True)

        def back_end():
            if not y_first:
                first_back(False).wait_recv()
            first_back(True).wait_recv()

        def only(condition, step):
            def run_if():
                pl.when(condition)(step)

            return run_if if y_first else step

        def edge_on():
            @pl.when(edge)
            def _():
                second_back().wait_recv()

            push_if(edge, first_back, True)

        stages.append(
            (
                start,
                second_start,
                only(inner, far_start),
                only(inner, cross_start),
                only(inner, back_start),
                edge_on if y_first else back_on,
                back_end,
            )
        )

    grads = (r.up_cut, r.up_grad, r.out_grad, r.qkv_grad)
    for index, (_, _, crosses, parts) in enumerate(WEIGHTS):
        for start_column, width, y_first in parts:
            weight(index, len(stages), crosses, (start_column, width), y_first, grads[index])

    def run(*codes):
        for code in codes:
            stages[code // 10][code % 10]()

    rest = []
    for item in finals:
        if item.func in (share_across, share_near) and item.args[0] is r.up_cut:
            item().wait_send()
        else:
            rest.append(item)
    finals[:] = rest

    def cut_product(target, left, right, width):
        for part in range(2):
            product = dot(
                left[:, :, part * HALF : (part + 1) * HALF].reshape(2 * length, HALF),
                right[...].reshape(2 * length, width),
                0,
                0,
            )
            for half in range(2):
                target[2 * part + half, :, 0:width] = product[
                    half * SLICE : (half + 1) * SLICE
                ].astype(BRAIN)

    steps = iter(PLAN)

    def plan():
        run(*next(steps))

    cut_product(r.up_cut, r.active, r.cotangent, D)
    run(40, 0, 10, 20, 30)
    plan()
    both(feed_back, 1)
    sum_on(0, ID_SUM_TWO, 1)
    cut_product(r.up_grad, r.hidden_two, r.lifted_grad, D)
    run(90, 50, 60, 70, 80)
    plan()

    for clip in (0, 1):
        grad_two = sum_end(0, ID_SUM_TWO, clip)
        normal, scale = normalize(r.middle_own[clip])
        r.columns[2:3, :] += row_sum(grad_two * normal)
        r.columns[3:4, :] += row_sum(grad_two)
        total = to_single(r.cotangent[clip, own, :]) + norm_back(
            grad_two, normal, scale, whole(G2)
        )
        r.input_grad_out[clip] = total
        r.gradient[clip, own, :] = total.astype(BRAIN)
        gather_start(r.gradient, ID_GRADIENT, clip)
        plan()

    def lower(clip, kind, carry):
        value = dot(r.active[clip, rows_of(kind), :], r.down_own[...], 1, 0)
        sum_step(1, ID_SUM_RESULT, clip, kind, value)
        return carry

    for clip in (0, 1):
        both(lower, clip)
        plan()

    def back_out(clip):
        gather_near(r.gradient, ID_GRADIENT, clip).wait_recv()
        gather_on(r.gradient, ID_GRADIENT, clip).wait_recv()
        grad = r.gradient[clip]
        r.columns[4:5, :] += row_sum(to_single(grad))
        r.mixed_grad[clip] = dot(grad, r.out_all[at(shard, SLICE), :], 1, 1).astype(BRAIN)

    def attend_back(clip, head):
        query = head_of(r.pairs, clip, head * HD)
        key = head_of(r.pairs, clip, SLICE + head * HD)
        value = head_of(r.pairs, clip, 2 * SLICE + head * HD)
        grad = head_of(r.mixed_grad, clip, head * HD)
        softened = r.soft[clip * LOCAL_HEADS + head]
        grad_soft = dot(value, grad, 1, 1)
        inner = row_sum(grad_soft * softened)
        grad_scores = (softened * (grad_soft - inner)).astype(BRAIN)
        entries = (
            (dot(key.T, grad_scores, 1, 0).T * HD**-0.5).astype(BRAIN),
            dot(grad_scores, query, 1, 0).astype(BRAIN),
            dot(softened.astype(BRAIN), grad, 1, 0).astype(BRAIN),
        )
        for part, entry in enumerate(entries):
            left = part * SLICE + head * HD
            r.pairs_grad[clip, :, left : left + HD] = entry

    for clip in (0, 1):
        gather_forward(r.gradient, ID_GRADIENT, clip)
        plan()
        back_out(clip)
        plan()
        if clip == 1:
            for other in (0, 1):
                sum_on(1, ID_SUM_RESULT, other)
        for head in range(LOCAL_HEADS):
            attend_back(clip, head)
            plan()
    product = None
    for clip in (0, 1):
        heads = jnp.concatenate(
            [r.mixed[shard, 2 * clip], r.mixed[shard, 1, :, clip * HD : (clip + 1) * HD]], 1
        )
        term = dot(heads, r.gradient[clip], 0, 0)
        product = term if product is None else product + term
    r.out_grad[0] = product.astype(BRAIN)
    run(100)
    plan()
    cut_product(r.qkv_grad, r.hidden_one, r.pairs_grad, QKV)
    r.qkv_grad[:, :, QKV:] = jnp.zeros((GROUP, SLICE, HD), BRAIN)
    run(110, 120, 130, 140, 150)
    plan()

    def back_project(clip, kind, carry):
        grad = r.pairs_grad[clip, rows_of(kind), :]
        r.columns[5:6, 0:QKV] += row_sum(to_single(grad))
        sum_step(0, ID_SUM_ONE, clip, kind, dot(grad, r.qkv_own[...], 1, 1))
        return carry

    for clip in (0, 1):
        both(back_project, clip)
        plan()
    for clip in (0, 1):
        sum_on(0, ID_SUM_ONE, clip)
    plan()
    for clip in (0, 1):
        live = 1.0 if clip == 0 else second_live
        result = r.middle_own[clip] + sum_end(1, ID_SUM_RESULT, clip) + whole(C2)
        r.result_out[clip] = (result * live).astype(BRAIN)
    plan()
    for clip in (0, 1):
        grad_one = sum_end(0, ID_SUM_ONE, clip)
        normal, scale = normalize(to_single(r.tokens[clip, own, :]))
        r.columns[6:7, :] += row_sum(grad_one * normal)
        r.columns[7:8, :] += row_sum(grad_one)
        r.input_grad_out[clip] += norm_back(grad_one, normal, scale, whole(G1))

    for member in range(GROUP):
        cols = slice(member * SLICE, (member + 1) * SLICE)
        for place, row in enumerate((6, 7, 2, 3, 4, 0)):
            r.small_sent[member, place : place + 1, :] = r.columns[row : row + 1, cols]

    def small_copy(step):
        return remote(
            r.small_sent.at[mate(step)],
            r.small_near.at[step - 1],
            ID_SMALL + step - 1,
            shard=mate(step),
        )

    for step in (1, 2, 3):
        push(small_copy, step)
    plan()
    for step in (1, 2, 3):
        small_copy(step).wait_recv()
    summed = r.small_sent[shard, 0:4, :]
    for step in (1, 2, 3):
        summed += r.small_near[step - 1, 0:4, :]
    r.small_all[replica, G1 : G1 + 2, :] = summed[0:2]
    r.small_all[replica, G2 : G2 + 2, :] = summed[2:4]
    r.small_all[replica, BO : BO + 1, :] = r.small_sent[shard, 4:5, :]
    r.small_all[replica, C2 : C2 + 1, :] = r.small_sent[shard, 5:6, :]
    r.small_all[replica, BQ : BQ + 1, :] = r.columns[5:6, 0:SLICE]
    r.small_all[replica, BV : BV + 1, :] = r.columns[5:6, 2 * SLICE : QKV]
    for part in range(GROUP):
        r.small_all[replica, C1 + part : C1 + part + 1, :] = r.columns[
            1:2, part * SLICE : (part + 1) * SLICE
        ]
    r.small_all[replica, C1 + GROUP :, :] = jnp.zeros((VECTOR_ROWS - C1 - GROUP, SLICE), SINGLE)

    def spread_copy(step):
        return pltpu.make_async_remote_copy(
            src_ref=r.small_all.at[replica],
            dst_ref=r.small_all.at[replica],
            send_sem=r.send_all.at[0, step],
            recv_sem=r.recv_all.at[0, step],
            device_id={"replica": (replica + step) % replicas},
            device_id_type=MESH,
        )

    def spread_start(step, carry):
        spread_copy(step).start()
        return carry

    lax.fori_loop(1, replicas, spread_start, 0)
    plan()

    def spread_wait(step, carry):
        spread_copy(step).wait()
        return carry

    lax.fori_loop(1, replicas, spread_wait, 0)
    small_sum = r.small_all[0]
    for step in range(1, replicas):
        small_sum += r.small_all[step]
    r.small_out[...] = small_sum
    for item in finals:
        item().wait_send()
    for condition, item in conditional:
        if condition is None:
            item().wait_send()
        else:

            @pl.when(condition)
            def _():
                item().wait_send()

    run(106)
    run(6, 16, 26, 36, 46)
    run(116, 126, 136, 146, 156)
    run(56, 66, 76, 86, 96)


def finish(fields, *refs):
    r = gathered(fields, refs)
    units = []

    def unit(wide, target, widen):
        units.append((pltpu.make_async_copy(wide, target, r.near.at[len(units)]), widen))

    def keep():
        pass

    def down(index):
        rows = slice(index * SLICE, (index + 1) * SLICE)

        def widen():
            r.wide[DOWN][rows, :] = to_single(r.narrow[DOWN][index])

        unit(r.wide[DOWN].at[rows], r.results[DOWN].at[rows], widen)

    def up(index):
        rows = slice(index * PIECE, (index + 1) * PIECE)

        def widen():
            for member in range(GROUP):
                r.wide[UP][rows, member * D : (member + 1) * D] = to_single(
                    r.narrow[UP][member, rows, :]
                )

        unit(r.wide[UP].at[rows], r.results[UP].at[rows], widen)

    def qkv(index):
        rows = slice(index * PIECE, (index + 1) * PIECE)

        def widen():
            for part in range(3):
                cols = slice(part * SLICE, (part + 1) * SLICE)
                r.wide[QKVS][rows, part * D : (part + 1) * D] = to_single(
                    jnp.concatenate(
                        [r.narrow[QKVS][member, rows, cols] for member in range(GROUP)], 1
                    )
                )

        unit(r.wide[QKVS].at[rows], r.results[QKVS].at[rows], widen)

    def out():
        def widen():
            r.wide[OUT][...] = to_single(r.narrow[OUT][0])

        unit(r.wide[OUT], r.results[OUT], widen)

    unit(r.input_grad_in, r.input_grad, keep)
    unit(r.result_in, r.result, keep)
    for index in range(GROUP):
        down(index)
        up(index)
    out()
    for index in range(GROUP):
        qkv(index)
    for row in range(8):
        r.vectors[row][...] = r.small_in[row : row + 1, :].reshape(SLICE)
    r.vectors[8][...] = jnp.concatenate(
        [r.small_in[C1 + part : C1 + part + 1, :] for part in range(GROUP)], 1
    ).reshape(D)
    for store, widen in units:
        widen()
        store.start()
    for store, _ in units:
        store.wait()


def layer(replicas, *arguments):
    (
        tokens, cotangent, clip_count, ln1_gain, ln1_bias, qkv_weight, q_bias, v_bias,
        out_weight, out_bias, ln2_gain, ln2_bias, fc1_weight, fc1_bias, fc2_weight, fc2_bias,
    ) = arguments
    slots, slot, _ = tokens.shape
    length = slot * GROUP
    levels = (replicas // 8).bit_length() - 1
    vectors = (
        ln1_gain, ln1_bias, out_bias, ln2_gain, ln2_bias, fc2_bias, q_bias, v_bias, fc1_bias,
    )
    anywhere = pl.BlockSpec(memory_space=pl.ANY)
    in_memory = pl.BlockSpec(memory_space=pltpu.VMEM)
    shape = jax.ShapeDtypeStruct

    inputs = dict(
        tokens_in=anywhere,
        cotangent_in=anywhere,
        count_in=pl.BlockSpec(memory_space=pltpu.SMEM),
        vectors_in=[anywhere] * 9,
        qkv_in=anywhere,
        out_in=anywhere,
        up_in=anywhere,
        down_in=anywhere,
    )
    outputs = dict(
        result_out=pltpu.VMEM(tokens.shape, BRAIN),
        input_grad_out=pltpu.VMEM(tokens.shape, SINGLE),
        small_out=pltpu.VMEM((VECTOR_ROWS, SLICE), SINGLE),
        fulls=[pltpu.VMEM((blocks, SLICE, columns), BRAIN) for blocks, columns, _, _ in WEIGHTS],
    )
    scratch = dict(
        qkv_wide=pltpu.VMEM(qkv_weight.shape, SINGLE),
        out_wide=pltpu.VMEM(out_weight.shape, SINGLE),
        up_wide=pltpu.VMEM(fc1_weight.shape, SINGLE),
        down_wide=pltpu.VMEM(fc2_weight.shape, SINGLE),
        qkv_cut=pltpu.VMEM((GROUP, SLICE, QKV), BRAIN),
        up_cut=pltpu.VMEM((GROUP, SLICE, D), BRAIN),
        qkv_own=pltpu.VMEM((D, QKV), BRAIN),
        up_own=pltpu.VMEM((D, D), BRAIN),
        out_all=pltpu.VMEM((D, D), BRAIN),
        down_own=pltpu.VMEM((D, D), BRAIN),
        vectors=pltpu.VMEM((GROUP, VECTOR_ROWS, SLICE), SINGLE),
        vectors_raw=[pltpu.VMEM(vector.shape, SINGLE) for vector in vectors],
        tokens=pltpu.VMEM((2, length, D), BRAIN),
        cotangent=pltpu.VMEM((2, length, D), BRAIN),
        hidden_one=pltpu.VMEM((2, length, D), BRAIN),
        pairs=pltpu.VMEM((2, length, QKV), BRAIN),
        soft=pltpu.VMEM((2 * LOCAL_HEADS, length, length), SINGLE),
        mixed=pltpu.VMEM((GROUP, 3, length, TILE), BRAIN),
        middle_own=pltpu.VMEM((2, slot, D), SINGLE),
        hidden_two=pltpu.VMEM((2, length, D), BRAIN),
        active=pltpu.VMEM((2, length, D), BRAIN),
        lifted_grad=pltpu.VMEM((2, length, D), BRAIN),
        gradient=pltpu.VMEM((2, length, D), BRAIN),
        mixed_grad=pltpu.VMEM((2, length, SLICE), BRAIN),
        pairs_grad=pltpu.VMEM((2, length, QKV), BRAIN),
        stage=pltpu.VMEM((2 * slot, D), SINGLE),
        sum_sent=pltpu.VMEM((2, 2, 3, slot, D), BRAIN),
        sum_near=pltpu.VMEM((2, 2, 2, slot, D), BRAIN),
        sum_far=pltpu.VMEM((2, 2, slot, D), BRAIN),
        sum_own=pltpu.VMEM((2, 2, slot, D), SINGLE),
        up_grad=pltpu.VMEM((GROUP, SLICE, D), BRAIN),
        out_grad=pltpu.VMEM((1, SLICE, D), BRAIN),
        qkv_grad=pltpu.VMEM((GROUP, SLICE, QKV + HD), BRAIN),
        columns=pltpu.VMEM((8, D), SINGLE),
        small_sent=pltpu.VMEM((GROUP, 8, SLICE), SINGLE),
        small_near=pltpu.VMEM((GROUP - 1, 8, SLICE), SINGLE),
        small_all=pltpu.VMEM((replicas, VECTOR_ROWS, SLICE), SINGLE),
        halves=[pltpu.VMEM((w[0], PAIR, w[1]), BRAIN) for w in WEIGHTS],
        lines=[pltpu.VMEM((w[0], PAIR, w[1]), BRAIN) for w in WEIGHTS],
        middles=[pltpu.VMEM((w[0], PAIR, w[1]), BRAIN) for w in WEIGHTS],
        crossed=[pltpu.VMEM((GROUP, PAIR, w[1]), BRAIN) for w in WEIGHTS if w[2]],
        extras=[
            pltpu.VMEM((levels, w[0], PAIR, w[1]) if levels else (1, 1, 16, TILE), BRAIN)
            for w in WEIGHTS
        ],
        send=pltpu.SemaphoreType.DMA((COPIES,)),
        recv=pltpu.SemaphoreType.DMA((COPIES,)),
        send_all=pltpu.SemaphoreType.DMA((1 + ITEMS, replicas)),
        recv_all=pltpu.SemaphoreType.DMA((1 + ITEMS, replicas)),
        near=pltpu.SemaphoreType.DMA((LOCALS,)),
    )
    sums = pl.pallas_call(
        functools.partial(kernel, replicas, counted(inputs) + counted(outputs) + counted(scratch)),
        out_shape=tuple(flat(outputs)),
        in_specs=flat(inputs),
        out_specs=(in_memory,) * len(flat(outputs)),
        scratch_shapes=flat(scratch),
        compiler_params=pltpu.CompilerParams(
            collective_id=0, has_side_effects=True, vmem_limit_bytes=60600 * 1024
        ),
        name="layer",
    )(
        tokens, cotangent, clip_count, *vectors, qkv_weight, out_weight, fc1_weight, fc2_weight
    )

    matrices = [fc2_weight, fc1_weight, out_weight, qkv_weight]
    last_inputs = dict(
        result_in=in_memory, input_grad_in=in_memory, small_in=in_memory, narrow=[in_memory] * 4
    )
    last_outputs = dict(
        result=shape(tokens.shape, BRAIN),
        input_grad=shape(tokens.shape, SINGLE),
        results=[shape(array.shape, SINGLE) for array in matrices],
        vectors=[shape(vector.shape, SINGLE) for vector in vectors],
    )
    last_scratch = dict(
        wide=[pltpu.VMEM(array.shape, SINGLE) for array in matrices],
        near=pltpu.SemaphoreType.DMA((16,)),
    )
    values = pl.pallas_call(
        functools.partial(
            finish, counted(last_inputs) + counted(last_outputs) + counted(last_scratch)
        ),
        out_shape=tuple(flat(last_outputs)),
        in_specs=flat(last_inputs),
        out_specs=(anywhere,) * 6 + (in_memory,) * 9,
        scratch_shapes=flat(last_scratch),
        compiler_params=pltpu.CompilerParams(vmem_limit_bytes=32 << 20),
        name="finish",
    )(*sums)
    o = gathered(counted(last_outputs), values)
    return (
        o.result,
        o.input_grad,
        o.vectors[G1],
        o.vectors[B1],
        o.results[QKVS],
        o.vectors[BQ],
        o.vectors[BV],
        o.results[OUT],
        o.vectors[BO],
        o.vectors[G2],
        o.vectors[B2],
        o.results[UP],
        o.vectors[C1],
        o.results[DOWN],
        o.vectors[C2],
    )


def solution(mesh):
    token, vector, matrix = P("replica", "shard", None), P("shard"), P("shard", None)
    return jax.shard_map(
        functools.partial(layer, mesh.shape["replica"]),
        mesh=mesh,
        in_specs=(
            token, token, P("replica"), vector, vector, matrix, vector, vector,
            matrix, vector, vector, vector, matrix, vector, matrix, vector,
        ),
        out_specs=(
            token, token, vector, vector, matrix, vector, vector, matrix,
            vector, vector, vector, matrix, vector, matrix, vector,
        ),
        check_vma=False,
    )
```

```python
import functools
import types

import jax
import jax.numpy as jnp
from jax import lax
from jax.experimental import pallas as pl
from jax.experimental.pallas import tpu as pltpu
from jax.sharding import PartitionSpec as P

D = 768
HD = 64
EPSILON = 1e-06
GROUP = 4
SLICE = D // GROUP
LOCAL_HEADS = SLICE // HD
HALF = D // 2
TILE = 128
PAIR = SLICE // 2
PIECE = SLICE // 4
QKV = 3 * SLICE
BRAIN = jnp.bfloat16
SINGLE = jnp.float32
MESH = pl.DeviceIdType.MESH

G1, B1, BO, G2, B2, C2, BQ, BV, C1 = range(9)
VECTOR_ROWS = 16

WEIGHTS = (
    (GROUP, D, False, ((0, 128, True), (128, 128, True), (256, 128, True), (384, 128, True), (512, 256, False))),
    (GROUP, D, True, ((0, 128, True), (128, 128, True), (256, 128, True), (384, 128, True), (512, 256, False))),
    (1, D, False, ((0, 768, False),)),
    (GROUP, 640, True, ((0, 128, True), (128, 128, True), (256, 128, True), (384, 128, True), (512, 128, True))),
)
DOWN, UP, OUT, QKVS = range(4)
ITEMS = sum(len(parts) for _, _, _, parts in WEIGHTS)

MIXES = (((0, 0), (0, 1)), ((0, 2), (1, 2)), ((1, 0), (1, 1)))


PLAN = (
    (),
    (),
    (1, 41, 11, 21),
    (),
    (91, 31),
    (2, 51),
    (12, 61),
    (),
    (22, 3, 4),
    (32, 13, 14),
    (),
    (52, 23, 24, 71),
    (81, 33, 62),
    (42, 72, 53),
    (5, 34, 82),
    (),
    (15, 92, 63),
    (25,),
    (),
    (73, 35, 43, 44, 111, 83, 101),
    (),
    (74, 121, 84, 131, 93, 141, 75, 64, 54, 112, 151, 85, 122, 45, 65, 113, 132, 102),
    (55, 123, 142, 114, 133, 152),
    (124, 94, 115, 134, 125, 143, 103, 104, 153, 144, 135, 154, 95, 145, 105, 155),
)


class Names:
    def __init__(self):
        self.total = 0

    def take(self, count):
        first = self.total
        self.total += count
        return first


ids = Names()
ID_TOKENS = ids.take(6)
ID_COTANGENT = ids.take(12)
ID_GRADIENT = ids.take(6)
ID_VECTORS = ids.take(3)
ID_QKV = ids.take(9)
ID_OUT = ids.take(9)
ID_UP = ids.take(9)
ID_MIX = ids.take(9)
ID_SUM_TWO = ids.take(6)
ID_SUM_RESULT = ids.take(6)
ID_SUM_ONE = ids.take(6)
ID_SMALL = ids.take(3)
ID_WEIGHTS = ids.take(9 * ITEMS)
COPIES = ids.total
LOCALS = 32


def to_single(value):
    return value.astype(SINGLE)


def rounded(value):
    return value.astype(BRAIN).astype(SINGLE)


def dot(left, right, left_dim, right_dim):
    return lax.dot_general(
        left, right, (((left_dim,), (right_dim,)), ((), ())), preferred_element_type=SINGLE
    )


def normalize(value):
    mean = jnp.sum(value, axis=-1, keepdims=True) * (1.0 / D)
    centred = value - mean
    spread = jnp.sum(centred * centred, axis=-1, keepdims=True) * (1.0 / D)
    scale = lax.rsqrt(spread + EPSILON)
    return centred * scale, scale


def norm_back(grad, normal, scale, gain):
    scaled = grad * gain
    first = jnp.sum(scaled, axis=-1, keepdims=True) * (1.0 / D)
    second = jnp.sum(scaled * normal, axis=-1, keepdims=True) * (1.0 / D)
    return scale * (scaled - first - normal * second)


def row_sum(value):
    return jnp.sum(value, axis=0, keepdims=True)


def gathered(fields, refs):
    result, refs = {}, list(refs)
    for name, count in fields:
        result[name] = [refs.pop(0) for _ in range(count)] if count > 1 else refs.pop(0)
    return types.SimpleNamespace(**result)


def counted(fields):
    return [(name, len(entry) if isinstance(entry, list) else 1) for name, entry in fields.items()]


def flat(fields):
    result = []
    for entry in fields.values():
        result += entry if isinstance(entry, list) else [entry]
    return result


def kernel(replicas, fields, *refs):
    r = gathered(fields, refs)
    levels = (replicas // 8).bit_length() - 1
    slot = r.tokens_in.shape[1]
    pair = 2 * slot
    length = GROUP * slot

    shard = lax.axis_index("shard")
    replica = lax.axis_index("replica")
    chip = shard // 2
    core = shard % 2
    y = replica % 2
    z_low = (replica // 2) % 2
    z_high = (replica // 4) % 2
    inner = (z_low + z_high) % 2 == 1
    edge = (z_low + z_high) % 2 == 0
    block_of_eight = replica // 8
    y_peer = replica + 1 - 2 * y
    z_pair = replica + 2 * (1 - 2 * z_low)

    def mate(step):
        return 2 * ((chip + step // 2) % 2) + (shard + step) % 2

    finals, conditional = [], []

    def remote(source, target, index, **where):
        return pltpu.make_async_remote_copy(
            src_ref=source,
            dst_ref=target,
            send_sem=r.send.at[index],
            recv_sem=r.recv.at[index],
            device_id=where,
            device_id_type=MESH,
        )

    def push(make, *arguments):
        make(*arguments).start()
        finals.append(functools.partial(make, *arguments))

    def push_if(condition, make, *arguments):
        @pl.when(condition)
        def _():
            make(*arguments).start()

        conditional.append((condition, functools.partial(make, *arguments)))

    def local(source, target, index):
        return pltpu.make_async_copy(source, target, r.near.at[index])

    def at(index, size, offset=0):
        return pl.ds(pl.multiple_of(index * size + offset, size), size)

    def here(ref, clip):
        return ref.at[clip, at(shard, slot), :]

    def quarter_rows(step):
        return at((2 * y + z_low + step) % 4, PIECE)

    qkv_loads = [
        local(r.qkv_in.at[quarter_rows(step)], r.qkv_wide.at[quarter_rows(step)], 25 + step)
        for step in range(4)
    ]
    token_loads = [local(r.tokens_in.at[clip], here(r.tokens, clip), 1 + clip) for clip in (0, 1)]
    vector_loads = [
        local(r.vectors_in[row], r.vectors_raw[row], 3 + row)
        for row in range(9)
    ]
    cotangent_loads = [
        local(r.cotangent_in.at[clip], here(r.cotangent, clip), 12 + clip) for clip in (0, 1)
    ]
    wide_loads = [
        local(r.up_in, r.up_wide, 14),
        local(r.out_in, r.out_wide, 15),
        local(r.down_in, r.down_wide, 16),
    ]
    for load in qkv_loads + token_loads + vector_loads + cotangent_loads + wide_loads:
        load.start()
    barrier = pltpu.get_barrier_semaphore()
    for step in (1, 2, 3):
        pl.semaphore_signal(barrier, inc=1, device_id={"shard": mate(step)}, device_id_type=MESH)

    def greet(step, carry):
        peer = (replica + step) % replicas
        pl.semaphore_signal(barrier, inc=1, device_id={"replica": peer}, device_id_type=MESH)
        return carry

    lax.fori_loop(1, replicas, greet, 0)

    def cut_rows(step):
        qkv_loads[step].wait()
        rows = quarter_rows(step)
        for member in range(GROUP):
            left = member * SLICE
            r.qkv_cut[member, rows, :] = jnp.concatenate(
                [
                    r.qkv_wide[rows, part * D + left : part * D + left + SLICE].astype(BRAIN)
                    for part in range(3)
                ],
                axis=1,
            )

    cut_rows(0)
    for load in token_loads + vector_loads:
        load.wait()
    pl.semaphore_wait(barrier, replicas + 2)

    def gather_part(buffer, clip, member):
        if clip >= 2:
            return buffer.at[0, at(2 * member + clip - 2, slot // 2), :]
        return buffer.at[clip, at(member, slot), :]

    def gather_near(buffer, base, clip):
        part = gather_part(buffer, clip, shard)
        return remote(part, part, base + 3 * clip, shard=mate(1))

    def gather_across(buffer, base, clip):
        part = gather_part(buffer, clip, shard)
        return remote(part, part, base + 3 * clip + 1, shard=mate(2))

    def gather_on(buffer, base, clip):
        part = gather_part(buffer, clip, mate(2))
        return remote(part, part, base + 3 * clip + 2, shard=mate(1))

    def gather_start(buffer, base, clip):
        push(gather_across, buffer, base, clip)
        push(gather_near, buffer, base, clip)

    def gather_forward(buffer, base, clip):
        gather_across(buffer, base, clip).wait_recv()
        push(gather_on, buffer, base, clip)

    def quarter(member, y_side, z_side):
        return at((member * 2 + y_side) * 2 + z_side, PIECE)

    def share_across(cut, buffer, base, step):
        source = buffer.at[quarter(shard, y, z_low), :]
        if cut is not None:
            source = cut.at[mate(step), at(2 * y + z_low, PIECE), :]
        return remote(
            source, buffer.at[quarter(shard, y, z_low), :], base + step - 2, shard=mate(step)
        )

    def share_z(buffer, base, step):
        part = buffer.at[quarter(mate(step), y, z_low), :]
        return remote(part, part, base + step, replica=z_pair)

    def share_y(buffer, base, step, second):
        side = 1 - z_low if second else z_low
        part = buffer.at[quarter(mate(step), y, side), :]
        return remote(part, part, base + 2 * second + 2 + step, replica=y_peer)

    def share_near(cut, buffer, base):
        target = buffer.at[at(shard, SLICE), :]
        source = target if cut is None else cut.at[mate(1)]
        return remote(source, target, base + 8, shard=mate(1))

    def share_first(cut, buffer, base, steps):
        for step in steps:
            push(share_across, cut, buffer, base, step)

    def share_start(cut, buffer, base, steps):
        share_first(cut, buffer, base, steps)
        push(share_near, cut, buffer, base)

    def share_on(cut, buffer, base, steps):
        for step in steps:
            share_across(cut, buffer, base, step).wait_recv()
            push(share_z, buffer, base, step)
            push(share_y, buffer, base, step, 0)

    def share_last(buffer, base, steps):
        for step in steps:
            share_z(buffer, base, step).wait_recv()
            push(share_y, buffer, base, step, 1)

    def share_wait(cut, buffer, base, steps):
        for step in steps:
            share_y(buffer, base, step, 0).wait_recv()
            share_y(buffer, base, step, 1).wait_recv()
        share_near(cut, buffer, base).wait_recv()

    BOTH, ONE = (2, 3), (2,)
    FIRST, SECOND = 2, 3

    share_first(r.qkv_cut, r.qkv_own, ID_QKV, BOTH)
    gather_start(r.tokens, ID_TOKENS, 0)
    for row in range(8):
        r.vectors[shard, row : row + 1, :] = rounded(
            r.vectors_raw[row][...].reshape(1, SLICE)
        )
    long_row = rounded(r.vectors_raw[8][...].reshape(1, D))
    for part in range(GROUP):
        r.vectors[shard, C1 + part : C1 + part + 1, :] = long_row[
            :, part * SLICE : (part + 1) * SLICE
        ]
    r.vectors[shard, C1 + GROUP :, :] = jnp.zeros((VECTOR_ROWS - C1 - GROUP, SLICE), SINGLE)

    def send_vectors(step):
        return remote(
            r.vectors.at[shard], r.vectors.at[shard], ID_VECTORS + step - 1, shard=mate(step)
        )

    for step in (1, 2, 3):
        push(send_vectors, step)
    for load in wide_loads:
        load.wait()
    for member in range(GROUP):
        r.up_cut[member] = r.up_wide[:, member * D : (member + 1) * D].astype(BRAIN)
    r.out_all[at(shard, SLICE), :] = r.out_wide[...].astype(BRAIN)
    share_start(None, r.out_all, ID_OUT, ONE)
    share_start(r.up_cut, r.up_own, ID_UP, BOTH)
    gather_start(r.tokens, ID_TOKENS, 1)

    for step in (1, 2, 3):
        cut_rows(step)
    push(share_near, r.qkv_cut, r.qkv_own, ID_QKV)
    r.qkv_own[at(shard, SLICE), :] = r.qkv_cut[shard]
    share_on(r.qkv_cut, r.qkv_own, ID_QKV, BOTH)
    for load in cotangent_loads:
        load.wait()
    second_live = to_single(jnp.minimum(r.count_in[0] - 1, 1))
    own = at(shard, slot)
    r.cotangent[1, own, :] = (to_single(r.cotangent[1, own, :]) * second_live).astype(BRAIN)
    r.up_own[at(shard, SLICE), :] = r.up_cut[shard]
    r.down_own[...] = r.down_wide[...].astype(BRAIN)
    r.columns[...] = jnp.zeros_like(r.columns)
    share_last(r.qkv_own, ID_QKV, BOTH)
    gather_forward(r.tokens, ID_TOKENS, 0)

    def whole(row):
        return jnp.concatenate([r.vectors[member, row : row + 1, :] for member in range(GROUP)], 1)

    def mine(row):
        return r.vectors[shard, row : row + 1, :]

    for step in (1, 2, 3):
        send_vectors(step).wait_recv()
    share_wait(r.qkv_cut, r.qkv_own, ID_QKV, BOTH)
    scale_row = jnp.where(lax.broadcasted_iota(jnp.int32, (1, QKV), 1) < SLICE, HD**-0.5, 1.0)
    qkv_bias = jnp.concatenate([mine(BQ), jnp.zeros((1, SLICE), SINGLE), mine(BV)], 1)

    def project(clip, side):
        rows = at((chip + side) % 2, pair)
        normal, _ = normalize(to_single(r.tokens[clip, rows, :]))
        hidden = (normal * whole(G1) + whole(B1)).astype(BRAIN)
        r.hidden_one[clip, rows, :] = hidden
        product = (dot(hidden, r.qkv_own[...], 1, 0) + qkv_bias) * scale_row
        r.pairs[clip, rows, :] = product.astype(BRAIN)

    def mix_near(part):
        ref = r.mixed.at[shard, part]
        return remote(ref, ref, ID_MIX + 3 * part, shard=mate(1))

    def mix_across(part):
        ref = r.mixed.at[shard, part]
        return remote(ref, ref, ID_MIX + 3 * part + 1, shard=mate(2))

    def mix_on(part):
        ref = r.mixed.at[mate(2), part]
        return remote(ref, ref, ID_MIX + 3 * part + 2, shard=mate(1))

    def mix_forward(part):
        mix_across(part).wait_recv()
        push(mix_on, part)

    def head_of(ref, clip, left):
        return ref[clip, :, left : left + HD]

    def attend(part, place):
        clip, head = MIXES[part][place]
        query = head_of(r.pairs, clip, head * HD)
        key = head_of(r.pairs, clip, SLICE + head * HD)
        value = head_of(r.pairs, clip, 2 * SLICE + head * HD)
        scores = dot(key, query, 1, 1)
        highest = jnp.max(scores, axis=0, keepdims=True)
        expanded = jnp.exp(scores - highest)
        softened = expanded * (1.0 / row_sum(expanded))
        r.soft[clip * LOCAL_HEADS + head] = softened
        mixture = dot(value.T, softened.astype(BRAIN), 1, 0).T.astype(BRAIN)
        r.mixed[shard, part, :, place * HD : (place + 1) * HD] = mixture

    def mix_start(part):
        push(mix_across, part)
        push(mix_near, part)

    gather_near(r.tokens, ID_TOKENS, 0).wait_recv()
    project(0, 0)
    gather_on(r.tokens, ID_TOKENS, 0).wait_recv()
    project(0, 1)
    attend(0, 0)
    share_on(None, r.out_all, ID_OUT, ONE)
    share_on(r.up_cut, r.up_own, ID_UP, BOTH)
    attend(0, 1)
    mix_start(0)
    gather_start(r.cotangent, ID_COTANGENT, FIRST)
    attend(1, 0)
    gather_near(r.tokens, ID_TOKENS, 1).wait_recv()
    project(1, 0)
    gather_forward(r.tokens, ID_TOKENS, 1)
    gather_on(r.tokens, ID_TOKENS, 1).wait_recv()
    project(1, 1)
    attend(1, 1)
    mix_start(1)
    gather_start(r.cotangent, ID_COTANGENT, SECOND)
    share_last(r.out_all, ID_OUT, ONE)
    share_last(r.up_own, ID_UP, BOTH)
    mix_forward(0)
    attend(2, 0)
    attend(2, 1)
    mix_start(2)
    gather_start(r.cotangent, ID_COTANGENT, 1)

    def out_on():
        part = r.out_all.at[at(mate(2), SLICE), :]
        return remote(part, part, ID_OUT + 1, shard=mate(1))

    share_wait(None, r.out_all, ID_OUT, ONE)
    push(out_on)
    mix_forward(1)
    out_on().wait_recv()
    for part in (0, 1):
        mix_near(part).wait_recv()
        mix_on(part).wait_recv()
    share_wait(r.up_cut, r.up_own, ID_UP, BOTH)

    def sum_near(which, base, clip, kind):
        return remote(
            r.sum_sent.at[which, clip, kind],
            r.sum_near.at[which, clip, kind],
            base + 3 * clip + kind,
            shard=mate(1),
        )

    def sum_far(which, base, clip):
        return remote(
            r.sum_sent.at[which, clip, 2],
            r.sum_far.at[which, clip],
            base + 3 * clip + 2,
            shard=mate(2),
        )

    def sum_kept(which, clip, kind):
        if which == 0:
            return r.sum_own.at[clip, kind]
        return r.up_wide.at[0:slot, at(2 * clip + kind, D)]

    def sum_step(which, base, clip, kind, value):
        r.stage[...] = value
        r.sum_sent[which, clip, kind] = r.stage[at(1 - core, slot), :].astype(BRAIN)
        sum_kept(which, clip, kind)[...] = r.stage[at(core, slot), :]
        remote(
            r.sum_sent.at[which, clip, kind],
            r.sum_near.at[which, clip, kind],
            base + 3 * clip + kind,
            shard=mate(1),
        ).start()

    def sum_on(which, base, clip):
        sum_near(which, base, clip, 0).wait_recv()
        r.sum_sent[which, clip, 2] = (
            sum_kept(which, clip, 0)[...] + to_single(r.sum_near[which, clip, 0])
        ).astype(BRAIN)
        sum_far(which, base, clip).start()

    def sum_end(which, base, clip):
        sum_near(which, base, clip, 0).wait_send()
        sum_near(which, base, clip, 1).wait()
        sum_far(which, base, clip).wait()
        return (
            sum_kept(which, clip, 1)[...]
            + to_single(r.sum_near[which, clip, 1])
            + to_single(r.sum_far[which, clip])
        )

    def rows_of(kind):
        return at((chip + 1 + kind) % 2, pair)

    long_bias = jnp.concatenate(
        [r.vectors[shard, C1 + part : C1 + part + 1, :] for part in range(GROUP)], 1
    )

    def pass_on(across, on):
        across.wait_recv()
        on.start()

    def feed(clip, kind, carry):
        rows = rows_of(kind)

        @pl.when(kind == 1)
        def _():
            for part in ((FIRST, SECOND), (1,))[clip]:
                pass_on(
                    gather_across(r.cotangent, ID_COTANGENT, part),
                    gather_on(r.cotangent, ID_COTANGENT, part),
                )

        total = to_single(r.tokens[clip, rows, :]) + whole(BO)
        for first in (0, 2):
            heads = jnp.concatenate(
                [r.mixed[member, 2 * clip, rows, :] for member in (first, first + 1)], 1
            )
            weights = jnp.concatenate(
                [
                    r.out_all[member * SLICE : member * SLICE + TILE, :]
                    for member in (first, first + 1)
                ],
                0,
            )
            total += dot(heads, weights, 1, 0)
        heads = jnp.concatenate(
            [r.mixed[member, 1, rows, clip * HD : (clip + 1) * HD] for member in range(GROUP)], 1
        )
        weights = jnp.concatenate(
            [
                r.out_all[member * SLICE + TILE : (member + 1) * SLICE, :]
                for member in range(GROUP)
            ],
            0,
        )
        total += dot(heads, weights, 1, 0)

        @pl.when(kind == 1)
        def _():
            r.stage[...] = total
            r.middle_own[clip] = r.stage[at(core, slot), :]

        normal, _ = normalize(total)
        hidden = (normal * whole(G2) + whole(B2)).astype(BRAIN)
        r.hidden_two[clip, rows, :] = hidden
        lifted = dot(hidden, r.up_own[...], 1, 0) + long_bias
        share = 0.5 + 0.5 * lax.erf(lifted * (0.5**0.5))
        r.active[clip, rows, :] = (lifted * share).astype(BRAIN)
        r.down_wide[at(kind, pair), :] = share + lifted * jnp.exp(lifted * lifted * -0.5) * 0.3989422804014327
        return carry

    def feed_back(clip, kind, carry):
        rows = rows_of(kind)
        if clip == 0:

            @pl.when(kind == 1)
            def _():
                pass_on(mix_across(2), mix_on(2))

        down = r.cotangent[clip, rows, :]
        r.columns[0:1, :] += row_sum(to_single(down))
        grad = (dot(down, r.down_own[...], 1, 1) * r.down_wide[at(kind, pair), :]).astype(BRAIN)
        r.lifted_grad[clip, rows, :] = grad
        r.columns[1:2, :] += row_sum(to_single(grad))
        sum_step(0, ID_SUM_TWO, clip, kind, dot(grad, r.up_own[...], 1, 1))
        return carry

    def both(step, clip):
        lax.fori_loop(0, 2, functools.partial(step, clip), 0)

    both(feed, 0)
    for half in (FIRST, SECOND):
        finals.append(functools.partial(gather_on, r.cotangent, ID_COTANGENT, half))
        gather_near(r.cotangent, ID_COTANGENT, half).wait_recv()
        gather_on(r.cotangent, ID_COTANGENT, half).wait_recv()
    both(feed_back, 0)
    finals.append(functools.partial(mix_on, 2))
    mix_near(2).wait_recv()
    mix_on(2).wait_recv()
    sum_on(0, ID_SUM_TWO, 0)
    both(feed, 1)
    finals.append(functools.partial(gather_on, r.cotangent, ID_COTANGENT, 1))
    gather_near(r.cotangent, ID_COTANGENT, 1).wait_recv()
    gather_on(r.cotangent, ID_COTANGENT, 1).wait_recv()
    stages = []

    def weight(index, number, crosses, columns, y_first, grad):
        base = ID_WEIGHTS + 9 * number
        halves, line, middle, full = (
            refs[index] for refs in (r.halves, r.lines, r.middles, r.fulls)
        )
        crossed = r.crossed[index // 2] if crosses else None
        blocks = grad.shape[0]
        cols = slice(columns[0], columns[0] + columns[1])
        size = PAIR if y_first else PIECE
        first, first_peer, second, second_peer = (
            (y, y_peer, z_low, z_pair) if y_first else (z_low, z_pair, y, y_peer)
        )
        source = (crossed if crosses else line).at[:, 0:size, cols]
        held = slice(0, PAIR) if y_first else at(second, PIECE)

        def final_rows(side):
            return at(first, PAIR) if y_first else at(2 * first + side, PIECE)

        def first_copy():
            return remote(
                grad.at[:, at(1 - first, PAIR), cols],
                halves.at[:, :, cols],
                base,
                replica=first_peer,
            )

        def second_copy():
            given = slice(0, PAIR) if y_first else at(1 - second, PIECE)
            return remote(
                halves.at[:, given, cols],
                line.at[:, 0:size, cols],
                base + 1,
                replica=second_peer,
            )

        def far_copy():
            apart = 2 if y_first else 4
            return remote(
                halves.at[:, held, cols],
                middle.at[:, 0:size, cols],
                base + 2,
                replica=replica + apart * (1 - 2 * z_high),
            )

        def farther_copy(level):
            apart = 8 * 2**level * (1 - 2 * ((block_of_eight // 2**level) % 2))
            return pltpu.make_async_remote_copy(
                src_ref=line.at[:, 0:size, cols],
                dst_ref=r.extras[index].at[level, :, 0:size, cols],
                send_sem=r.send_all.at[number + 1, level],
                recv_sem=r.recv_all.at[number + 1, level],
                device_id={"replica": replica + apart},
                device_id_type=MESH,
            )

        def cross_copy(step):
            return remote(
                line.at[mate(step), 0:size, cols],
                crossed.at[shard, 0:size, cols],
                base + 2 + step,
                shard=mate(step),
            )

        def second_back():
            return remote(
                source, full.at[:, final_rows(second), cols], base + 6, replica=second_peer
            )

        def first_back(late):
            if not late:
                return remote(
                    source, full.at[:, final_rows(second), cols], base + 7, replica=first_peer
                )
            ref = full.at[:, final_rows(1 - second), cols]
            return remote(ref, ref, base + 8 - y_first, replica=first_peer)

        def start():
            push(first_copy)

        def second_start():
            first_copy().wait_recv()
            for block in range(blocks):
                halves[block, :, cols] = (
                    to_single(grad[block, at(first, PAIR), cols])
                    + to_single(halves[block, :, cols])
                ).astype(BRAIN)
            if y_first:
                push_if(edge, second_copy)
            else:
                push(second_copy)

        def far_start():
            second_copy().wait_recv()
            for block in range(blocks):
                halves[block, held, cols] = (
                    to_single(halves[block, held, cols]) + to_single(line[block, 0:size, cols])
                ).astype(BRAIN)
            far_copy().start()

        def cross_start():
            far_copy().wait()
            for block in range(blocks):
                line[block, 0:size, cols] = (
                    to_single(halves[block, held, cols]) + to_single(middle[block, 0:size, cols])
                ).astype(BRAIN)
            for level in range(levels):
                farther_copy(level).start()
                farther_copy(level).wait()
                line[:, 0:size, cols] = (
                    to_single(line[:, 0:size, cols])
                    + to_single(r.extras[index][level, :, 0:size, cols])
                ).astype(BRAIN)
            if crosses:
                crossed[shard, 0:size, cols] = line[shard, 0:size, cols]
                for step in (2, 3, 1):
                    cross_copy(step).start()

        def back_start():
            if crosses:
                for step in (1, 2, 3):
                    cross_copy(step).wait()
            second_back().start()
            first_back(False).start()
            for block in range(blocks):
                full[block, final_rows(second), cols] = source[block]
            conditional.append((inner if y_first else None, second_back))
            conditional.append(
                (inner if y_first else None, functools.partial(first_back, False))
            )

        def back_on():
            second_back().wait_recv()
            push(first_back, True)

        def back_end():
            if not y_first:
                first_back(False).wait_recv()
            first_back(True).wait_recv()

        def only(condition, step):
            def run_if():
                pl.when(condition)(step)

            return run_if if y_first else step

        def edge_on():
            @pl.when(edge)
            def _():
                second_back().wait_recv()

            push_if(edge, first_back, True)

        stages.append(
            (
                start,
                second_start,
                only(inner, far_start),
                only(inner, cross_start),
                only(inner, back_start),
                edge_on if y_first else back_on,
                back_end,
            )
        )

    grads = (r.up_cut, r.up_grad, r.out_grad, r.qkv_grad)
    for index, (_, _, crosses, parts) in enumerate(WEIGHTS):
        for start_column, width, y_first in parts:
            weight(index, len(stages), crosses, (start_column, width), y_first, grads[index])

    def run(*codes):
        for code in codes:
            stages[code // 10][code % 10]()

    rest = []
    for item in finals:
        if item.func in (share_across, share_near) and item.args[0] is r.up_cut:
            item().wait_send()
        else:
            rest.append(item)
    finals[:] = rest

    def cut_product(target, left, right, width):
        for part in range(2):
            product = dot(
                left[:, :, part * HALF : (part + 1) * HALF].reshape(2 * length, HALF),
                right[...].reshape(2 * length, width),
                0,
                0,
            )
            for half in range(2):
                target[2 * part + half, :, 0:width] = product[
                    half * SLICE : (half + 1) * SLICE
                ].astype(BRAIN)

    steps = iter(PLAN)

    def plan():
        run(*next(steps))

    cut_product(r.up_cut, r.active, r.cotangent, D)
    run(40, 0, 10, 20, 30)
    plan()
    both(feed_back, 1)
    sum_on(0, ID_SUM_TWO, 1)
    cut_product(r.up_grad, r.hidden_two, r.lifted_grad, D)
    run(90, 50, 60, 70, 80)
    plan()

    for clip in (0, 1):
        grad_two = sum_end(0, ID_SUM_TWO, clip)
        normal, scale = normalize(r.middle_own[clip])
        r.columns[2:3, :] += row_sum(grad_two * normal)
        r.columns[3:4, :] += row_sum(grad_two)
        total = to_single(r.cotangent[clip, own, :]) + norm_back(
            grad_two, normal, scale, whole(G2)
        )
        r.input_grad_out[clip] = total
        r.gradient[clip, own, :] = total.astype(BRAIN)
        gather_start(r.gradient, ID_GRADIENT, clip)
        plan()

    def lower(clip, kind, carry):
        value = dot(r.active[clip, rows_of(kind), :], r.down_own[...], 1, 0)
        sum_step(1, ID_SUM_RESULT, clip, kind, value)
        return carry

    for clip in (0, 1):
        both(lower, clip)
        plan()

    def back_out(clip):
        gather_near(r.gradient, ID_GRADIENT, clip).wait_recv()
        gather_on(r.gradient, ID_GRADIENT, clip).wait_recv()
        grad = r.gradient[clip]
        r.columns[4:5, :] += row_sum(to_single(grad))
        r.mixed_grad[clip] = dot(grad, r.out_all[at(shard, SLICE), :], 1, 1).astype(BRAIN)

    def attend_back(clip, head):
        query = head_of(r.pairs, clip, head * HD)
        key = head_of(r.pairs, clip, SLICE + head * HD)
        value = head_of(r.pairs, clip, 2 * SLICE + head * HD)
        grad = head_of(r.mixed_grad, clip, head * HD)
        softened = r.soft[clip * LOCAL_HEADS + head]
        grad_soft = dot(value, grad, 1, 1)
        inner = row_sum(grad_soft * softened)
        grad_scores = (softened * (grad_soft - inner)).astype(BRAIN)
        entries = (
            (dot(key.T, grad_scores, 1, 0).T * HD**-0.5).astype(BRAIN),
            dot(grad_scores, query, 1, 0).astype(BRAIN),
            dot(softened.astype(BRAIN), grad, 1, 0).astype(BRAIN),
        )
        for part, entry in enumerate(entries):
            left = part * SLICE + head * HD
            r.pairs_grad[clip, :, left : left + HD] = entry

    for clip in (0, 1):
        gather_forward(r.gradient, ID_GRADIENT, clip)
        plan()
        back_out(clip)
        plan()
        if clip == 1:
            for other in (0, 1):
                sum_on(1, ID_SUM_RESULT, other)
        for head in range(LOCAL_HEADS):
            attend_back(clip, head)
            plan()
    product = None
    for clip in (0, 1):
        heads = jnp.concatenate(
            [r.mixed[shard, 2 * clip], r.mixed[shard, 1, :, clip * HD : (clip + 1) * HD]], 1
        )
        term = dot(heads, r.gradient[clip], 0, 0)
        product = term if product is None else product + term
    r.out_grad[0] = product.astype(BRAIN)
    run(100)
    plan()
    cut_product(r.qkv_grad, r.hidden_one, r.pairs_grad, QKV)
    r.qkv_grad[:, :, QKV:] = jnp.zeros((GROUP, SLICE, HD), BRAIN)
    run(110, 120, 130, 140, 150)
    plan()

    def back_project(clip, kind, carry):
        grad = r.pairs_grad[clip, rows_of(kind), :]
        r.columns[5:6, 0:QKV] += row_sum(to_single(grad))
        sum_step(0, ID_SUM_ONE, clip, kind, dot(grad, r.qkv_own[...], 1, 1))
        return carry

    for clip in (0, 1):
        both(back_project, clip)
        plan()
    for clip in (0, 1):
        sum_on(0, ID_SUM_ONE, clip)
    plan()
    for clip in (0, 1):
        live = 1.0 if clip == 0 else second_live
        result = r.middle_own[clip] + sum_end(1, ID_SUM_RESULT, clip) + whole(C2)
        r.result_out[clip] = (result * live).astype(BRAIN)
    plan()
    for clip in (0, 1):
        grad_one = sum_end(0, ID_SUM_ONE, clip)
        normal, scale = normalize(to_single(r.tokens[clip, own, :]))
        r.columns[6:7, :] += row_sum(grad_one * normal)
        r.columns[7:8, :] += row_sum(grad_one)
        r.input_grad_out[clip] += norm_back(grad_one, normal, scale, whole(G1))

    for member in range(GROUP):
        cols = slice(member * SLICE, (member + 1) * SLICE)
        for place, row in enumerate((6, 7, 2, 3, 4, 0)):
            r.small_sent[member, place : place + 1, :] = r.columns[row : row + 1, cols]

    def small_copy(step):
        return remote(
            r.small_sent.at[mate(step)],
            r.small_near.at[step - 1],
            ID_SMALL + step - 1,
            shard=mate(step),
        )

    for step in (1, 2, 3):
        push(small_copy, step)
    plan()
    for step in (1, 2, 3):
        small_copy(step).wait_recv()
    summed = r.small_sent[shard, 0:4, :]
    for step in (1, 2, 3):
        summed += r.small_near[step - 1, 0:4, :]
    r.small_all[replica, G1 : G1 + 2, :] = summed[0:2]
    r.small_all[replica, G2 : G2 + 2, :] = summed[2:4]
    r.small_all[replica, BO : BO + 1, :] = r.small_sent[shard, 4:5, :]
    r.small_all[replica, C2 : C2 + 1, :] = r.small_sent[shard, 5:6, :]
    r.small_all[replica, BQ : BQ + 1, :] = r.columns[5:6, 0:SLICE]
    r.small_all[replica, BV : BV + 1, :] = r.columns[5:6, 2 * SLICE : QKV]
    for part in range(GROUP):
        r.small_all[replica, C1 + part : C1 + part + 1, :] = r.columns[
            1:2, part * SLICE : (part + 1) * SLICE
        ]
    r.small_all[replica, C1 + GROUP :, :] = jnp.zeros((VECTOR_ROWS - C1 - GROUP, SLICE), SINGLE)

    def spread_copy(step):
        return pltpu.make_async_remote_copy(
            src_ref=r.small_all.at[replica],
            dst_ref=r.small_all.at[replica],
            send_sem=r.send_all.at[0, step],
            recv_sem=r.recv_all.at[0, step],
            device_id={"replica": (replica + step) % replicas},
            device_id_type=MESH,
        )

    def spread_start(step, carry):
        spread_copy(step).start()
        return carry

    lax.fori_loop(1, replicas, spread_start, 0)
    plan()

    def spread_wait(step, carry):
        spread_copy(step).wait()
        return carry

    lax.fori_loop(1, replicas, spread_wait, 0)
    small_sum = r.small_all[0]
    for step in range(1, replicas):
        small_sum += r.small_all[step]
    r.small_out[...] = small_sum
    for item in finals:
        item().wait_send()
    for condition, item in conditional:
        if condition is None:
            item().wait_send()
        else:

            @pl.when(condition)
            def _():
                item().wait_send()

    run(106)
    run(6, 16, 26, 36, 46)
    run(116, 126, 136, 146, 156)
    run(56, 66, 76, 86, 96)


def finish(fields, *refs):
    r = gathered(fields, refs)
    units = []

    def unit(wide, target, widen):
        units.append((pltpu.make_async_copy(wide, target, r.near.at[len(units)]), widen))

    def keep():
        pass

    def down(index):
        rows = slice(index * SLICE, (index + 1) * SLICE)

        def widen():
            r.wide[DOWN][rows, :] = to_single(r.narrow[DOWN][index])

        unit(r.wide[DOWN].at[rows], r.results[DOWN].at[rows], widen)

    def up(index):
        rows = slice(index * PIECE, (index + 1) * PIECE)

        def widen():
            for member in range(GROUP):
                r.wide[UP][rows, member * D : (member + 1) * D] = to_single(
                    r.narrow[UP][member, rows, :]
                )

        unit(r.wide[UP].at[rows], r.results[UP].at[rows], widen)

    def qkv(index):
        rows = slice(index * PIECE, (index + 1) * PIECE)

        def widen():
            for part in range(3):
                cols = slice(part * SLICE, (part + 1) * SLICE)
                r.wide[QKVS][rows, part * D : (part + 1) * D] = to_single(
                    jnp.concatenate(
                        [r.narrow[QKVS][member, rows, cols] for member in range(GROUP)], 1
                    )
                )

        unit(r.wide[QKVS].at[rows], r.results[QKVS].at[rows], widen)

    def out():
        def widen():
            r.wide[OUT][...] = to_single(r.narrow[OUT][0])

        unit(r.wide[OUT], r.results[OUT], widen)

    unit(r.input_grad_in, r.input_grad, keep)
    unit(r.result_in, r.result, keep)
    for index in range(GROUP):
        down(index)
        up(index)
    out()
    for index in range(GROUP):
        qkv(index)
    for row in range(8):
        r.vectors[row][...] = r.small_in[row : row + 1, :].reshape(SLICE)
    r.vectors[8][...] = jnp.concatenate(
        [r.small_in[C1 + part : C1 + part + 1, :] for part in range(GROUP)], 1
    ).reshape(D)
    for store, widen in units:
        widen()
        store.start()
    for store, _ in units:
        store.wait()


def layer(replicas, *arguments):
    (
        tokens, cotangent, clip_count, ln1_gain, ln1_bias, qkv_weight, q_bias, v_bias,
        out_weight, out_bias, ln2_gain, ln2_bias, fc1_weight, fc1_bias, fc2_weight, fc2_bias,
    ) = arguments
    slots, slot, _ = tokens.shape
    length = slot * GROUP
    levels = (replicas // 8).bit_length() - 1
    vectors = (
        ln1_gain, ln1_bias, out_bias, ln2_gain, ln2_bias, fc2_bias, q_bias, v_bias, fc1_bias,
    )
    anywhere = pl.BlockSpec(memory_space=pl.ANY)
    in_memory = pl.BlockSpec(memory_space=pltpu.VMEM)
    shape = jax.ShapeDtypeStruct

    inputs = dict(
        tokens_in=anywhere,
        cotangent_in=anywhere,
        count_in=pl.BlockSpec(memory_space=pltpu.SMEM),
        vectors_in=[anywhere] * 9,
        qkv_in=anywhere,
        out_in=anywhere,
        up_in=anywhere,
        down_in=anywhere,
    )
    outputs = dict(
        result_out=pltpu.VMEM(tokens.shape, BRAIN),
        input_grad_out=pltpu.VMEM(tokens.shape, SINGLE),
        small_out=pltpu.VMEM((VECTOR_ROWS, SLICE), SINGLE),
        fulls=[pltpu.VMEM((blocks, SLICE, columns), BRAIN) for blocks, columns, _, _ in WEIGHTS],
    )
    scratch = dict(
        qkv_wide=pltpu.VMEM(qkv_weight.shape, SINGLE),
        out_wide=pltpu.VMEM(out_weight.shape, SINGLE),
        up_wide=pltpu.VMEM(fc1_weight.shape, SINGLE),
        down_wide=pltpu.VMEM(fc2_weight.shape, SINGLE),
        qkv_cut=pltpu.VMEM((GROUP, SLICE, QKV), BRAIN),
        up_cut=pltpu.VMEM((GROUP, SLICE, D), BRAIN),
        qkv_own=pltpu.VMEM((D, QKV), BRAIN),
        up_own=pltpu.VMEM((D, D), BRAIN),
        out_all=pltpu.VMEM((D, D), BRAIN),
        down_own=pltpu.VMEM((D, D), BRAIN),
        vectors=pltpu.VMEM((GROUP, VECTOR_ROWS, SLICE), SINGLE),
        vectors_raw=[pltpu.VMEM(vector.shape, SINGLE) for vector in vectors],
        tokens=pltpu.VMEM((2, length, D), BRAIN),
        cotangent=pltpu.VMEM((2, length, D), BRAIN),
        hidden_one=pltpu.VMEM((2, length, D), BRAIN),
        pairs=pltpu.VMEM((2, length, QKV), BRAIN),
        soft=pltpu.VMEM((2 * LOCAL_HEADS, length, length), SINGLE),
        mixed=pltpu.VMEM((GROUP, 3, length, TILE), BRAIN),
        middle_own=pltpu.VMEM((2, slot, D), SINGLE),
        hidden_two=pltpu.VMEM((2, length, D), BRAIN),
        active=pltpu.VMEM((2, length, D), BRAIN),
        lifted_grad=pltpu.VMEM((2, length, D), BRAIN),
        gradient=pltpu.VMEM((2, length, D), BRAIN),
        mixed_grad=pltpu.VMEM((2, length, SLICE), BRAIN),
        pairs_grad=pltpu.VMEM((2, length, QKV), BRAIN),
        stage=pltpu.VMEM((2 * slot, D), SINGLE),
        sum_sent=pltpu.VMEM((2, 2, 3, slot, D), BRAIN),
        sum_near=pltpu.VMEM((2, 2, 2, slot, D), BRAIN),
        sum_far=pltpu.VMEM((2, 2, slot, D), BRAIN),
        sum_own=pltpu.VMEM((2, 2, slot, D), SINGLE),
        up_grad=pltpu.VMEM((GROUP, SLICE, D), BRAIN),
        out_grad=pltpu.VMEM((1, SLICE, D), BRAIN),
        qkv_grad=pltpu.VMEM((GROUP, SLICE, QKV + HD), BRAIN),
        columns=pltpu.VMEM((8, D), SINGLE),
        small_sent=pltpu.VMEM((GROUP, 8, SLICE), SINGLE),
        small_near=pltpu.VMEM((GROUP - 1, 8, SLICE), SINGLE),
        small_all=pltpu.VMEM((replicas, VECTOR_ROWS, SLICE), SINGLE),
        halves=[pltpu.VMEM((w[0], PAIR, w[1]), BRAIN) for w in WEIGHTS],
        lines=[pltpu.VMEM((w[0], PAIR, w[1]), BRAIN) for w in WEIGHTS],
        middles=[pltpu.VMEM((w[0], PAIR, w[1]), BRAIN) for w in WEIGHTS],
        crossed=[pltpu.VMEM((GROUP, PAIR, w[1]), BRAIN) for w in WEIGHTS if w[2]],
        extras=[
            pltpu.VMEM((levels, w[0], PAIR, w[1]) if levels else (1, 1, 16, TILE), BRAIN)
            for w in WEIGHTS
        ],
        send=pltpu.SemaphoreType.DMA((COPIES,)),
        recv=pltpu.SemaphoreType.DMA((COPIES,)),
        send_all=pltpu.SemaphoreType.DMA((1 + ITEMS, replicas)),
        recv_all=pltpu.SemaphoreType.DMA((1 + ITEMS, replicas)),
        near=pltpu.SemaphoreType.DMA((LOCALS,)),
    )
    sums = pl.pallas_call(
        functools.partial(kernel, replicas, counted(inputs) + counted(outputs) + counted(scratch)),
        out_shape=tuple(flat(outputs)),
        in_specs=flat(inputs),
        out_specs=(in_memory,) * len(flat(outputs)),
        scratch_shapes=flat(scratch),
        compiler_params=pltpu.CompilerParams(
            collective_id=0, has_side_effects=True, vmem_limit_bytes=60600 * 1024
        ),
        name="layer",
    )(
        tokens, cotangent, clip_count, *vectors, qkv_weight, out_weight, fc1_weight, fc2_weight
    )

    matrices = [fc2_weight, fc1_weight, out_weight, qkv_weight]
    last_inputs = dict(
        result_in=in_memory, input_grad_in=in_memory, small_in=in_memory, narrow=[in_memory] * 4
    )
    last_outputs = dict(
        result=shape(tokens.shape, BRAIN),
        input_grad=shape(tokens.shape, SINGLE),
        results=[shape(array.shape, SINGLE) for array in matrices],
        vectors=[shape(vector.shape, SINGLE) for vector in vectors],
    )
    last_scratch = dict(
        wide=[pltpu.VMEM(array.shape, SINGLE) for array in matrices],
        near=pltpu.SemaphoreType.DMA((16,)),
    )
    values = pl.pallas_call(
        functools.partial(
            finish, counted(last_inputs) + counted(last_outputs) + counted(last_scratch)
        ),
        out_shape=tuple(flat(last_outputs)),
        in_specs=flat(last_inputs),
        out_specs=(anywhere,) * 6 + (in_memory,) * 9,
        scratch_shapes=flat(last_scratch),
        compiler_params=pltpu.CompilerParams(vmem_limit_bytes=32 << 20),
        name="finish",
    )(*sums)
    o = gathered(counted(last_outputs), values)
    return (
        o.result,
        o.input_grad,
        o.vectors[G1],
        o.vectors[B1],
        o.results[QKVS],
        o.vectors[BQ],
        o.vectors[BV],
        o.results[OUT],
        o.vectors[BO],
        o.vectors[G2],
        o.vectors[B2],
        o.results[UP],
        o.vectors[C1],
        o.results[DOWN],
        o.vectors[C2],
    )


def solution(mesh):
    token, vector, matrix = P("replica", "shard", None), P("shard"), P("shard", None)
    return jax.shard_map(
        functools.partial(layer, mesh.shape["replica"]),
        mesh=mesh,
        in_specs=(
            token, token, P("replica"), vector, vector, matrix, vector, vector,
            matrix, vector, vector, vector, matrix, vector, matrix, vector,
        ),
        out_specs=(
            token, token, vector, vector, matrix, vector, vector, matrix,
            vector, vector, vector, matrix, vector, matrix, vector,
        ),
        check_vma=False,
    )
```

```python
import functools
import types

import jax
import jax.numpy as jnp
from jax import lax
from jax.experimental import pallas as pl
from jax.experimental.pallas import tpu as pltpu
from jax.sharding import PartitionSpec as P

D = 768
HD = 64
EPSILON = 1e-06
GROUP = 4
SLICE = D // GROUP
LOCAL_HEADS = SLICE // HD
HALF = D // 2
TILE = 128
PAIR = SLICE // 2
PIECE = SLICE // 4
QKV = 3 * SLICE
BRAIN = jnp.bfloat16
SINGLE = jnp.float32
MESH = pl.DeviceIdType.MESH

G1, B1, BO, G2, B2, C2, BQ, BV, C1 = range(9)
VECTOR_ROWS = 16

WEIGHTS = (
    (GROUP, D, False, ((0, 128, True), (128, 128, True), (256, 128, True), (384, 128, True), (512, 256, False))),
    (GROUP, D, True, ((0, 128, True), (128, 128, True), (256, 128, True), (384, 128, True), (512, 256, False))),
    (1, D, False, ((0, 768, False),)),
    (GROUP, 512, True, ((0, 128, True), (128, 128, True), (256, 128, True), (384, 128, True))),
    (2, 128, True, ((0, 128, True),)),
)
DOWN, UP, OUT, QKVS, TAIL = range(5)
TAIL_LEFT = 512
ITEMS = sum(len(parts) for _, _, _, parts in WEIGHTS)

MIXES = (((0, 0), (0, 1)), ((0, 2), (1, 2)), ((1, 0), (1, 1)))


PLAN = (
    (),
    (),
    (1, 41, 11, 21),
    (),
    (91, 31),
    (2, 51),
    (12, 61),
    (),
    (22, 3, 4),
    (32, 13, 14),
    (),
    (52, 23, 24, 71),
    (81, 33, 62),
    (42, 72, 53),
    (5, 34, 82),
    (),
    (15, 92, 63),
    (25,),
    (),
    (73, 35, 43, 44, 111, 83, 101),
    (),
    (74, 121, 84, 131, 93, 141, 75, 64, 54, 112, 151, 85, 122, 45, 65, 113, 132, 102),
    (55, 123, 142, 114, 133, 152),
    (124, 94, 115, 134, 125, 143, 103, 104, 153, 144, 135, 154, 95, 145, 105, 155),
)


class Names:
    def __init__(self):
        self.total = 0

    def take(self, count):
        first = self.total
        self.total += count
        return first


ids = Names()
ID_TOKENS = ids.take(6)
ID_COTANGENT = ids.take(12)
ID_GRADIENT = ids.take(6)
ID_VECTORS = ids.take(3)
ID_QKV = ids.take(9)
ID_OUT = ids.take(9)
ID_UP = ids.take(9)
ID_MIX = ids.take(9)
ID_SUM_TWO = ids.take(6)
ID_SUM_RESULT = ids.take(6)
ID_SUM_ONE = ids.take(6)
ID_SMALL = ids.take(3)
ID_WEIGHTS = ids.take(9 * ITEMS)
COPIES = ids.total
LOCALS = 32


def to_single(value):
    return value.astype(SINGLE)


def rounded(value):
    return value.astype(BRAIN).astype(SINGLE)


def dot(left, right, left_dim, right_dim):
    return lax.dot_general(
        left, right, (((left_dim,), (right_dim,)), ((), ())), preferred_element_type=SINGLE
    )


def normalize(value):
    mean = jnp.sum(value, axis=-1, keepdims=True) * (1.0 / D)
    centred = value - mean
    spread = jnp.sum(centred * centred, axis=-1, keepdims=True) * (1.0 / D)
    scale = lax.rsqrt(spread + EPSILON)
    return centred * scale, scale


def norm_back(grad, normal, scale, gain):
    scaled = grad * gain
    first = jnp.sum(scaled, axis=-1, keepdims=True) * (1.0 / D)
    second = jnp.sum(scaled * normal, axis=-1, keepdims=True) * (1.0 / D)
    return scale * (scaled - first - normal * second)


def row_sum(value):
    return jnp.sum(value, axis=0, keepdims=True)


def gathered(fields, refs):
    result, refs = {}, list(refs)
    for name, count in fields:
        result[name] = [refs.pop(0) for _ in range(count)] if count > 1 else refs.pop(0)
    return types.SimpleNamespace(**result)


def counted(fields):
    return [(name, len(entry) if isinstance(entry, list) else 1) for name, entry in fields.items()]


def flat(fields):
    result = []
    for entry in fields.values():
        result += entry if isinstance(entry, list) else [entry]
    return result


def kernel(replicas, fields, *refs):
    r = gathered(fields, refs)
    levels = (replicas // 8).bit_length() - 1
    slot = r.tokens_in.shape[1]
    pair = 2 * slot
    length = GROUP * slot

    shard = lax.axis_index("shard")
    replica = lax.axis_index("replica")
    chip = shard // 2
    core = shard % 2
    y = replica % 2
    z_low = (replica // 2) % 2
    z_high = (replica // 4) % 2
    inner = (z_low + z_high) % 2 == 1
    edge = (z_low + z_high) % 2 == 0
    block_of_eight = replica // 8
    y_peer = replica + 1 - 2 * y
    z_pair = replica + 2 * (1 - 2 * z_low)

    def mate(step):
        return 2 * ((chip + step // 2) % 2) + (shard + step) % 2

    finals, conditional = [], []

    def remote(source, target, index, **where):
        return pltpu.make_async_remote_copy(
            src_ref=source,
            dst_ref=target,
            send_sem=r.send.at[index],
            recv_sem=r.recv.at[index],
            device_id=where,
            device_id_type=MESH,
        )

    def push(make, *arguments):
        make(*arguments).start()
        finals.append(functools.partial(make, *arguments))

    def push_if(condition, make, *arguments):
        @pl.when(condition)
        def _():
            make(*arguments).start()

        conditional.append((condition, functools.partial(make, *arguments)))

    def local(source, target, index):
        return pltpu.make_async_copy(source, target, r.near.at[index])

    def at(index, size, offset=0):
        return pl.ds(pl.multiple_of(index * size + offset, size), size)

    def here(ref, clip):
        return ref.at[clip, at(shard, slot), :]

    def quarter_rows(step):
        return at((2 * y + z_low + step) % 4, PIECE)

    qkv_loads = [
        local(r.qkv_in.at[quarter_rows(step)], r.qkv_wide.at[quarter_rows(step)], 25 + step)
        for step in range(4)
    ]
    token_loads = [local(r.tokens_in.at[clip], here(r.tokens, clip), 1 + clip) for clip in (0, 1)]
    vector_loads = [
        local(r.vectors_in[row], r.vectors_raw[row], 3 + row)
        for row in range(9)
    ]
    cotangent_loads = [
        local(r.cotangent_in.at[clip], here(r.cotangent, clip), 12 + clip) for clip in (0, 1)
    ]
    wide_loads = [
        local(r.up_in, r.up_wide, 14),
        local(r.out_in, r.out_wide, 15),
        local(r.down_in, r.down_wide, 16),
    ]
    for load in qkv_loads + token_loads + vector_loads + cotangent_loads + wide_loads:
        load.start()
    barrier = pltpu.get_barrier_semaphore()
    for step in (1, 2, 3):
        pl.semaphore_signal(barrier, inc=1, device_id={"shard": mate(step)}, device_id_type=MESH)

    def greet(step, carry):
        peer = (replica + step) % replicas
        pl.semaphore_signal(barrier, inc=1, device_id={"replica": peer}, device_id_type=MESH)
        return carry

    lax.fori_loop(1, replicas, greet, 0)

    def cut_rows(step):
        qkv_loads[step].wait()
        rows = quarter_rows(step)
        for member in range(GROUP):
            left = member * SLICE
            r.qkv_cut[member, rows, :] = jnp.concatenate(
                [
                    r.qkv_wide[rows, part * D + left : part * D + left + SLICE].astype(BRAIN)
                    for part in range(3)
                ],
                axis=1,
            )

    cut_rows(0)
    for load in token_loads + vector_loads:
        load.wait()
    pl.semaphore_wait(barrier, replicas + 2)

    def gather_part(buffer, clip, member):
        if clip >= 2:
            return buffer.at[0, at(2 * member + clip - 2, slot // 2), :]
        return buffer.at[clip, at(member, slot), :]

    def gather_near(buffer, base, clip):
        part = gather_part(buffer, clip, shard)
        return remote(part, part, base + 3 * clip, shard=mate(1))

    def gather_across(buffer, base, clip):
        part = gather_part(buffer, clip, shard)
        return remote(part, part, base + 3 * clip + 1, shard=mate(2))

    def gather_on(buffer, base, clip):
        part = gather_part(buffer, clip, mate(2))
        return remote(part, part, base + 3 * clip + 2, shard=mate(1))

    def gather_start(buffer, base, clip):
        push(gather_across, buffer, base, clip)
        push(gather_near, buffer, base, clip)

    def gather_forward(buffer, base, clip):
        gather_across(buffer, base, clip).wait_recv()
        push(gather_on, buffer, base, clip)

    def quarter(member, y_side, z_side):
        return at((member * 2 + y_side) * 2 + z_side, PIECE)

    def share_across(cut, buffer, base, step):
        source = buffer.at[quarter(shard, y, z_low), :]
        if cut is not None:
            source = cut.at[mate(step), at(2 * y + z_low, PIECE), :]
        return remote(
            source, buffer.at[quarter(shard, y, z_low), :], base + step - 2, shard=mate(step)
        )

    def share_z(buffer, base, step):
        part = buffer.at[quarter(mate(step), y, z_low), :]
        return remote(part, part, base + step, replica=z_pair)

    def share_y(buffer, base, step, second):
        side = 1 - z_low if second else z_low
        part = buffer.at[quarter(mate(step), y, side), :]
        return remote(part, part, base + 2 * second + 2 + step, replica=y_peer)

    def share_near(cut, buffer, base):
        target = buffer.at[at(shard, SLICE), :]
        source = target if cut is None else cut.at[mate(1)]
        return remote(source, target, base + 8, shard=mate(1))

    def share_first(cut, buffer, base, steps):
        for step in steps:
            push(share_across, cut, buffer, base, step)

    def share_start(cut, buffer, base, steps):
        share_first(cut, buffer, base, steps)
        push(share_near, cut, buffer, base)

    def share_on(cut, buffer, base, steps):
        for step in steps:
            share_across(cut, buffer, base, step).wait_recv()
            push(share_z, buffer, base, step)
            push(share_y, buffer, base, step, 0)

    def share_last(buffer, base, steps):
        for step in steps:
            share_z(buffer, base, step).wait_recv()
            push(share_y, buffer, base, step, 1)

    def share_wait(cut, buffer, base, steps):
        for step in steps:
            share_y(buffer, base, step, 0).wait_recv()
            share_y(buffer, base, step, 1).wait_recv()
        share_near(cut, buffer, base).wait_recv()

    BOTH, ONE = (2, 3), (2,)
    FIRST, SECOND = 2, 3

    share_first(r.qkv_cut, r.qkv_own, ID_QKV, BOTH)
    gather_start(r.tokens, ID_TOKENS, 0)
    for row in range(8):
        r.vectors[shard, row : row + 1, :] = rounded(
            r.vectors_raw[row][...].reshape(1, SLICE)
        )
    long_row = rounded(r.vectors_raw[8][...].reshape(1, D))
    for part in range(GROUP):
        r.vectors[shard, C1 + part : C1 + part + 1, :] = long_row[
            :, part * SLICE : (part + 1) * SLICE
        ]
    r.vectors[shard, C1 + GROUP :, :] = jnp.zeros((VECTOR_ROWS - C1 - GROUP, SLICE), SINGLE)

    def send_vectors(step):
        return remote(
            r.vectors.at[shard], r.vectors.at[shard], ID_VECTORS + step - 1, shard=mate(step)
        )

    for step in (1, 2, 3):
        push(send_vectors, step)
    for load in wide_loads:
        load.wait()
    for member in range(GROUP):
        r.up_cut[member] = r.up_wide[:, member * D : (member + 1) * D].astype(BRAIN)
    r.out_all[at(shard, SLICE), :] = r.out_wide[...].astype(BRAIN)
    share_start(None, r.out_all, ID_OUT, ONE)
    share_start(r.up_cut, r.up_own, ID_UP, BOTH)
    gather_start(r.tokens, ID_TOKENS, 1)

    for step in (1, 2, 3):
        cut_rows(step)
    push(share_near, r.qkv_cut, r.qkv_own, ID_QKV)
    r.qkv_own[at(shard, SLICE), :] = r.qkv_cut[shard]
    share_on(r.qkv_cut, r.qkv_own, ID_QKV, BOTH)
    for load in cotangent_loads:
        load.wait()
    second_live = to_single(jnp.minimum(r.count_in[0] - 1, 1))
    own = at(shard, slot)
    r.cotangent[1, own, :] = (to_single(r.cotangent[1, own, :]) * second_live).astype(BRAIN)
    r.up_own[at(shard, SLICE), :] = r.up_cut[shard]
    r.down_own[...] = r.down_wide[...].astype(BRAIN)
    r.columns[...] = jnp.zeros_like(r.columns)
    share_last(r.qkv_own, ID_QKV, BOTH)
    gather_forward(r.tokens, ID_TOKENS, 0)

    def whole(row):
        return jnp.concatenate([r.vectors[member, row : row + 1, :] for member in range(GROUP)], 1)

    def mine(row):
        return r.vectors[shard, row : row + 1, :]

    for step in (1, 2, 3):
        send_vectors(step).wait_recv()
    share_wait(r.qkv_cut, r.qkv_own, ID_QKV, BOTH)
    scale_row = jnp.where(lax.broadcasted_iota(jnp.int32, (1, QKV), 1) < SLICE, HD**-0.5, 1.0)
    qkv_bias = jnp.concatenate([mine(BQ), jnp.zeros((1, SLICE), SINGLE), mine(BV)], 1)

    def project(clip, side):
        rows = at((chip + side) % 2, pair)
        normal, _ = normalize(to_single(r.tokens[clip, rows, :]))
        hidden = (normal * whole(G1) + whole(B1)).astype(BRAIN)
        r.hidden_one[clip, rows, :] = hidden
        product = (dot(hidden, r.qkv_own[...], 1, 0) + qkv_bias) * scale_row
        r.pairs[clip, rows, :] = product.astype(BRAIN)

    def mix_near(part):
        ref = r.mixed.at[shard, part]
        return remote(ref, ref, ID_MIX + 3 * part, shard=mate(1))

    def mix_across(part):
        ref = r.mixed.at[shard, part]
        return remote(ref, ref, ID_MIX + 3 * part + 1, shard=mate(2))

    def mix_on(part):
        ref = r.mixed.at[mate(2), part]
        return remote(ref, ref, ID_MIX + 3 * part + 2, shard=mate(1))

    def mix_forward(part):
        mix_across(part).wait_recv()
        push(mix_on, part)

    def head_of(ref, clip, left):
        return ref[clip, :, left : left + HD]

    def attend(part, place):
        clip, head = MIXES[part][place]
        query = head_of(r.pairs, clip, head * HD)
        key = head_of(r.pairs, clip, SLICE + head * HD)
        value = head_of(r.pairs, clip, 2 * SLICE + head * HD)
        scores = dot(key, query, 1, 1)
        highest = jnp.max(scores, axis=0, keepdims=True)
        expanded = jnp.exp(scores - highest)
        softened = expanded * (1.0 / row_sum(expanded))
        r.soft[clip * LOCAL_HEADS + head] = softened
        mixture = dot(value.T, softened.astype(BRAIN), 1, 0).T.astype(BRAIN)
        r.mixed[shard, part, :, place * HD : (place + 1) * HD] = mixture

    def mix_start(part):
        push(mix_across, part)
        push(mix_near, part)

    gather_near(r.tokens, ID_TOKENS, 0).wait_recv()
    project(0, 0)
    gather_on(r.tokens, ID_TOKENS, 0).wait_recv()
    project(0, 1)
    attend(0, 0)
    share_on(None, r.out_all, ID_OUT, ONE)
    share_on(r.up_cut, r.up_own, ID_UP, BOTH)
    attend(0, 1)
    mix_start(0)
    gather_start(r.cotangent, ID_COTANGENT, FIRST)
    attend(1, 0)
    gather_near(r.tokens, ID_TOKENS, 1).wait_recv()
    project(1, 0)
    gather_forward(r.tokens, ID_TOKENS, 1)
    gather_on(r.tokens, ID_TOKENS, 1).wait_recv()
    project(1, 1)
    attend(1, 1)
    mix_start(1)
    gather_start(r.cotangent, ID_COTANGENT, SECOND)
    share_last(r.out_all, ID_OUT, ONE)
    share_last(r.up_own, ID_UP, BOTH)
    mix_forward(0)
    attend(2, 0)
    attend(2, 1)
    mix_start(2)
    gather_start(r.cotangent, ID_COTANGENT, 1)

    def out_on():
        part = r.out_all.at[at(mate(2), SLICE), :]
        return remote(part, part, ID_OUT + 1, shard=mate(1))

    share_wait(None, r.out_all, ID_OUT, ONE)
    push(out_on)
    mix_forward(1)
    out_on().wait_recv()
    for part in (0, 1):
        mix_near(part).wait_recv()
        mix_on(part).wait_recv()
    share_wait(r.up_cut, r.up_own, ID_UP, BOTH)

    def sum_near(which, base, clip, kind):
        return remote(
            r.sum_sent.at[which, clip, kind],
            r.sum_near.at[which, clip, kind],
            base + 3 * clip + kind,
            shard=mate(1),
        )

    def sum_far(which, base, clip):
        return remote(
            r.sum_sent.at[which, clip, 2],
            r.sum_far.at[which, clip],
            base + 3 * clip + 2,
            shard=mate(2),
        )

    def sum_kept(which, clip, kind):
        if which == 0:
            return r.sum_own.at[clip, kind]
        return r.up_wide.at[0:slot, at(2 * clip + kind, D)]

    def sum_step(which, base, clip, kind, value):
        r.stage[...] = value
        r.sum_sent[which, clip, kind] = r.stage[at(1 - core, slot), :].astype(BRAIN)
        sum_kept(which, clip, kind)[...] = r.stage[at(core, slot), :]
        remote(
            r.sum_sent.at[which, clip, kind],
            r.sum_near.at[which, clip, kind],
            base + 3 * clip + kind,
            shard=mate(1),
        ).start()

    def sum_on(which, base, clip):
        sum_near(which, base, clip, 0).wait_recv()
        r.sum_sent[which, clip, 2] = (
            sum_kept(which, clip, 0)[...] + to_single(r.sum_near[which, clip, 0])
        ).astype(BRAIN)
        sum_far(which, base, clip).start()

    def sum_end(which, base, clip):
        sum_near(which, base, clip, 0).wait_send()
        sum_near(which, base, clip, 1).wait()
        sum_far(which, base, clip).wait()
        return (
            sum_kept(which, clip, 1)[...]
            + to_single(r.sum_near[which, clip, 1])
            + to_single(r.sum_far[which, clip])
        )

    def rows_of(kind):
        return at((chip + 1 + kind) % 2, pair)

    long_bias = jnp.concatenate(
        [r.vectors[shard, C1 + part : C1 + part + 1, :] for part in range(GROUP)], 1
    )

    def pass_on(across, on):
        across.wait_recv()
        on.start()

    def feed(clip, kind, carry):
        rows = rows_of(kind)

        @pl.when(kind == 1)
        def _():
            for part in ((FIRST, SECOND), (1,))[clip]:
                pass_on(
                    gather_across(r.cotangent, ID_COTANGENT, part),
                    gather_on(r.cotangent, ID_COTANGENT, part),
                )

        total = to_single(r.tokens[clip, rows, :]) + whole(BO)
        for first in (0, 2):
            heads = jnp.concatenate(
                [r.mixed[member, 2 * clip, rows, :] for member in (first, first + 1)], 1
            )
            weights = jnp.concatenate(
                [
                    r.out_all[member * SLICE : member * SLICE + TILE, :]
                    for member in (first, first + 1)
                ],
                0,
            )
            total += dot(heads, weights, 1, 0)
        heads = jnp.concatenate(
            [r.mixed[member, 1, rows, clip * HD : (clip + 1) * HD] for member in range(GROUP)], 1
        )
        weights = jnp.concatenate(
            [
                r.out_all[member * SLICE + TILE : (member + 1) * SLICE, :]
                for member in range(GROUP)
            ],
            0,
        )
        total += dot(heads, weights, 1, 0)

        @pl.when(kind == 1)
        def _():
            r.stage[...] = total
            r.middle_own[clip] = r.stage[at(core, slot), :]

        normal, _ = normalize(total)
        hidden = (normal * whole(G2) + whole(B2)).astype(BRAIN)
        r.hidden_two[clip, rows, :] = hidden
        lifted = dot(hidden, r.up_own[...], 1, 0) + long_bias
        share = 0.5 + 0.5 * lax.erf(lifted * (0.5**0.5))
        r.active[clip, rows, :] = (lifted * share).astype(BRAIN)
        r.down_wide[at(kind, pair), :] = share + lifted * jnp.exp(lifted * lifted * -0.5) * 0.3989422804014327
        return carry

    def feed_back(clip, kind, carry):
        rows = rows_of(kind)
        if clip == 0:

            @pl.when(kind == 1)
            def _():
                pass_on(mix_across(2), mix_on(2))

        down = r.cotangent[clip, rows, :]
        r.columns[0:1, :] += row_sum(to_single(down))
        grad = (dot(down, r.down_own[...], 1, 1) * r.down_wide[at(kind, pair), :]).astype(BRAIN)
        r.lifted_grad[clip, rows, :] = grad
        r.columns[1:2, :] += row_sum(to_single(grad))
        sum_step(0, ID_SUM_TWO, clip, kind, dot(grad, r.up_own[...], 1, 1))
        return carry

    def both(step, clip):
        lax.fori_loop(0, 2, functools.partial(step, clip), 0)

    both(feed, 0)
    for half in (FIRST, SECOND):
        finals.append(functools.partial(gather_on, r.cotangent, ID_COTANGENT, half))
        gather_near(r.cotangent, ID_COTANGENT, half).wait_recv()
        gather_on(r.cotangent, ID_COTANGENT, half).wait_recv()
    both(feed_back, 0)
    finals.append(functools.partial(mix_on, 2))
    mix_near(2).wait_recv()
    mix_on(2).wait_recv()
    sum_on(0, ID_SUM_TWO, 0)
    both(feed, 1)
    finals.append(functools.partial(gather_on, r.cotangent, ID_COTANGENT, 1))
    gather_near(r.cotangent, ID_COTANGENT, 1).wait_recv()
    gather_on(r.cotangent, ID_COTANGENT, 1).wait_recv()
    stages = []

    def weight(index, number, crosses, columns, y_first, grad):
        base = ID_WEIGHTS + 9 * number
        halves, line, middle, full = (
            refs[index] for refs in (r.halves, r.lines, r.middles, r.fulls)
        )
        crossed = r.crossed[index // 2] if crosses else None
        blocks = grad.shape[0]
        share = full.shape[0] // blocks
        cols = slice(columns[0], columns[0] + columns[1])
        size = PAIR if y_first else PIECE
        first, first_peer, second, second_peer = (
            (y, y_peer, z_low, z_pair) if y_first else (z_low, z_pair, y, y_peer)
        )
        source = (crossed if crosses else line).at[:, 0:size, cols]
        held = slice(0, PAIR) if y_first else at(second, PIECE)

        def final_rows(side):
            return at(first, PAIR) if y_first else at(2 * first + side, PIECE)

        def first_copy():
            return remote(
                grad.at[:, at(1 - first, PAIR), cols],
                halves.at[:, :, cols],
                base,
                replica=first_peer,
            )

        def second_copy():
            given = slice(0, PAIR) if y_first else at(1 - second, PIECE)
            return remote(
                halves.at[:, given, cols],
                line.at[:, 0:size, cols],
                base + 1,
                replica=second_peer,
            )

        def far_copy():
            apart = 2 if y_first else 4
            return remote(
                halves.at[:, held, cols],
                middle.at[:, 0:size, cols],
                base + 2,
                replica=replica + apart * (1 - 2 * z_high),
            )

        def farther_copy(level):
            apart = 8 * 2**level * (1 - 2 * ((block_of_eight // 2**level) % 2))
            return pltpu.make_async_remote_copy(
                src_ref=line.at[:, 0:size, cols],
                dst_ref=r.extras[index].at[level, :, 0:size, cols],
                send_sem=r.send_all.at[number + 1, level],
                recv_sem=r.recv_all.at[number + 1, level],
                device_id={"replica": replica + apart},
                device_id_type=MESH,
            )

        def cross_copy(step):
            return remote(
                line.at[mate(step) // share, 0:size, cols],
                crossed.at[shard, 0:size, cols],
                base + 2 + step,
                shard=mate(step),
            )

        def second_back():
            return remote(
                source, full.at[:, final_rows(second), cols], base + 6, replica=second_peer
            )

        def first_back(late):
            if not late:
                return remote(
                    source, full.at[:, final_rows(second), cols], base + 7, replica=first_peer
                )
            ref = full.at[:, final_rows(1 - second), cols]
            return remote(ref, ref, base + 8 - y_first, replica=first_peer)

        def start():
            push(first_copy)

        def second_start():
            first_copy().wait_recv()
            for block in range(blocks):
                halves[block, :, cols] = (
                    to_single(grad[block, at(first, PAIR), cols])
                    + to_single(halves[block, :, cols])
                ).astype(BRAIN)
            if y_first:
                push_if(edge, second_copy)
            else:
                push(second_copy)

        def far_start():
            second_copy().wait_recv()
            for block in range(blocks):
                halves[block, held, cols] = (
                    to_single(halves[block, held, cols]) + to_single(line[block, 0:size, cols])
                ).astype(BRAIN)
            far_copy().start()

        def cross_start():
            far_copy().wait()
            for block in range(blocks):
                line[block, 0:size, cols] = (
                    to_single(halves[block, held, cols]) + to_single(middle[block, 0:size, cols])
                ).astype(BRAIN)
            for level in range(levels):
                farther_copy(level).start()
                farther_copy(level).wait()
                line[:, 0:size, cols] = (
                    to_single(line[:, 0:size, cols])
                    + to_single(r.extras[index][level, :, 0:size, cols])
                ).astype(BRAIN)
            if crosses:
                crossed[shard, 0:size, cols] = line[shard // share, 0:size, cols]
                for step in (2, 3, 1):
                    cross_copy(step).start()

        def back_start():
            if crosses:
                for step in (1, 2, 3):
                    cross_copy(step).wait()
            second_back().start()
            first_back(False).start()
            for block in range(full.shape[0]):
                full[block, final_rows(second), cols] = source[block]
            conditional.append((inner if y_first else None, second_back))
            conditional.append(
                (inner if y_first else None, functools.partial(first_back, False))
            )

        def back_on():
            second_back().wait_recv()
            push(first_back, True)

        def back_end():
            if not y_first:
                first_back(False).wait_recv()
            first_back(True).wait_recv()

        def only(condition, step):
            def run_if():
                pl.when(condition)(step)

            return run_if if y_first else step

        def edge_on():
            @pl.when(edge)
            def _():
                second_back().wait_recv()

            push_if(edge, first_back, True)

        stages.append(
            (
                start,
                second_start,
                only(inner, far_start),
                only(inner, cross_start),
                only(inner, back_start),
                edge_on if y_first else back_on,
                back_end,
            )
        )

    grads = (r.up_cut, r.up_grad, r.out_grad, r.qkv_grad, r.tail_grad)
    for index, (_, _, crosses, parts) in enumerate(WEIGHTS):
        for start_column, width, y_first in parts:
            weight(index, len(stages), crosses, (start_column, width), y_first, grads[index])

    def run(*codes):
        for code in codes:
            stages[code // 10][code % 10]()

    rest = []
    for item in finals:
        if item.func in (share_across, share_near) and item.args[0] is r.up_cut:
            item().wait_send()
        else:
            rest.append(item)
    finals[:] = rest

    def cut_product(target, left, right, width):
        for part in range(2):
            product = dot(
                left[:, :, part * HALF : (part + 1) * HALF].reshape(2 * length, HALF),
                right[...].reshape(2 * length, width),
                0,
                0,
            )
            kept = min(width, target.shape[2])
            for half in range(2):
                rows = slice(half * SLICE, (half + 1) * SLICE)
                target[2 * part + half] = product[rows, 0:kept].astype(BRAIN)
                if kept < width:
                    r.tail_grad[part, :, half * HD : (half + 1) * HD] = product[
                        rows, kept:width
                    ].astype(BRAIN)

    steps = iter(PLAN)

    def plan():
        run(*next(steps))

    cut_product(r.up_cut, r.active, r.cotangent, D)
    run(40, 0, 10, 20, 30)
    plan()
    both(feed_back, 1)
    sum_on(0, ID_SUM_TWO, 1)
    cut_product(r.up_grad, r.hidden_two, r.lifted_grad, D)
    run(90, 50, 60, 70, 80)
    plan()

    for clip in (0, 1):
        grad_two = sum_end(0, ID_SUM_TWO, clip)
        normal, scale = normalize(r.middle_own[clip])
        r.columns[2:3, :] += row_sum(grad_two * normal)
        r.columns[3:4, :] += row_sum(grad_two)
        total = to_single(r.cotangent[clip, own, :]) + norm_back(
            grad_two, normal, scale, whole(G2)
        )
        r.input_grad_out[clip] = total
        r.gradient[clip, own, :] = total.astype(BRAIN)
        gather_start(r.gradient, ID_GRADIENT, clip)
        plan()

    def lower(clip, kind, carry):
        value = dot(r.active[clip, rows_of(kind), :], r.down_own[...], 1, 0)
        sum_step(1, ID_SUM_RESULT, clip, kind, value)
        return carry

    for clip in (0, 1):
        both(lower, clip)
        plan()

    def back_out(clip):
        gather_near(r.gradient, ID_GRADIENT, clip).wait_recv()
        gather_on(r.gradient, ID_GRADIENT, clip).wait_recv()
        grad = r.gradient[clip]
        r.columns[4:5, :] += row_sum(to_single(grad))
        r.mixed_grad[clip] = dot(grad, r.out_all[at(shard, SLICE), :], 1, 1).astype(BRAIN)

    def attend_back(clip, head):
        query = head_of(r.pairs, clip, head * HD)
        key = head_of(r.pairs, clip, SLICE + head * HD)
        value = head_of(r.pairs, clip, 2 * SLICE + head * HD)
        grad = head_of(r.mixed_grad, clip, head * HD)
        softened = r.soft[clip * LOCAL_HEADS + head]
        grad_soft = dot(value, grad, 1, 1)
        inner = row_sum(grad_soft * softened)
        grad_scores = (softened * (grad_soft - inner)).astype(BRAIN)
        entries = (
            (dot(key.T, grad_scores, 1, 0).T * HD**-0.5).astype(BRAIN),
            dot(grad_scores, query, 1, 0).astype(BRAIN),
            dot(softened.astype(BRAIN), grad, 1, 0).astype(BRAIN),
        )
        for part, entry in enumerate(entries):
            left = part * SLICE + head * HD
            r.pairs_grad[clip, :, left : left + HD] = entry

    for clip in (0, 1):
        gather_forward(r.gradient, ID_GRADIENT, clip)
        plan()
        back_out(clip)
        plan()
        if clip == 1:
            for other in (0, 1):
                sum_on(1, ID_SUM_RESULT, other)
        for head in range(LOCAL_HEADS):
            attend_back(clip, head)
            plan()
    product = None
    for clip in (0, 1):
        heads = jnp.concatenate(
            [r.mixed[shard, 2 * clip], r.mixed[shard, 1, :, clip * HD : (clip + 1) * HD]], 1
        )
        term = dot(heads, r.gradient[clip], 0, 0)
        product = term if product is None else product + term
    r.out_grad[0] = product.astype(BRAIN)
    run(100)
    plan()
    cut_product(r.qkv_grad, r.hidden_one, r.pairs_grad, QKV)
    run(110, 120, 130, 140, 150)
    plan()

    def back_project(clip, kind, carry):
        grad = r.pairs_grad[clip, rows_of(kind), :]
        r.columns[5:6, 0:QKV] += row_sum(to_single(grad))
        sum_step(0, ID_SUM_ONE, clip, kind, dot(grad, r.qkv_own[...], 1, 1))
        return carry

    for clip in (0, 1):
        both(back_project, clip)
        plan()
    for clip in (0, 1):
        sum_on(0, ID_SUM_ONE, clip)
    plan()
    for clip in (0, 1):
        live = 1.0 if clip == 0 else second_live
        result = r.middle_own[clip] + sum_end(1, ID_SUM_RESULT, clip) + whole(C2)
        r.result_out[clip] = (result * live).astype(BRAIN)
    plan()
    for clip in (0, 1):
        grad_one = sum_end(0, ID_SUM_ONE, clip)
        normal, scale = normalize(to_single(r.tokens[clip, own, :]))
        r.columns[6:7, :] += row_sum(grad_one * normal)
        r.columns[7:8, :] += row_sum(grad_one)
        r.input_grad_out[clip] += norm_back(grad_one, normal, scale, whole(G1))

    for member in range(GROUP):
        cols = slice(member * SLICE, (member + 1) * SLICE)
        for place, row in enumerate((6, 7, 2, 3, 4, 0)):
            r.small_sent[member, place : place + 1, :] = r.columns[row : row + 1, cols]

    def small_copy(step):
        return remote(
            r.small_sent.at[mate(step)],
            r.small_near.at[step - 1],
            ID_SMALL + step - 1,
            shard=mate(step),
        )

    for step in (1, 2, 3):
        push(small_copy, step)
    plan()
    for step in (1, 2, 3):
        small_copy(step).wait_recv()
    summed = r.small_sent[shard, 0:4, :]
    for step in (1, 2, 3):
        summed += r.small_near[step - 1, 0:4, :]
    r.small_all[replica, G1 : G1 + 2, :] = summed[0:2]
    r.small_all[replica, G2 : G2 + 2, :] = summed[2:4]
    r.small_all[replica, BO : BO + 1, :] = r.small_sent[shard, 4:5, :]
    r.small_all[replica, C2 : C2 + 1, :] = r.small_sent[shard, 5:6, :]
    r.small_all[replica, BQ : BQ + 1, :] = r.columns[5:6, 0:SLICE]
    r.small_all[replica, BV : BV + 1, :] = r.columns[5:6, 2 * SLICE : QKV]
    for part in range(GROUP):
        r.small_all[replica, C1 + part : C1 + part + 1, :] = r.columns[
            1:2, part * SLICE : (part + 1) * SLICE
        ]
    r.small_all[replica, C1 + GROUP :, :] = jnp.zeros((VECTOR_ROWS - C1 - GROUP, SLICE), SINGLE)

    def spread_copy(step):
        return pltpu.make_async_remote_copy(
            src_ref=r.small_all.at[replica],
            dst_ref=r.small_all.at[replica],
            send_sem=r.send_all.at[0, step],
            recv_sem=r.recv_all.at[0, step],
            device_id={"replica": (replica + step) % replicas},
            device_id_type=MESH,
        )

    def spread_start(step, carry):
        spread_copy(step).start()
        return carry

    lax.fori_loop(1, replicas, spread_start, 0)
    plan()

    def spread_wait(step, carry):
        spread_copy(step).wait()
        return carry

    lax.fori_loop(1, replicas, spread_wait, 0)
    small_sum = r.small_all[0]
    for step in range(1, replicas):
        small_sum += r.small_all[step]
    r.small_out[...] = small_sum
    for item in finals:
        item().wait_send()
    for condition, item in conditional:
        if condition is None:
            item().wait_send()
        else:

            @pl.when(condition)
            def _():
                item().wait_send()

    run(106)
    run(6, 16, 26, 36, 46)
    run(116, 126, 136, 146, 156)
    run(56, 66, 76, 86, 96)


def finish(fields, *refs):
    r = gathered(fields, refs)
    odd = lax.axis_index("shard") % 2 == 1
    units = []

    def unit(wide, target, widen):
        units.append((pltpu.make_async_copy(wide, target, r.near.at[len(units)]), widen))

    def keep():
        pass

    def down(index):
        rows = slice(index * SLICE, (index + 1) * SLICE)

        def widen():
            r.wide[DOWN][rows, :] = to_single(r.narrow[DOWN][index])

        unit(r.wide[DOWN].at[rows], r.results[DOWN].at[rows], widen)

    def up(index):
        rows = slice(index * PIECE, (index + 1) * PIECE)

        def widen():
            for member in range(GROUP):
                r.wide[UP][rows, member * D : (member + 1) * D] = to_single(
                    r.narrow[UP][member, rows, :]
                )

        unit(r.wide[UP].at[rows], r.results[UP].at[rows], widen)

    def qkv(index):
        rows = slice(index * PIECE, (index + 1) * PIECE)

        def widen():
            for part in range(3):
                cols = slice(part * SLICE, min((part + 1) * SLICE, TAIL_LEFT))
                pieces = []
                for member in range(GROUP):
                    pieces.append(to_single(r.narrow[QKVS][member, rows, cols]))
                    if part == 2:
                        last = to_single(r.narrow[TAIL][member, rows, :])
                        pieces.append(jnp.where(odd, last[:, HD:], last[:, 0:HD]))
                r.wide[QKVS][rows, part * D : (part + 1) * D] = jnp.concatenate(pieces, 1)

        unit(r.wide[QKVS].at[rows], r.results[QKVS].at[rows], widen)

    def out():
        def widen():
            r.wide[OUT][...] = to_single(r.narrow[OUT][0])

        unit(r.wide[OUT], r.results[OUT], widen)

    unit(r.input_grad_in, r.input_grad, keep)
    unit(r.result_in, r.result, keep)
    for index in range(GROUP):
        down(index)
        up(index)
    out()
    for index in range(GROUP):
        qkv(index)
    for row in range(8):
        r.vectors[row][...] = r.small_in[row : row + 1, :].reshape(SLICE)
    r.vectors[8][...] = jnp.concatenate(
        [r.small_in[C1 + part : C1 + part + 1, :] for part in range(GROUP)], 1
    ).reshape(D)
    for store, widen in units:
        widen()
        store.start()
    for store, _ in units:
        store.wait()


def layer(replicas, *arguments):
    (
        tokens, cotangent, clip_count, ln1_gain, ln1_bias, qkv_weight, q_bias, v_bias,
        out_weight, out_bias, ln2_gain, ln2_bias, fc1_weight, fc1_bias, fc2_weight, fc2_bias,
    ) = arguments
    slots, slot, _ = tokens.shape
    length = slot * GROUP
    levels = (replicas // 8).bit_length() - 1
    vectors = (
        ln1_gain, ln1_bias, out_bias, ln2_gain, ln2_bias, fc2_bias, q_bias, v_bias, fc1_bias,
    )
    anywhere = pl.BlockSpec(memory_space=pl.ANY)
    in_memory = pl.BlockSpec(memory_space=pltpu.VMEM)
    shape = jax.ShapeDtypeStruct

    inputs = dict(
        tokens_in=anywhere,
        cotangent_in=anywhere,
        count_in=pl.BlockSpec(memory_space=pltpu.SMEM),
        vectors_in=[anywhere] * 9,
        qkv_in=anywhere,
        out_in=anywhere,
        up_in=anywhere,
        down_in=anywhere,
    )
    outputs = dict(
        result_out=pltpu.VMEM(tokens.shape, BRAIN),
        input_grad_out=pltpu.VMEM(tokens.shape, SINGLE),
        small_out=pltpu.VMEM((VECTOR_ROWS, SLICE), SINGLE),
        fulls=[
            pltpu.VMEM((GROUP if w[2] else w[0], SLICE, w[1]), BRAIN) for w in WEIGHTS
        ],
    )
    scratch = dict(
        qkv_wide=pltpu.VMEM(qkv_weight.shape, SINGLE),
        out_wide=pltpu.VMEM(out_weight.shape, SINGLE),
        up_wide=pltpu.VMEM(fc1_weight.shape, SINGLE),
        down_wide=pltpu.VMEM(fc2_weight.shape, SINGLE),
        qkv_cut=pltpu.VMEM((GROUP, SLICE, QKV), BRAIN),
        up_cut=pltpu.VMEM((GROUP, SLICE, D), BRAIN),
        qkv_own=pltpu.VMEM((D, QKV), BRAIN),
        up_own=pltpu.VMEM((D, D), BRAIN),
        out_all=pltpu.VMEM((D, D), BRAIN),
        down_own=pltpu.VMEM((D, D), BRAIN),
        vectors=pltpu.VMEM((GROUP, VECTOR_ROWS, SLICE), SINGLE),
        vectors_raw=[pltpu.VMEM(vector.shape, SINGLE) for vector in vectors],
        tokens=pltpu.VMEM((2, length, D), BRAIN),
        cotangent=pltpu.VMEM((2, length, D), BRAIN),
        hidden_one=pltpu.VMEM((2, length, D), BRAIN),
        pairs=pltpu.VMEM((2, length, QKV), BRAIN),
        soft=pltpu.VMEM((2 * LOCAL_HEADS, length, length), SINGLE),
        mixed=pltpu.VMEM((GROUP, 3, length, TILE), BRAIN),
        middle_own=pltpu.VMEM((2, slot, D), SINGLE),
        hidden_two=pltpu.VMEM((2, length, D), BRAIN),
        active=pltpu.VMEM((2, length, D), BRAIN),
        lifted_grad=pltpu.VMEM((2, length, D), BRAIN),
        gradient=pltpu.VMEM((2, length, D), BRAIN),
        mixed_grad=pltpu.VMEM((2, length, SLICE), BRAIN),
        pairs_grad=pltpu.VMEM((2, length, QKV), BRAIN),
        stage=pltpu.VMEM((2 * slot, D), SINGLE),
        sum_sent=pltpu.VMEM((2, 2, 3, slot, D), BRAIN),
        sum_near=pltpu.VMEM((2, 2, 2, slot, D), BRAIN),
        sum_far=pltpu.VMEM((2, 2, slot, D), BRAIN),
        sum_own=pltpu.VMEM((2, 2, slot, D), SINGLE),
        up_grad=pltpu.VMEM((GROUP, SLICE, D), BRAIN),
        out_grad=pltpu.VMEM((1, SLICE, D), BRAIN),
        qkv_grad=pltpu.VMEM((GROUP, SLICE, TAIL_LEFT), BRAIN),
        tail_grad=pltpu.VMEM((2, SLICE, TILE), BRAIN),
        columns=pltpu.VMEM((8, D), SINGLE),
        small_sent=pltpu.VMEM((GROUP, 8, SLICE), SINGLE),
        small_near=pltpu.VMEM((GROUP - 1, 8, SLICE), SINGLE),
        small_all=pltpu.VMEM((replicas, VECTOR_ROWS, SLICE), SINGLE),
        halves=[pltpu.VMEM((w[0], PAIR, w[1]), BRAIN) for w in WEIGHTS],
        lines=[pltpu.VMEM((w[0], PAIR, w[1]), BRAIN) for w in WEIGHTS],
        middles=[pltpu.VMEM((w[0], PAIR, w[1]), BRAIN) for w in WEIGHTS],
        crossed=[pltpu.VMEM((GROUP, PAIR, w[1]), BRAIN) for w in WEIGHTS if w[2]],
        extras=[
            pltpu.VMEM((levels, w[0], PAIR, w[1]) if levels else (1, 1, 16, TILE), BRAIN)
            for w in WEIGHTS
        ],
        send=pltpu.SemaphoreType.DMA((COPIES,)),
        recv=pltpu.SemaphoreType.DMA((COPIES,)),
        send_all=pltpu.SemaphoreType.DMA((1 + ITEMS, replicas)),
        recv_all=pltpu.SemaphoreType.DMA((1 + ITEMS, replicas)),
        near=pltpu.SemaphoreType.DMA((LOCALS,)),
    )
    sums = pl.pallas_call(
        functools.partial(kernel, replicas, counted(inputs) + counted(outputs) + counted(scratch)),
        out_shape=tuple(flat(outputs)),
        in_specs=flat(inputs),
        out_specs=(in_memory,) * len(flat(outputs)),
        scratch_shapes=flat(scratch),
        compiler_params=pltpu.CompilerParams(
            collective_id=0, has_side_effects=True, vmem_limit_bytes=60600 * 1024
        ),
        name="layer",
    )(
        tokens, cotangent, clip_count, *vectors, qkv_weight, out_weight, fc1_weight, fc2_weight
    )

    matrices = [fc2_weight, fc1_weight, out_weight, qkv_weight]
    last_inputs = dict(
        result_in=in_memory, input_grad_in=in_memory, small_in=in_memory, narrow=[in_memory] * len(WEIGHTS)
    )
    last_outputs = dict(
        result=shape(tokens.shape, BRAIN),
        input_grad=shape(tokens.shape, SINGLE),
        results=[shape(array.shape, SINGLE) for array in matrices],
        vectors=[shape(vector.shape, SINGLE) for vector in vectors],
    )
    last_scratch = dict(
        wide=[pltpu.VMEM(array.shape, SINGLE) for array in matrices],
        near=pltpu.SemaphoreType.DMA((16,)),
    )
    values = pl.pallas_call(
        functools.partial(
            finish, counted(last_inputs) + counted(last_outputs) + counted(last_scratch)
        ),
        out_shape=tuple(flat(last_outputs)),
        in_specs=flat(last_inputs),
        out_specs=(anywhere,) * 6 + (in_memory,) * 9,
        scratch_shapes=flat(last_scratch),
        compiler_params=pltpu.CompilerParams(vmem_limit_bytes=32 << 20),
        name="finish",
    )(*sums)
    o = gathered(counted(last_outputs), values)
    return (
        o.result,
        o.input_grad,
        o.vectors[G1],
        o.vectors[B1],
        o.results[QKVS],
        o.vectors[BQ],
        o.vectors[BV],
        o.results[OUT],
        o.vectors[BO],
        o.vectors[G2],
        o.vectors[B2],
        o.results[UP],
        o.vectors[C1],
        o.results[DOWN],
        o.vectors[C2],
    )


def solution(mesh):
    token, vector, matrix = P("replica", "shard", None), P("shard"), P("shard", None)
    return jax.shard_map(
        functools.partial(layer, mesh.shape["replica"]),
        mesh=mesh,
        in_specs=(
            token, token, P("replica"), vector, vector, matrix, vector, vector,
            matrix, vector, vector, vector, matrix, vector, matrix, vector,
        ),
        out_specs=(
            token, token, vector, vector, matrix, vector, vector, matrix,
            vector, vector, vector, matrix, vector, matrix, vector,
        ),
        check_vma=False,
    )
```
